32 devices in a mesh: dp: 8 (over z, x), fsdp: 4 (over y, core).
Axes of the slice: x: 2, y: 2, z: 4, core: 2. Of those that a mesh axis runs over, the one named last changes fastest.
Arguments:
- tokens: bfloat16 [2, 8192, 768], P(None, ('dp', 'fsdp')), may hold values from -6 to 6
- cotangent: bfloat16 [2, 8192, 768], P(None, ('dp', 'fsdp')), may hold values from -6 to 6
- target: int32 [2, 8192], P(None, ('dp', 'fsdp')), may hold values from 0 to 8191, as said below
- lengths: int32 [2, 32, 4], P(None, ('dp', 'fsdp')), may hold values from 1 to 128, 256 in all within a row
- w_qkv: bfloat16 [768, 2304], P(('dp', 'fsdp')), may hold values from -0.21875 to 0.21875
- qv_bias: bfloat16 [1536], P(('dp', 'fsdp')), may hold values from -1.75 to 1.75
- w_out: bfloat16 [768, 768], P(('dp', 'fsdp')), may hold values from -0.875 to 0.875
- out_bias: bfloat16 [768], P(('dp', 'fsdp')), may hold values from -1.75 to 1.75
- gain_one: bfloat16 [768], P(('dp', 'fsdp')), may hold values from 0.5 to 1.5
- shift_one: bfloat16 [768], P(('dp', 'fsdp')), may hold values from -1.75 to 1.75
- w_up: bfloat16 [768, 6144], P(('dp', 'fsdp')), may hold values from -0.21875 to 0.21875
- up_bias: bfloat16 [6144], P(('dp', 'fsdp')), may hold values from -1.75 to 1.75
- w_down: bfloat16 [3072, 768], P(('dp', 'fsdp')), may hold values from -0.109375 to 0.109375
- down_bias: bfloat16 [768], P(('dp', 'fsdp')), may hold values from -1.75 to 1.75
- gain_two: bfloat16 [768], P(('dp', 'fsdp')), may hold values from 0.5 to 1.5
- shift_two: bfloat16 [768], P(('dp', 'fsdp')), may hold values from -1.75 to 1.75
Outputs:
- out_tokens: bfloat16 [2, 8192, 768], P(None, ('dp', 'fsdp'))
- grad_tokens: bfloat16 [2, 8192, 768], P(None, ('dp', 'fsdp'))
- grad_w_qkv: float32 [768, 2304], P(('dp', 'fsdp'))
- grad_qv_bias: float32 [1536], P(('dp', 'fsdp'))
- grad_w_out: float32 [768, 768], P(('dp', 'fsdp'))
- grad_out_bias: float32 [768], P(('dp', 'fsdp'))
- grad_gain_one: float32 [768], P(('dp', 'fsdp'))
- grad_shift_one: float32 [768], P(('dp', 'fsdp'))
- grad_w_up: float32 [768, 6144], P(('dp', 'fsdp'))
- grad_up_bias: float32 [6144], P(('dp', 'fsdp'))
- grad_w_down: float32 [3072, 768], P(('dp', 'fsdp'))
- grad_down_bias: float32 [768], P(('dp', 'fsdp'))
- grad_gain_two: float32 [768], P(('dp', 'fsdp'))
- grad_shift_two: float32 [768], P(('dp', 'fsdp'))
The draws below stay inside these ranges and needn't reach their ends.
Inputs may be any that keep to these rules, and one draw needn't show every extreme that they name: In each micro-batch target is a permutation of the placed positions; position t lies in the buffer of device t // 256, and the 256 tokens that one device holds in the given order go exactly 8 to each device's buffer.
All inputs are finite; a program needn't handle non-finite values.
Results may differ from the reference program's by a relative error of at most 0.017.
Values may be sent and summed in bfloat16 or wider, within the bound.
No kernel may reach another device: no remote copies, remote signals or barrier semaphores. Data moves between devices by JAX's collectives and lax.ppermute only.
A program may use at most 192 MiB of HBM per device.

```python
import math
import jax
import jax.numpy as jnp
import numpy as np
from jax import lax

D = 768
HEADS = 12
HEAD_DIM = 64
FF = 3072
SLOT = 256
SEQS = 4
MB = 2
GROUPS = 32
TOKENS_MB = 8192


def draw_target(key, part):
    per_pair = SLOT // GROUPS

    def one_batch(batch_key):
        row_key, slot_key = jax.random.split(batch_key)
        row_orders = jax.vmap(lambda item: jax.random.permutation(item, SLOT))(jax.random.split(row_key, GROUPS)).astype(jnp.int32)
        slot_orders = jax.vmap(lambda item: jax.random.permutation(item, SLOT))(jax.random.split(slot_key, GROUPS)).astype(jnp.int32)
        place = jnp.arange(SLOT, dtype=jnp.int32)
        dest = place // per_pair
        within = place % per_pair
        source = jnp.arange(GROUPS, dtype=jnp.int32)
        chosen = slot_orders[dest[None, :], source[:, None] * per_pair + within[None, :]]
        values = dest[None, :] * SLOT + chosen
        filled = jnp.zeros((GROUPS, SLOT), jnp.int32).at[source[:, None], row_orders].set(values)
        return filled.reshape(GROUPS * SLOT)
    return jax.vmap(one_batch)(jax.random.split(key, MB))


def block_levels(stream_key, shape, pieces, least, top_value):
    level, own = 1.0, jax.random.fold_in(stream_key, 6)
    for dim, blocks in pieces:
        heights = jnp.exp(jax.random.uniform(jax.random.fold_in(own, dim), (blocks,), jnp.float32, least / len(pieces), top_value / len(pieces)))
        level = level * jnp.repeat(heights, shape[dim] // blocks).reshape([-1 if axis == dim else 1 for axis in range(len(shape))])
    return level


def split_up(number_of, total, bound, skew):
    loads = [(1 << 20) // math.isqrt(rank ** skew) + 1 for rank in range(2, number_of + 1)]
    spare, counts = total - bound - (number_of - 1), [1] * (number_of - 1)
    while spare > 0:
        free = [i for i in range(number_of - 1) if counts[i] < bound]
        mass, left = sum([loads[i] for i in free]), spare
        for i in free:
            more = min(bound - counts[i], max(1, left * loads[i] // mass), spare)
            counts[i] = counts[i] + more
            spare = spare - more
    return np.array([bound] + counts)


def ragged_sizes(own_key, number_of, total, bound, skew):
    if number_of == 2:
        one = jax.random.randint(own_key, (), max(1, total - bound), min(bound, total - 1) + 1)
        return jnp.stack([one, total - one])
    sizes = jnp.asarray(split_up(number_of, total, bound, skew), jnp.int32)
    pairs = (number_of - 1) // 2
    giver, receiver = sizes[1:1 + 2 * pairs:2], sizes[2:2 + 2 * pairs:2]
    room = jnp.minimum(giver - 1, bound - receiver)
    moved = jax.random.randint(jax.random.fold_in(own_key, 1), (pairs,), 0, 1 << 20) % (room + 1)
    sizes = sizes.at[1:1 + 2 * pairs:2].set(giver - moved).at[2:2 + 2 * pairs:2].set(receiver + moved)
    return sizes[jax.random.permutation(jax.random.fold_in(own_key, 2), number_of)]


def noise(key, shape, scale, bound, pieces=(), kind=jnp.bfloat16):
    values = jax.random.normal(key, shape, jnp.float32) * scale
    if len(pieces) > 0:
        values = block_levels(key, shape, pieces, -0.22, 0.18) * values
    return jnp.clip(values, min=-bound, max=bound).astype(kind)


def setup_inputs(seed: int = 0) -> dict:
    key_of = jax.random.split(jax.random.key(seed), 17)
    tokens = noise(key_of[0], (MB, TOKENS_MB, D), 1.0, 6.0, ((1, 32),))
    cotangent = noise(key_of[1], (MB, TOKENS_MB, D), 1.0, 6.0, ((1, 32),))
    target = draw_target(jax.random.fold_in(key_of[16], 71), 0)
    lengths = jax.vmap(lambda own: ragged_sizes(own, SEQS, SLOT, SLOT // 2, 2))(jax.random.split(key_of[3], MB * GROUPS)).reshape((MB, GROUPS, SEQS)).astype(jnp.int32)
    w_qkv = noise(key_of[4], (D, 3 * D), D ** -0.5, 0.21875, ((0, 32),))
    qv_bias = noise(key_of[5], (2 * D,), 0.3, 1.75, ((0, 32),))
    w_out = noise(key_of[6], (D, D), (D // 16) ** -0.5, 0.875, ((0, 32),))
    out_bias = noise(key_of[7], (D,), 0.3, 1.75, ((0, 32),))
    gain_one = jnp.clip(1.0 + 0.1 * jax.random.normal(key_of[8], (D,), jnp.float32), 0.5, 1.5).astype(jnp.bfloat16)
    shift_one = noise(key_of[9], (D,), 0.3, 1.75, ((0, 32),))
    w_up = noise(key_of[10], (D, 2 * FF), D ** -0.5, 0.21875, ((0, 32),))
    up_bias = noise(key_of[11], (2 * FF,), 0.3, 1.75, ((0, 32),))
    w_down = noise(key_of[12], (FF, D), FF ** -0.5, 0.109375, ((0, 32),))
    down_bias = noise(key_of[13], (D,), 0.3, 1.75, ((0, 32),))
    gain_two = jnp.clip(1.0 + 0.1 * jax.random.normal(key_of[14], (D,), jnp.float32), 0.5, 1.5).astype(jnp.bfloat16)
    shift_two = noise(key_of[15], (D,), 0.3, 1.75, ((0, 32),))
    return dict(tokens=tokens, cotangent=cotangent, target=target, lengths=lengths, w_qkv=w_qkv, qv_bias=qv_bias, w_out=w_out, out_bias=out_bias, gain_one=gain_one, shift_one=shift_one, w_up=w_up, up_bias=up_bias, w_down=w_down, down_bias=down_bias, gain_two=gain_two, shift_two=shift_two)


EPS = 1e-05
NEGATIVE = -1e+30

@jax.custom_vjp
def low(v):
    return lax.optimization_barrier(v.astype(jnp.bfloat16)).astype(jnp.float32)

@jax.custom_vjp
def low_back(v):
    return v

def low_keep(v):
    return (low(v), None)

def low_pass(kept, grad):
    return (grad,)

def back_keep(v):
    return (v, None)

def back_low(kept, grad):
    return (low(grad),)
low.defvjp(low_keep, low_pass)
low_back.defvjp(back_keep, back_low)

def layer_norm(values, gain, shift):
    centre = lax.optimization_barrier(jnp.mean(values, axis=-1, keepdims=True))
    centred = values - centre
    spread = lax.optimization_barrier(jnp.mean(centred * centred, axis=-1, keepdims=True))
    return centred * lax.rsqrt(spread + EPS) * gain + shift

def product(left, right):
    return jnp.dot(left, right, precision=lax.Precision.HIGHEST, preferred_element_type=jnp.float32)

def alibi_offsets(count):
    slopes = jnp.exp2(-8.0 * (jnp.arange(HEADS, dtype=jnp.float32) + 1.0) / HEADS)
    place = jnp.arange(count, dtype=jnp.float32)
    return slopes[:, None, None] * jnp.abs(place[:, None] - place[None, :])

def block_layer(rows, segment, params):
    w_qkv, qv_bias, w_out, out_bias, gain_one, shift_one, w_up, up_bias, w_down, down_bias, gain_two, shift_two = params
    count = rows.shape[0]
    full_bias = jnp.concatenate([qv_bias[:D], jnp.zeros((D,), jnp.float32), qv_bias[D:]])
    qkv = low_back(low(product(rows, w_qkv) + full_bias))
    triple = qkv.reshape(count, 3, HEADS, HEAD_DIM)
    query = triple[:, 0]
    keyed = triple[:, 1]
    value = triple[:, 2]
    scores = jnp.einsum('qhd,khd->hqk', query, keyed, precision=lax.Precision.HIGHEST) * 0.125 - alibi_offsets(count)
    scores = low_back(scores)
    same = segment[:, None] == segment[None, :]
    scores = jnp.where(same[None], scores, NEGATIVE)
    top = lax.optimization_barrier(jnp.max(scores, axis=-1, keepdims=True))
    raised = jnp.exp(scores - top)
    probs = low(raised / lax.optimization_barrier(jnp.sum(raised, axis=-1, keepdims=True)))
    mixed = jnp.einsum('hqk,khd->qhd', probs, value, precision=lax.Precision.HIGHEST).reshape(count, D)
    merged = low_back(low(mixed))
    branch = low_back(product(merged, w_out) + out_bias)
    first = low(layer_norm(rows + branch, gain_one, shift_one))
    upward = low_back(product(first, w_up) + up_bias)
    active = low_back(low(jax.nn.gelu(upward[:, :FF], approximate=False) * upward[:, FF:]))
    downward = low_back(product(active, w_down) + down_bias)
    return layer_norm(first + downward, gain_two, shift_two)

def reference(tokens, cotangent, target, lengths, w_qkv, qv_bias, w_out, out_bias, gain_one, shift_one, w_up, up_bias, w_down, down_bias, gain_two, shift_two):
    params = tuple((item.astype(jnp.float32) for item in (w_qkv, qv_bias, w_out, out_bias, gain_one, shift_one, w_up, up_bias, w_down, down_bias, gain_two, shift_two)))
    target = target.astype(jnp.int32)

    def one_placed(batch, dest):
        return jnp.zeros((TOKENS_MB, D), jnp.float32).at[dest].set(batch)

    def to_placed(values):
        return jax.vmap(one_placed)(values.astype(jnp.float32), target).reshape(MB * GROUPS, SLOT, D)
    bounds = jnp.cumsum(lengths.astype(jnp.int32), axis=-1).astype(jnp.int32)
    place = jnp.arange(SLOT, dtype=jnp.int32)
    segment = lax.optimization_barrier(jnp.sum((bounds[..., :, None] <= place).astype(jnp.int32), axis=-2)).astype(jnp.int32).reshape(MB * GROUPS, SLOT)

    def whole(inputs, *weights):

        def one_block(item):
            return block_layer(item[0], item[1], weights)
        return lax.map(jax.checkpoint(one_block), (inputs, segment))
    outputs, pull = jax.vjp(whole, to_placed(tokens), *params)
    grads = pull(to_placed(cotangent))

    def to_given(values):
        flat = values.reshape(MB, TOKENS_MB, D)
        return jax.vmap(lambda batch, dest: batch[dest])(flat, target).astype(jnp.bfloat16)
    return (to_given(outputs), to_given(grads[0]), grads[1], grads[2], grads[3], grads[4], grads[5], grads[6], grads[7], grads[8], grads[9], grads[10], grads[11], grads[12])
```

```python
import jax
import jax.numpy as jnp
from jax import lax
from jax.sharding import PartitionSpec as P

D = 768
HEADS = 12
HEAD_DIM = 64
FF = 3072

EPS = 1e-05
NEGATIVE = -1e30
AXES = ("dp", "fsdp")
BF = jnp.bfloat16
F32 = jnp.float32


def bit_roles(mesh):
    devices = mesh.devices.reshape(-1)
    count = devices.size.bit_length() - 1
    roles = []
    for bit in range(count):
        here, there = devices[0], devices[1 << bit]
        a, b = getattr(here, "coords", None), getattr(there, "coords", None)
        if a is None or b is None:
            roles.append("cyxzzzzzzz"[bit])
        elif tuple(a) == tuple(b):
            roles.append("c")
        else:
            roles.append("xyz"[[i for i in range(3) if a[i] != b[i]][0]])
    return roles


def orders(mesh):
    roles = bit_roles(mesh)

    def of(role):
        return [b for b in reversed(range(len(roles))) if roles[b] == role]

    one = of("z") + of("x") + of("y") + of("c")
    two = of("z") + of("y") + of("x") + of("c")
    return one, two


def swap(value, bit, count):
    return lax.ppermute(value, AXES, [(i, i ^ (1 << bit)) for i in range(count)])


def gather_rows(shard, order, me, count):
    buf = shard[None]
    done = []
    for bit in order:
        got = swap(buf, bit, count)
        mine = (me >> bit) & 1
        buf = jnp.stack([jnp.where(mine == 0, buf, got), jnp.where(mine == 0, got, buf)])
        done.insert(0, bit)
    rest = shard.shape
    buf = buf.reshape((2,) * len(done) + rest)
    by_bit = sorted(range(len(done)), key=lambda i: -done[i])
    buf = buf.transpose(tuple(by_bit) + tuple(range(len(done), len(done) + len(rest))))
    return buf.reshape((count,) + rest)


def scatter_rows(full, order, me, count):
    bits = len(order)
    rest = full.shape[1:]
    acc = full.reshape((2,) * bits + rest)
    left = list(reversed(range(bits)))
    for bit in reversed(order):
        axis = left.index(bit)
        mine = (me >> bit) & 1
        keep = lax.dynamic_index_in_dim(acc, mine, axis, keepdims=False)
        send = lax.dynamic_index_in_dim(acc, 1 - mine, axis, keepdims=False).astype(BF)
        acc = keep.astype(F32) + swap(send, bit, count).astype(F32)
        left.pop(axis)
        if left:
            acc = acc.astype(BF)
    return acc


def norm_stats(values):
    centre = jnp.mean(values, axis=-1, keepdims=True)
    centred = values - centre
    spread = jnp.mean(centred * centred, axis=-1, keepdims=True)
    inverse = lax.rsqrt(spread + EPS)
    return centred * inverse, inverse


def norm_back(normed, inverse, gain, upstream):
    scaled = upstream * gain
    first = jnp.mean(scaled, axis=-1, keepdims=True)
    second = jnp.mean(scaled * normed, axis=-1, keepdims=True)
    return (scaled - first - normed * second) * inverse


def dot(left, right):
    return jnp.dot(left, right, preferred_element_type=F32)


def dot_rows(left, right):
    return lax.dot_general(left, right, (((0,), (0,)), ((), ())), preferred_element_type=F32)


def dot_back(left, right):
    return lax.dot_general(left, right, (((1,), (1,)), ((), ())), preferred_element_type=F32)


def build(mesh):
    count = mesh.devices.size
    order_a, order_b = orders(mesh)

    def on_device(
        tokens,
        cotangent,
        target,
        lengths,
        w_qkv,
        qv_bias,
        w_out,
        out_bias,
        gain_one,
        shift_one,
        w_up,
        up_bias,
        w_down,
        down_bias,
        gain_two,
        shift_two,
    ):
        me = lax.axis_index(AXES)
        batches, slot, width = tokens.shape
        per = slot // count
        place = jnp.arange(slot, dtype=jnp.int32)

        smalls = [qv_bias, out_bias, gain_one, shift_one, up_bias, down_bias, gain_two, shift_two]
        sizes = [v.shape[0] for v in smalls]
        packed = jnp.concatenate(smalls)
        total = packed.shape[0]

        rank = jnp.sum((target[:, None, :] < target[:, :, None]).astype(jnp.int32), axis=2)
        pick = (rank[:, None, :] == place[None, :, None]).astype(BF)
        slots = (target % slot).astype(BF)
        out_rows = jnp.einsum("bri,bid->brd", pick, tokens, preferred_element_type=F32).astype(BF)
        out_up = jnp.einsum("bri,bid->brd", pick, cotangent, preferred_element_type=F32).astype(BF)
        out_slots = jnp.einsum("bri,bi->br", pick, slots, preferred_element_type=F32).astype(BF)

        def by_device(v):
            return v.reshape((batches, count, per) + v.shape[2:]).swapaxes(0, 1).reshape(
                (count, batches * per) + v.shape[2:]
            )

        extra_rows = batches * per
        lanes = 128 * -(-(total // extra_rows + 2) // 128)
        cols = lanes - 1
        side = jnp.zeros((extra_rows * cols,), BF).at[:total].set(packed).reshape(extra_rows, cols)
        payload = jnp.concatenate(
            [
                by_device(out_rows),
                by_device(out_slots)[..., None],
                jnp.broadcast_to(side[None], (count, extra_rows, cols)),
            ],
            axis=2,
        )
        first = lax.all_to_all(payload, AXES, split_axis=0, concat_axis=0, tiled=True)
        second = lax.all_to_all(by_device(out_up), AXES, split_axis=0, concat_axis=0, tiled=True)

        def by_batch(v):
            return v.reshape((count, batches, per) + v.shape[2:]).swapaxes(0, 1).reshape(
                (batches, slot) + v.shape[2:]
            )

        got_slots = by_batch(first[:, :, width]).astype(jnp.int32)
        put = (got_slots[:, None, :] == place[None, :, None]).astype(BF)
        x = jnp.einsum("bpk,bkd->bpd", put, by_batch(first[:, :, :width]), preferred_element_type=F32).astype(BF)
        e = jnp.einsum("bpk,bkd->bpd", put, by_batch(second), preferred_element_type=F32)
        flat_side = first[:, :, width + 1 :].reshape(count, -1)
        vectors, at = [], 0
        for size in sizes:
            vectors.append(flat_side[:, at : at + size].reshape(-1).astype(F32))
            at += size
        qv_b, out_b, gain1, shift1, up_b, down_b, gain2, shift2 = vectors

        attn_shard = jnp.concatenate([w_qkv, w_out], axis=1)
        attn = gather_rows(attn_shard, order_b, me, count).reshape(D, 4 * D)
        wqkv, wout = attn[:, : 3 * D], attn[:, 3 * D :]
        wup = gather_rows(w_up, order_a, me, count).reshape(D, 2 * FF)
        wdown = gather_rows(w_down, order_b, me, count).reshape(FF, D)

        rows = batches * slot
        x = x.reshape(rows, D)
        e = e.reshape(rows, D)
        bounds = jnp.cumsum(lengths[:, 0], axis=-1)
        segment = jnp.sum((bounds[:, :, None] <= place).astype(jnp.int32), axis=1)
        same = segment[:, :, None] == segment[:, None, :]
        slopes = jnp.exp2(-8.0 * (jnp.arange(HEADS, dtype=F32) + 1.0) / HEADS)
        gap = jnp.abs(place[:, None] - place[None, :]).astype(F32)
        bias = jnp.where(same[:, None], -slopes[None, :, None, None] * gap, NEGATIVE)

        full_bias = jnp.concatenate([qv_b[:D], jnp.zeros((D,), F32), qv_b[D:]])
        qkv = (dot(x, wqkv) + full_bias).astype(BF)
        triple = qkv.reshape(batches, slot, 3, HEADS, HEAD_DIM)
        q, k, v = triple[:, :, 0], triple[:, :, 1], triple[:, :, 2]
        scores = jnp.einsum("bqhd,bkhd->bhqk", q, k, preferred_element_type=F32) * 0.125 + bias
        top = jnp.max(scores, axis=-1, keepdims=True)
        raised = jnp.exp(scores - top)
        probs = raised / jnp.sum(raised, axis=-1, keepdims=True)
        probs_low = probs.astype(BF)
        merged = jnp.einsum("bhqk,bkhd->bqhd", probs_low, v, preferred_element_type=F32).astype(BF).reshape(rows, D)
        n1, inv1 = norm_stats(x.astype(F32) + dot(merged, wout) + out_b)
        h = (n1 * gain1 + shift1).astype(BF)
        up = dot(h, wup) + up_b
        gate, lin = up[:, :FF], up[:, FF:]
        cdf = 0.5 * (1.0 + lax.erf(gate * (0.5**0.5)))
        act = gate * cdf
        a = (act * lin).astype(BF)
        n2, inv2 = norm_stats(h.astype(F32) + dot(a, wdown) + down_b)
        result = (n2 * gain2 + shift2).astype(BF)

        dr2 = norm_back(n2, inv2, gain2, e)
        g_gain2 = jnp.sum(e * n2, axis=0)
        g_shift2 = jnp.sum(e, axis=0)
        df = dr2.astype(BF)
        g_down_b = jnp.sum(df.astype(F32), axis=0)
        g_wdown = dot_rows(a, df).astype(BF).reshape(count, FF // count, D)
        s_wdown = scatter_rows(g_wdown, order_b, me, count)
        da = dot_back(df, wdown).astype(BF).astype(F32)
        slope = cdf + gate * jnp.exp(-0.5 * gate * gate) * (1.0 / (2.0 * jnp.pi) ** 0.5)
        du = jnp.concatenate([da * lin * slope, da * act], axis=1).astype(BF)
        g_up_b = jnp.sum(du.astype(F32), axis=0)
        g_wup = dot_rows(h, du).astype(BF).reshape(count, D // count, 2 * FF)
        s_wup = scatter_rows(g_wup, order_a, me, count)
        dh = dot_back(du, wup) + dr2
        dr1 = norm_back(n1, inv1, gain1, dh)
        g_gain1 = jnp.sum(dh * n1, axis=0)
        g_shift1 = jnp.sum(dh, axis=0)
        dbr = dr1.astype(BF)
        g_out_b = jnp.sum(dbr.astype(F32), axis=0)
        g_wout = dot_rows(merged, dbr).astype(BF)
        do = dot_back(dbr, wout).astype(BF).reshape(batches, slot, HEADS, HEAD_DIM)
        dp = jnp.einsum("bqhd,bkhd->bhqk", do, v, preferred_element_type=F32)
        dv = jnp.einsum("bhqk,bqhd->bkhd", probs_low, do, preferred_element_type=F32)
        delta = jnp.sum(probs * dp, axis=-1, keepdims=True)
        ds = (probs * (dp - delta)).astype(BF)
        dq = jnp.einsum("bhqk,bkhd->bqhd", ds, k, preferred_element_type=F32) * 0.125
        dk = jnp.einsum("bhqk,bqhd->bkhd", ds, q, preferred_element_type=F32) * 0.125
        dqkv = jnp.stack([dq, dk, dv], axis=2).reshape(rows, 3 * D).astype(BF)
        sums = jnp.sum(dqkv.astype(F32), axis=0)
        g_qv_b = jnp.concatenate([sums[:D], sums[2 * D :]])
        g_wqkv = dot_rows(x, dqkv).astype(BF)
        g_attn = jnp.concatenate([g_wqkv, g_wout], axis=1).reshape(count, D // count, 4 * D)
        s_attn = scatter_rows(g_attn, order_b, me, count)
        dx = (dr1 + dot_back(dqkv, wqkv)).astype(BF)

        def back(rows_here):
            sent = jnp.einsum(
                "bpk,bpd->bkd", put, rows_here.reshape(batches, slot, D), preferred_element_type=F32
            ).astype(BF)
            got = lax.all_to_all(by_device(sent), AXES, split_axis=0, concat_axis=0, tiled=True)
            return jnp.einsum("bri,brd->bid", pick, by_batch(got), preferred_element_type=F32).astype(BF)

        out_tokens = back(result)
        grad_tokens = back(dx)

        small_grads = [g_qv_b, g_out_b, g_gain1, g_shift1, g_up_b, g_down_b, g_gain2, g_shift2]
        small_send = jnp.concatenate([g.reshape(count, -1) for g in small_grads], axis=1)
        pad = -small_send.shape[1] % 128
        small_send = jnp.pad(small_send, ((0, 0), (0, pad)))[:, None]
        small_got = lax.all_to_all(small_send, AXES, split_axis=0, concat_axis=0, tiled=True)
        small_sum = jnp.sum(small_got, axis=(0, 1))
        outs, at = [], 0
        for size in sizes:
            outs.append(small_sum[at : at + size])
            at += size
        return (
            out_tokens,
            grad_tokens,
            s_attn[:, : 3 * D],
            outs[0],
            s_attn[:, 3 * D :],
            outs[1],
            outs[2],
            outs[3],
            s_wup,
            outs[4],
            s_wdown,
            outs[5],
            outs[6],
            outs[7],
        )

    return on_device


def solution(mesh):
    rows = P(None, AXES, None)
    matrix, vector = P(AXES, None), P(AXES)
    return jax.shard_map(
        build(mesh),
        mesh=mesh,
        in_specs=(rows, rows, P(None, AXES), rows)
        + (matrix, vector, matrix, vector, vector, vector, matrix, vector, matrix, vector, vector, vector),
        out_specs=(rows, rows)
        + (matrix, vector, matrix, vector, vector, vector, matrix, vector, matrix, vector, vector, vector),
        check_vma=False,
    )
```

```python
import jax
import jax.numpy as jnp
from jax import lax
from jax.experimental import pallas as pl
from jax.experimental.pallas import tpu as pltpu
from jax.sharding import PartitionSpec as P

D = 768
HEADS = 12
HEAD_DIM = 64
FF = 3072

EPS = 1e-05
NEGATIVE = -1e30
AXES = ("dp", "fsdp")
BF = jnp.bfloat16
F32 = jnp.float32
I32 = jnp.int32


def bit_roles(mesh):
    devices = mesh.devices.reshape(-1)
    count = devices.size.bit_length() - 1
    roles = []
    for bit in range(count):
        here, there = devices[0], devices[1 << bit]
        a, b = getattr(here, "coords", None), getattr(there, "coords", None)
        if a is None or b is None:
            roles.append("cyxzzzzzzz"[bit])
        elif tuple(a) == tuple(b):
            roles.append("c")
        else:
            roles.append("xyz"[[i for i in range(3) if a[i] != b[i]][0]])
    return roles


def swap(value, bit, count):
    return lax.ppermute(value, AXES, [(i, i ^ (1 << bit)) for i in range(count)])


def tie(value, *others):
    if not others:
        return value
    return lax.optimization_barrier((value,) + tuple(others))[0]


def column_chunk(columns):
    return columns // 3 if columns % 384 == 0 else columns


CHEAP = pl.CostEstimate(flops=1000, bytes_accessed=1000, transcendentals=0)


def spread(t, positions):
    out = 0
    for k, position in enumerate(positions):
        out = out | (((t >> k) & 1) << position)
    return out


def settle(mine, first, second, positions):
    half, rows, columns = first.shape
    wide = column_chunk(columns)

    def body(mine_ref, a_ref, b_ref, o_ref):
        me = mine_ref[0]

        def move(t, carry):
            o_ref[me ^ spread(t, positions)] = a_ref[t]
            o_ref[me ^ spread(t + half, positions)] = b_ref[t]
            return carry

        lax.fori_loop(0, half, move, 0)

    out = jax.ShapeDtypeStruct((2 * half, rows, columns), first.dtype)
    return pl.pallas_call(
        body,
        out_shape=out,
        grid_spec=pltpu.PrefetchScalarGridSpec(
            num_scalar_prefetch=1,
            grid=(columns // wide,),
            in_specs=[pl.BlockSpec((half, rows, wide), lambda i, m: (0, 0, i))] * 2,
            out_specs=pl.BlockSpec((2 * half, rows, wide), lambda i, m: (0, 0, i)),
        ),
        cost_estimate=CHEAP,
        compiler_params=pltpu.CompilerParams(vmem_limit_bytes=14 * 1024 * 1024),
        name="settle",
    )(mine, first, second)


def insert_bit(index, position, value):
    low = index & ((1 << position) - 1)
    return ((index >> position) << (position + 1)) | (value << position) | low


def whole_vmem(*arrays):
    total = sum(a.size * a.dtype.itemsize for a in arrays)
    return pltpu.CompilerParams(vmem_limit_bytes=min(2 * total + (4 << 20), 60 << 20))


def columns_of(sources):
    spans, at = [], 0
    for source in sources:
        spans.append((at, at + source.shape[2]))
        at += source.shape[2]
    return spans, at


SCALAR = pl.BlockSpec(memory_space=pltpu.SMEM)
WHOLE = pl.BlockSpec(memory_space=pltpu.VMEM)


def pick(mine, sources, position, bit):
    blocks, rows, _ = sources[0].shape
    spans, columns = columns_of(sources)

    def body(mine_ref, *refs):
        o_ref = refs[-1]
        other = 1 - ((mine_ref[0] >> bit) & 1)

        def move(t, carry):
            index = insert_bit(t, position, other)
            for g_ref, (lo, hi) in zip(refs[:-1], spans):
                o_ref[t, :, lo:hi] = g_ref[index]
            return carry

        lax.fori_loop(0, blocks // 2, move, 0)

    out = jax.ShapeDtypeStruct((blocks // 2, rows, columns), BF)
    return pl.pallas_call(
        body,
        out_shape=out,
        in_specs=[SCALAR] + [WHOLE] * len(sources),
        out_specs=WHOLE,
        cost_estimate=CHEAP,
        compiler_params=whole_vmem(*sources, out),
        name="pick",
    )(mine, *sources)


def fold(mine, sources, got, now, position, bit):
    blocks, rows, columns = got.shape
    spans, _ = columns_of(sources)

    def body(mine_ref, *refs):
        k_refs, r_ref, s_ref, n_ref = refs[:-3], refs[-3], refs[-2], refs[-1]
        side = (mine_ref[0] >> bit) & 1

        def put_total(out_ref, t, index):
            source = index
            if now is not None:
                source = insert_bit(index, now[0], (mine_ref[0] >> now[1]) & 1)
            for k_ref, (lo, hi) in zip(k_refs, spans):
                out_ref[t, :, lo:hi] = (k_ref[source].astype(F32) + r_ref[index, :, lo:hi].astype(F32)).astype(BF)

        def move(t, carry):
            put_total(s_ref, t, insert_bit(t, position, 1 - side))
            put_total(n_ref, t, insert_bit(t, position, side))
            return carry

        lax.fori_loop(0, blocks // 2, move, 0)

    out = jax.ShapeDtypeStruct((blocks // 2, rows, columns), BF)
    return pl.pallas_call(
        body,
        out_shape=(out, out),
        in_specs=[SCALAR] + [WHOLE] * (len(sources) + 1),
        out_specs=[WHOLE] * 2,
        cost_estimate=CHEAP,
        compiler_params=whole_vmem(*sources, got, out, out),
        name="fold",
    )(mine, *sources, got)


class Gather:
    def __init__(self, block, order, count):
        self.held, self.order, self.count, self.at = block, order, count, 0
        self.got = None

    def step(self, *after):
        if self.got is not None:
            self.held = jnp.concatenate([self.held, self.got], axis=0)
        self.got = swap(tie(self.held, *after), self.order[self.at], self.count)
        self.at += 1
        return self.got


class Scatter:
    def __init__(self, mine, sources, left, order, count):
        self.mine, self.kept, self.left, self.order, self.count = mine, list(sources), list(left), order, count
        self.at, self.now, self.got, self.sent = 0, None, None, None

    def ready(self, *after):
        bit = self.order[self.at]
        if self.got is None:
            position = self.left.index(bit)
            self.kept[0] = tie(self.kept[0], *after)
            self.sent = pick(self.mine, self.kept, position, bit)
            self.now = (position, bit)
        else:
            got = tie(self.got, *after)
            self.sent, kept = fold(self.mine, self.kept, got, self.now, self.left.index(bit), bit)
            self.kept, self.now = [kept], None
        return self.sent

    def step(self, *after):
        self.ready(*after)
        bit = self.order[self.at]
        self.got = swap(self.sent, bit, self.count)
        self.left.remove(bit)
        self.at += 1
        return self.got

    def total(self):
        return self.kept[0][0].astype(F32) + self.got[0].astype(F32)


def halves_of(shard, block):
    pieces = shard.shape[1] // (2 * block)

    def body(w_ref, even_ref, odd_ref):
        values = w_ref[...].astype(F32)
        for out, start in ((even_ref, 0), (odd_ref, block)):
            parts = [values[:, i * 2 * block + start : i * 2 * block + start + block] for i in range(pieces)]
            out[...] = jnp.concatenate(parts, axis=1).astype(out.dtype)

    out = jax.ShapeDtypeStruct((shard.shape[0], shard.shape[1] // 2), shard.dtype)
    return pl.pallas_call(
        body, out_shape=(out, out), cost_estimate=CHEAP, compiler_params=whole_vmem(shard, out, out), name="halves"
    )(shard)


def join_halves(even, odd, block):
    pieces = even.shape[1] // block

    def body(even_ref, odd_ref, o_ref):
        a, b = even_ref[...].astype(F32), odd_ref[...].astype(F32)
        parts = []
        for i in range(pieces):
            parts += [a[:, i * block : (i + 1) * block], b[:, i * block : (i + 1) * block]]
        o_ref[...] = jnp.concatenate(parts, axis=1)

    out = jax.ShapeDtypeStruct((even.shape[0], 2 * even.shape[1]), F32)
    return pl.pallas_call(
        body, out_shape=out, cost_estimate=CHEAP, compiler_params=whole_vmem(even, odd, out, out), name="join"
    )(even, odd)


def attend(qk, v, segment_row, segment_column, slopes, batches, slot):
    pairs = HEADS // 2
    width = 2 * HEAD_DIM

    def body(slope_ref, qk_ref, v_ref, row_ref, column_ref, o_ref, p_ref):
        pair = pl.program_id(1)
        at = pl.multiple_of(pair * width, width)
        query = qk_ref[:, pl.ds(at, width)]
        keyed = qk_ref[:, pl.ds(D + at, width)]
        value = v_ref[:, pl.ds(at, width)]
        lane = lax.broadcasted_iota(I32, (slot, width), 1)
        gap = jnp.abs(
            lax.broadcasted_iota(I32, (slot, slot), 0) - lax.broadcasted_iota(I32, (slot, slot), 1)
        ).astype(F32)
        same = column_ref[0] == row_ref[0]
        mixed = []
        for which in range(2):
            own = (lane >= HEAD_DIM) if which else (lane < HEAD_DIM)
            only = jnp.where(own, query, jnp.zeros_like(query))
            scores = lax.dot_general(only, keyed, (((1,), (1,)), ((), ())), preferred_element_type=F32)
            scores = jnp.where(same, scores * 0.125 - slope_ref[2 * pair + which] * gap, NEGATIVE)
            raised = jnp.exp(scores - jnp.max(scores, axis=1, keepdims=True))
            probs = (raised / jnp.sum(raised, axis=1, keepdims=True)).astype(BF)
            p_ref[0, 0, which] = probs
            mixed.append(jnp.dot(probs, value, preferred_element_type=F32))
        o_ref[:, pl.ds(at, width)] = jnp.where(lane < HEAD_DIM, mixed[0], mixed[1]).astype(BF)

    rows = batches * slot
    merged = jax.ShapeDtypeStruct((rows, D), BF)
    probs = jax.ShapeDtypeStruct((batches, pairs, 2, slot, slot), BF)
    return pl.pallas_call(
        body,
        out_shape=(merged, probs),
        grid=(batches, pairs),
        in_specs=[
            pl.BlockSpec(memory_space=pltpu.SMEM),
            pl.BlockSpec((slot, 2 * D), lambda b, h: (b, 0)),
            pl.BlockSpec((slot, D), lambda b, h: (b, 0)),
            pl.BlockSpec((1, 1, slot), lambda b, h: (b, 0, 0)),
            pl.BlockSpec((1, slot, 1), lambda b, h: (b, 0, 0)),
        ],
        out_specs=[
            pl.BlockSpec((slot, D), lambda b, h: (b, 0)),
            pl.BlockSpec((1, 1, 2, slot, slot), lambda b, h: (b, h, 0, 0, 0)),
        ],
        cost_estimate=CHEAP,
        compiler_params=pltpu.CompilerParams(vmem_limit_bytes=24 * 1024 * 1024),
        name="attend",
    )(slopes, qk, v, segment_row, segment_column)


def attend_back(qk, v, probs, do, batches, slot):
    pairs = HEADS // 2
    width = 2 * HEAD_DIM
    first = (((0,), (0,)), ((), ()))
    second = (((1,), (1,)), ((), ()))

    def body(qk_ref, v_ref, p_ref, do_ref, dqk_ref, dv_ref):
        at = pl.multiple_of(pl.program_id(1) * width, width)
        query = qk_ref[:, pl.ds(at, width)]
        keyed = qk_ref[:, pl.ds(D + at, width)]
        value = v_ref[:, pl.ds(at, width)]
        upstream = do_ref[:, pl.ds(at, width)]
        lane = lax.broadcasted_iota(I32, (slot, width), 1)
        dq, dk, dv = [], [], []
        for which in range(2):
            own = (lane >= HEAD_DIM) if which else (lane < HEAD_DIM)
            low = p_ref[0, 0, which]
            high = low.astype(F32)
            only = jnp.where(own, upstream, jnp.zeros_like(upstream))
            dp = lax.dot_general(only, value, second, preferred_element_type=F32)
            delta = jnp.sum(high * dp, axis=1, keepdims=True)
            ds = (high * (dp - delta)).astype(BF)
            dq.append(jnp.dot(ds, keyed, preferred_element_type=F32))
            dk.append(lax.dot_general(ds, query, first, preferred_element_type=F32))
            dv.append(lax.dot_general(low, upstream, first, preferred_element_type=F32))
        early = lane < HEAD_DIM
        dqk_ref[:, pl.ds(at, width)] = (jnp.where(early, dq[0], dq[1]) * 0.125).astype(BF)
        dqk_ref[:, pl.ds(D + at, width)] = (jnp.where(early, dk[0], dk[1]) * 0.125).astype(BF)
        dv_ref[:, pl.ds(at, width)] = jnp.where(early, dv[0], dv[1]).astype(BF)

    rows = batches * slot
    return pl.pallas_call(
        body,
        out_shape=(jax.ShapeDtypeStruct((rows, 2 * D), BF), jax.ShapeDtypeStruct((rows, D), BF)),
        grid=(batches, pairs),
        in_specs=[
            pl.BlockSpec((slot, 2 * D), lambda b, h: (b, 0)),
            pl.BlockSpec((slot, D), lambda b, h: (b, 0)),
            pl.BlockSpec((1, 1, 2, slot, slot), lambda b, h: (b, h, 0, 0, 0)),
            pl.BlockSpec((slot, D), lambda b, h: (b, 0)),
        ],
        out_specs=[
            pl.BlockSpec((slot, 2 * D), lambda b, h: (b, 0)),
            pl.BlockSpec((slot, D), lambda b, h: (b, 0)),
        ],
        cost_estimate=CHEAP,
        compiler_params=pltpu.CompilerParams(vmem_limit_bytes=24 * 1024 * 1024),
        name="attend_back",
    )(qk, v, probs, do)


TILE = 256
ROWS = (((0,), (0,)), ((), ()))
BACK = (((1,), (1,)), ((), ()))


def in_vmem(body, outs, *arrays, name, scratch=16 << 20):
    total = sum(a.size * a.dtype.itemsize for a in arrays + tuple(outs))
    return pl.pallas_call(
        body,
        out_shape=tuple(outs),
        in_specs=[WHOLE] * len(arrays),
        out_specs=tuple([WHOLE] * len(outs)),
        cost_estimate=CHEAP,
        compiler_params=pltpu.CompilerParams(vmem_limit_bytes=min(total + scratch, 62 << 20)),
        name=name,
    )(*arrays)


def product(left, right, dims):
    return lax.dot_general(left, right, dims, preferred_element_type=F32)


def tiles(count, step):
    def run(i, carry):
        step(pl.multiple_of(i * TILE, TILE))
        return carry

    lax.fori_loop(0, count // TILE, run, 0)


def down_weight_grad(a, df, df_other):
    rows = df.shape[0]

    def body(a_ref, d_ref, o_ref, g_ref):
        def step(at):
            g = product(a_ref[:rows, pl.ds(at, TILE)], d_ref[...], ROWS)
            g += product(a_ref[rows:, pl.ds(at, TILE)], o_ref[...], ROWS)
            g_ref[pl.ds(at, TILE), :] = g.astype(BF)

        tiles(a.shape[1], step)

    out = jax.ShapeDtypeStruct((a.shape[1], df.shape[1]), BF)
    return in_vmem(body, [out], a, df, df_other, name="down_grad")[0]


def units_back(df, df_other, w_dn, slope, act):
    rows, hidden = df.shape[0], w_dn.shape[0]

    def body(d_ref, o_ref, w_ref, s_ref, a_ref, du1_ref, du2_ref, sum_ref):
        sum_ref[...] = jnp.zeros_like(sum_ref)
        for base, source in ((0, d_ref), (rows, o_ref)):

            def step(at, base=base, source=source):
                da = product(source[pl.ds(at, TILE), :], w_ref[...], BACK).astype(BF).astype(F32)
                here = pl.ds(base + at, TILE)
                du1 = (da * s_ref[here, :].astype(F32)).astype(BF)
                du2 = (da * a_ref[here, :].astype(F32)).astype(BF)
                du1_ref[here, :] = du1
                du2_ref[here, :] = du2
                sum_ref[0:1, :] += jnp.sum(du1.astype(F32), axis=0, keepdims=True)
                sum_ref[1:2, :] += jnp.sum(du2.astype(F32), axis=0, keepdims=True)

            tiles(rows, step)

    du = jax.ShapeDtypeStruct((2 * rows, hidden), BF)
    sums = jax.ShapeDtypeStruct((2, hidden), F32)
    return in_vmem(body, [du, du, sums], df, df_other, w_dn, slope, act, name="units_back")


def up_weight_grad(h, h_other, du):
    rows = h.shape[0]

    def body(h_ref, o_ref, d_ref, g_ref):
        def step(at):
            g = product(h_ref[:, pl.ds(at, TILE)], d_ref[:rows, :], ROWS)
            g += product(o_ref[:, pl.ds(at, TILE)], d_ref[rows:, :], ROWS)
            g_ref[pl.ds(at, TILE), :] = g.astype(BF)

        tiles(h.shape[1], step)

    out = jax.ShapeDtypeStruct((h.shape[1], du.shape[1]), BF)
    return in_vmem(body, [out], h, h_other, du, name="up_grad")[0]


def hidden_back(du1, du2, w_gate, w_lin):
    rows = du1.shape[0] // 2

    def body(d1_ref, d2_ref, g_ref, l_ref, own_ref, other_ref):
        for base, out in ((0, own_ref), (rows, other_ref)):

            def step(at, base=base, out=out):
                here = pl.ds(base + at, TILE)
                dh = product(d1_ref[here, :], g_ref[...], BACK) + product(d2_ref[here, :], l_ref[...], BACK)
                out[pl.ds(at, TILE), :] = dh.astype(out.dtype)

            tiles(rows, step)

    own = jax.ShapeDtypeStruct((rows, D), F32)
    other = jax.ShapeDtypeStruct((rows, D), BF)
    return in_vmem(body, [own, other], du1, du2, w_gate, w_lin, name="hidden_back")


def down_product(a, w_dn):
    rows = a.shape[0] // 2

    def body(a_ref, w_ref, own_ref, other_ref):
        for base, out in ((0, own_ref), (rows, other_ref)):

            def step(at, base=base, out=out):
                out[pl.ds(at, TILE), :] = jnp.dot(
                    a_ref[pl.ds(base + at, TILE), :], w_ref[...], preferred_element_type=F32
                ).astype(out.dtype)

            tiles(rows, step)

    own = jax.ShapeDtypeStruct((rows, D), F32)
    other = jax.ShapeDtypeStruct((rows, D), BF)
    return in_vmem(body, [own, other], a, w_dn, name="down_product")


def attention_weight_grads(x, dqk, dv, merged, dbr):
    def body(x_ref, qk_ref, v_ref, m_ref, d_ref, gqk_ref, gv_ref, go_ref, sum_ref):
        def step(at):
            here = pl.ds(at, TILE)
            gqk_ref[here, :] = product(x_ref[:, here], qk_ref[...], ROWS).astype(BF)
            gv_ref[here, :] = product(x_ref[:, here], v_ref[...], ROWS).astype(BF)
            go_ref[here, :] = product(m_ref[:, here], d_ref[...], ROWS).astype(BF)

        tiles(D, step)
        sum_ref[0:1, :] = jnp.sum(qk_ref[:, :D].astype(F32), axis=0, keepdims=True)
        sum_ref[1:2, :] = jnp.sum(v_ref[...].astype(F32), axis=0, keepdims=True)

    outs = [jax.ShapeDtypeStruct((D, n * D), BF) for n in (2, 1, 1)] + [jax.ShapeDtypeStruct((2, D), F32)]
    return in_vmem(body, outs, x, dqk, dv, merged, dbr, name="attention_grads")


def input_back(dr1, dqk, dv, w_qk, w_vo):
    def body(r_ref, qk_ref, v_ref, wqk_ref, wvo_ref, out_ref):
        def step(at):
            here = pl.ds(at, TILE)
            dx = r_ref[here, :] + product(qk_ref[here, :], wqk_ref[...], BACK)
            out_ref[here, :] = (dx + product(v_ref[here, :], wvo_ref[:, :D], BACK)).astype(BF)

        tiles(dr1.shape[0], step)

    return in_vmem(body, [jax.ShapeDtypeStruct(dr1.shape, BF)], dr1, dqk, dv, w_qk, w_vo, name="input_back")[0]


def norm_stats(values):
    centre = jnp.mean(values, axis=-1, keepdims=True)
    centred = values - centre
    spread_of = jnp.mean(centred * centred, axis=-1, keepdims=True)
    inverse = lax.rsqrt(spread_of + EPS)
    return centred * inverse, inverse


def norm_back(normed, inverse, gain, upstream):
    scaled = upstream * gain
    first = jnp.mean(scaled, axis=-1, keepdims=True)
    second = jnp.mean(scaled * normed, axis=-1, keepdims=True)
    return (scaled - first - normed * second) * inverse


def dot(left, right):
    return jnp.dot(left, right, preferred_element_type=F32)


def dot_rows(left, right):
    return lax.dot_general(left, right, (((0,), (0,)), ((), ())), preferred_element_type=F32)


def dot_back(left, right):
    return lax.dot_general(left, right, (((1,), (1,)), ((), ())), preferred_element_type=F32)


def build(mesh):
    count = mesh.devices.size
    roles = bit_roles(mesh)
    every = list(range(len(roles)))

    def of(role):
        return [b for b in reversed(every) if roles[b] == role]

    core = roles.index("c")
    chips = [b for b in every if b != core]
    one = of("z") + of("x") + of("y")
    two = of("z") + of("y") + of("x")

    def chip_position(bit):
        return bit if bit < core else bit - 1

    def on_device(
        tokens,
        cotangent,
        target,
        lengths,
        w_qkv,
        qv_bias,
        w_out,
        out_bias,
        gain_one,
        shift_one,
        w_up,
        up_bias,
        w_down,
        down_bias,
        gain_two,
        shift_two,
    ):
        me = lax.axis_index(AXES).astype(I32)
        my_core = (me >> core) & 1
        mine = me.reshape(1)
        low = me & ((1 << core) - 1)
        my_chip = (((me >> (core + 1)) << core) | low).reshape(1)
        batches, slot, width = tokens.shape
        rows = batches * slot
        per = slot // count
        place = jnp.arange(slot, dtype=I32)
        unit_block = (FF // count) << core
        hidden = FF // 2

        even, odd = halves_of(w_up, unit_block)
        up_send = jnp.where(my_core == 0, odd, even)
        up_hold = jnp.where(my_core == 0, even, odd)
        chain_qk = Gather(w_qkv[None, :, : 2 * D], one + [core], count)
        chain_vo = Gather(jnp.concatenate([w_qkv[:, 2 * D :], w_out], axis=1)[None], two + [core], count)
        up_got = swap(up_send, core, count)
        up_pair = jnp.stack([up_hold, up_got])
        chain_gate = Gather(up_pair[:, :, :hidden], one, count)
        chain_lin = Gather(up_pair[:, :, hidden:], two, count)
        down_order = of("y") + of("x") + of("z")
        chain_down = Gather(w_down[None], down_order, count)

        smalls = [qv_bias, out_bias, gain_one, shift_one, up_bias, down_bias, gain_two, shift_two]
        sizes = [v.shape[0] for v in smalls]
        packed = jnp.concatenate(smalls)
        total = packed.shape[0]

        rank = jnp.sum((target[:, None, :] < target[:, :, None]).astype(I32), axis=2)
        chosen = (rank[:, None, :] == place[None, :, None]).astype(BF)
        slots = (target % slot).astype(BF)
        out_rows = jnp.einsum("bri,bid->brd", chosen, tokens, preferred_element_type=F32).astype(BF)
        out_up = jnp.einsum("bri,bid->brd", chosen, cotangent, preferred_element_type=F32).astype(BF)
        out_slots = jnp.einsum("bri,bi->br", chosen, slots, preferred_element_type=F32).astype(BF)

        def by_device(v):
            return v.reshape((batches, count, per) + v.shape[2:]).swapaxes(0, 1).reshape(
                (count, batches * per) + v.shape[2:]
            )

        extra_rows = batches * per
        lanes = 128 * -(-(total // extra_rows + 2) // 128)
        cols = lanes - 1
        side = jnp.zeros((extra_rows * cols,), BF).at[:total].set(packed).reshape(extra_rows, cols)
        payload = jnp.concatenate(
            [
                by_device(out_rows),
                by_device(out_slots)[..., None],
                jnp.broadcast_to(side[None], (count, extra_rows, cols)),
            ],
            axis=2,
        )
        first = lax.all_to_all(payload, AXES, split_axis=0, concat_axis=0, tiled=True)

        zs = len(of("z"))
        flat = len(one) - zs
        for _ in range(zs):
            chain_qk.step()
            chain_vo.step()
        for _ in range(flat):
            chain_down.step()
        after_z = (chain_qk.got, chain_vo.got)
        for step in range(zs, len(one)):
            chain_qk.step()
            chain_vo.step()
            if step == zs:
                for _ in range(zs):
                    chain_gate.step(*after_z)
                    chain_lin.step(*after_z)
                    after_z = ()
        after_chips = (chain_qk.got, chain_vo.got)
        after_z = (chain_gate.got, chain_lin.got)

        def by_batch(v):
            return v.reshape((count, batches, per) + v.shape[2:]).swapaxes(0, 1).reshape(
                (batches, slot) + v.shape[2:]
            )

        got_slots = by_batch(first[:, :, width]).astype(I32)
        put = (got_slots[:, None, :] == place[None, :, None]).astype(BF)
        x = jnp.einsum("bpk,bkd->bpd", put, by_batch(first[:, :, :width]), preferred_element_type=F32).astype(BF)
        flat_side = first[:, :, width + 1 :].reshape(count, -1)
        vectors, at = [], 0
        for size in sizes:
            vectors.append(flat_side[:, at : at + size].reshape(-1).astype(F32))
            at += size
        qv_b, out_b, gain1, shift1, up_b, down_b, gain2, shift2 = vectors

        x = x.reshape(rows, D)
        chain_qk.step(x, *vectors)
        chain_vo.step(x, *vectors)
        for _ in range(flat - 1):
            chain_gate.step(*after_chips)
            chain_lin.step(*after_chips)
            after_chips = ()
        for _ in range(zs - 1):
            chain_down.step(*after_z)
            after_z = ()
        bounds = jnp.cumsum(lengths[:, 0], axis=-1)
        segment = jnp.sum((bounds[:, :, None] <= place).astype(I32), axis=1)
        slopes = jnp.exp2(-8.0 * (jnp.arange(HEADS, dtype=F32) + 1.0) / HEADS)

        w_qk = settle(mine, chain_qk.held, chain_qk.got, one + [core]).reshape(D, 2 * D)
        w_vo = settle(mine, chain_vo.held, chain_vo.got, two + [core]).reshape(D, 2 * D)
        w_v, w_o = w_vo[:, :D], w_vo[:, D:]
        qk = (dot(x, w_qk) + jnp.concatenate([qv_b[:D], jnp.zeros((D,), F32)])).astype(BF)
        v = (dot(x, w_v) + qv_b[D:]).astype(BF)
        qk = tie(qk, chain_gate.got, chain_lin.got)
        chain_down.step(chain_gate.got, chain_lin.got)
        chain_gate.step()
        chain_lin.step()
        merged, probs = attend(qk, v, segment[:, None, :], segment[:, :, None], slopes, batches, slot)
        second = lax.all_to_all(tie(by_device(out_up), merged), AXES, split_axis=0, concat_axis=0, tiled=True)
        n1, inv1 = norm_stats(x.astype(F32) + dot(merged, w_o) + out_b)
        h = (n1 * gain1 + shift1).astype(BF)

        h_other = swap(h, core, count)
        both_h = jnp.concatenate([h, h_other])
        w_gate = settle(mine, chain_gate.held, chain_gate.got, [core] + one).reshape(D, hidden)
        w_lin = settle(mine, chain_lin.held, chain_lin.got, [core] + two).reshape(D, hidden)
        w_dn = settle(
            my_chip, chain_down.held, chain_down.got, [chip_position(b) for b in down_order]
        ).reshape(hidden, D)
        even_b, odd_b = halves_of(up_b.reshape(1, 2 * FF), unit_block)
        half_b = jnp.where(my_core == 0, even_b, odd_b).reshape(2, hidden)
        gate = dot(both_h, w_gate) + half_b[0]
        lin = dot(both_h, w_lin) + half_b[1]
        cdf = 0.5 * (1.0 + lax.erf(gate * (0.5**0.5)))
        act = gate * cdf
        a = (act * lin).astype(BF)
        slope = cdf + gate * jnp.exp(-0.5 * gate * gate) * (1.0 / (2.0 * jnp.pi) ** 0.5)
        slope_low = (slope * lin).astype(BF)
        act_low = act.astype(BF)
        down, down_send = down_product(a, w_dn)
        down_other = swap(down_send, core, count)
        n2, inv2 = norm_stats(h.astype(F32) + down + down_other.astype(F32) + down_b)
        result = (n2 * gain2 + shift2).astype(BF)

        def back(rows_here):
            sent = jnp.einsum(
                "bpk,bpd->bkd", put, rows_here.reshape(batches, slot, D), preferred_element_type=F32
            ).astype(BF)
            return lax.all_to_all(by_device(sent), AXES, split_axis=0, concat_axis=0, tiled=True)

        def given(got):
            return jnp.einsum("bri,brd->bid", chosen, by_batch(got), preferred_element_type=F32).astype(BF)

        back_out = back(result)

        e = jnp.einsum("bpk,bkd->bpd", put, by_batch(second), preferred_element_type=F32).reshape(rows, D)
        dr2 = norm_back(n2, inv2, gain2, e)
        g_gain2 = jnp.sum(e * n2, axis=0)
        g_shift2 = jnp.sum(e, axis=0)
        df = dr2.astype(BF)
        g_down_b = jnp.sum(df.astype(F32), axis=0)
        df_other = swap(df, core, count)
        g_down = down_weight_grad(a, df, df_other).reshape(count // 2, FF // count, D)
        scatter_down = Scatter(mine, [g_down], chips, two[::-1], count)
        scatter_down.step()
        du1, du2, g_half_b = units_back(tie(df, scatter_down.sent), df_other, w_dn, slope_low, act_low)
        blocks = (count, D // count, -1)
        scatter_gate = Scatter(mine, [up_weight_grad(h, h_other, du1).reshape(blocks)], every, one[::-1] + [core], count)
        scatter_gate.step()
        du2 = tie(du2, scatter_gate.sent)
        scatter_lin = Scatter(mine, [up_weight_grad(h, h_other, du2).reshape(blocks)], every, two[::-1] + [core], count)
        scatter_lin.step()
        du1 = tie(du1, scatter_lin.sent)
        dh_own, dh_send = hidden_back(du1, du2, w_gate, w_lin)
        scatter_down.step(dh_own)
        dh_other = swap(tie(dh_send, scatter_down.sent), core, count)
        scatter_gate.step(scatter_down.sent)
        dh = tie(dh_own, scatter_gate.sent) + dh_other.astype(F32) + dr2
        dr1 = norm_back(n1, inv1, gain1, dh)
        g_gain1 = jnp.sum(dh * n1, axis=0)
        g_shift1 = jnp.sum(dh, axis=0)
        dbr = dr1.astype(BF)
        g_out_b = jnp.sum(dbr.astype(F32), axis=0)
        do = dot_back(dbr, w_o).astype(BF)
        scatter_down.step(do)
        do = tie(do, scatter_down.sent, back_out)
        dqk, dv = attend_back(qk, v, probs, do, batches, slot)
        scatter_lin.step(dqk)
        scatter_gate.step(scatter_lin.sent)
        dqk = tie(dqk, scatter_gate.sent)
        g_qk, g_v, g_out, qv_sums = attention_weight_grads(x, dqk, dv, merged, dbr)
        g_qk, g_v, g_out = g_qk.reshape(blocks), g_v.reshape(blocks), g_out.reshape(blocks)

        g_qv_b = qv_sums.reshape(-1)
        g_half = g_half_b.reshape(1, FF)
        g_up_b = join_halves(
            jnp.where(my_core == 0, g_half, 0.0), jnp.where(my_core == 0, 0.0, g_half), unit_block
        )
        small_grads = [g_qv_b, g_out_b, g_gain1, g_shift1, g_up_b, g_down_b, g_gain2, g_shift2]
        small_send = jnp.concatenate([g.reshape(count, -1) for g in small_grads], axis=1)
        used = small_send.shape[1]
        small_send = jnp.pad(small_send, ((0, 0), (0, -used % 128))).astype(BF).reshape(count, -1, 128)
        small_send = jnp.pad(small_send, ((0, 0), (0, D // count - small_send.shape[1]), (0, 0)))

        scatter_attn = Scatter(mine, [g_qk, g_v, g_out, small_send], every, [core] + one[::-1], count)
        scatter_attn.step()
        scatter_down.step(scatter_attn.sent)
        scatter_lin.step(scatter_down.sent)
        dx = input_back(tie(dr1, scatter_lin.sent), dqk, dv, w_qk, w_vo)
        back_dx = back(dx)

        out_tokens = given(back_out)
        grad_tokens = given(back_dx)

        last = dx

        def go(chain):
            nonlocal last
            chain.step(last)
            last = chain.sent

        go(scatter_attn)
        while scatter_gate.at < len(one) or scatter_lin.at < len(one):
            if scatter_gate.at < len(one):
                go(scatter_gate)
            if scatter_lin.at < len(one):
                go(scatter_lin)
        while scatter_down.at < len(one):
            go(scatter_down)
        while scatter_attn.at < len(every) - zs:
            go(scatter_attn)
        gate_last = scatter_gate.ready(last)
        lin_last = scatter_lin.ready(gate_last)
        up_last = jnp.concatenate([gate_last[0], lin_last[0]], axis=1)
        up_kept = jnp.concatenate([scatter_gate.kept[0][0], scatter_lin.kept[0][0]], axis=1)
        up_came = swap(up_last, core, count)
        last = up_last
        while scatter_attn.at < len(every):
            go(scatter_attn)
        s_up = join_halves(
            jnp.where(my_core == 0, up_kept, up_came), jnp.where(my_core == 0, up_came, up_kept), unit_block
        )
        s_attn = scatter_attn.total()
        small_sum = s_attn[:, 4 * D :].reshape(-1)
        outs, at = [], 0
        for size in sizes:
            outs.append(small_sum[at : at + size])
            at += size
        return (
            out_tokens,
            grad_tokens,
            s_attn[:, : 3 * D],
            outs[0],
            s_attn[:, 3 * D : 4 * D],
            outs[1],
            outs[2],
            outs[3],
            s_up,
            outs[4],
            scatter_down.total(),
            outs[5],
            outs[6],
            outs[7],
        )

    return on_device


def solution(mesh):
    rows = P(None, AXES, None)
    matrix, vector = P(AXES, None), P(AXES)
    return jax.shard_map(
        build(mesh),
        mesh=mesh,
        in_specs=(rows, rows, P(None, AXES), rows)
        + (matrix, vector, matrix, vector, vector, vector, matrix, vector, matrix, vector, vector, vector),
        out_specs=(rows, rows)
        + (matrix, vector, matrix, vector, vector, vector, matrix, vector, matrix, vector, vector, vector),
        check_vma=False,
    )
```

```python
import jax
import jax.numpy as jnp
from jax import lax
from jax.experimental import pallas as pl
from jax.experimental.pallas import tpu as pltpu
from jax.sharding import PartitionSpec as P

D = 768
HEADS = 12
HEAD_DIM = 64
FF = 3072

EPS = 1e-05
NEGATIVE = -1e30
AXES = ("dp", "fsdp")
BF = jnp.bfloat16
F32 = jnp.float32
I32 = jnp.int32


def bit_roles(mesh):
    devices = mesh.devices.reshape(-1)
    count = devices.size.bit_length() - 1
    roles = []
    for bit in range(count):
        here, there = devices[0], devices[1 << bit]
        a, b = getattr(here, "coords", None), getattr(there, "coords", None)
        if a is None or b is None:
            roles.append("cyxzzzzzzz"[bit])
        elif tuple(a) == tuple(b):
            roles.append("c")
        else:
            roles.append("xyz"[[i for i in range(3) if a[i] != b[i]][0]])
    return roles


def swap(value, bit, count):
    return lax.ppermute(value, AXES, [(i, i ^ (1 << bit)) for i in range(count)])


def tie(value, *others):
    if not others:
        return value
    return lax.optimization_barrier((value,) + tuple(others))[0]


CHEAP = pl.CostEstimate(flops=1000, bytes_accessed=1000, transcendentals=0)


SCALAR = pl.BlockSpec(memory_space=pltpu.SMEM)
WHOLE = pl.BlockSpec(memory_space=pltpu.VMEM)


def grant(*arrays):
    total = sum(a.size * a.dtype.itemsize for a in arrays)
    return pltpu.CompilerParams(vmem_limit_bytes=min(2 * total + (4 << 20), 60 << 20))


def spread(t, positions):
    out = 0
    for k, position in enumerate(positions):
        out = out | (((t >> k) & 1) << position)
    return out


def settle(mine, *parts):
    half, rows, _ = parts[0][0].shape
    spans, columns = [], 0
    for first, _, _ in parts:
        spans.append(slice(columns, columns + first.shape[2]))
        columns += first.shape[2]

    def body(mine_ref, *refs):
        me, o_ref = mine_ref[0], refs[-1]

        def move(t, carry):
            for k, (here, (_, _, order)) in enumerate(zip(spans, parts)):
                o_ref[me ^ spread(t, order), :, here] = refs[2 * k][t]
                o_ref[me ^ spread(t + half, order), :, here] = refs[2 * k + 1][t]
            return carry

        lax.fori_loop(0, half, move, 0)

    arrays = [a for part in parts for a in part[:2]]
    out = jax.ShapeDtypeStruct((2 * half, rows, columns), BF)
    return pl.pallas_call(
        body,
        out_shape=out,
        in_specs=[SCALAR] + [WHOLE] * len(arrays),
        out_specs=WHOLE,
        cost_estimate=CHEAP,
        compiler_params=grant(*arrays, out),
        name="settle",
    )(mine, *arrays)


def insert_bit(index, position, value):
    low = index & ((1 << position) - 1)
    return ((index >> position) << (position + 1)) | (value << position) | low


def pieces_of(arrays):
    return [(a, 0, a.shape[2]) for a in arrays]


def cut(pieces, low, high):
    out, at = [], 0
    for array, start, width in pieces:
        lo, hi = max(low, at), min(high, at + width)
        if lo < hi:
            out.append((array, start + lo - at, hi - lo))
        at += width
    return out


def segments(*lists):
    edges = {0}
    for pieces in lists:
        at = 0
        for _, _, width in pieces:
            at += width
            edges.add(at)
    edges = sorted(edges)
    out = []
    for low, high in zip(edges, edges[1:]):
        found = []
        for pieces in lists:
            at = 0
            for k, (_, start, width) in enumerate(pieces):
                if at <= low < at + width:
                    found.append((k, start + low - at))
                at += width
        out.append((low, high, found))
    return out


def pick(mine, pieces, position, bit):
    blocks, rows, _ = pieces[0][0].shape
    spans = segments(pieces)
    columns = spans[-1][1]

    def body(mine_ref, *refs):
        o_ref = refs[-1]
        other = 1 - ((mine_ref[0] >> bit) & 1)

        def move(t, carry):
            index = insert_bit(t, position, other)
            for low, high, ((k, at),) in spans:
                o_ref[t, :, low:high] = refs[k][index, :, at : at + high - low]
            return carry

        lax.fori_loop(0, blocks // 2, move, 0)

    sources = [p[0] for p in pieces]
    out = jax.ShapeDtypeStruct((blocks // 2, rows, columns), BF)
    return pl.pallas_call(
        body,
        out_shape=out,
        in_specs=[SCALAR] + [WHOLE] * len(sources),
        out_specs=WHOLE,
        cost_estimate=CHEAP,
        compiler_params=grant(*sources, out),
        name="pick",
    )(mine, *sources)


def fold(mine, kept, got, now, position, bit):
    blocks, rows, _ = got[0][0].shape
    spans = segments(kept, got)
    columns = spans[-1][1]

    def body(mine_ref, *refs):
        k_refs, r_refs, s_ref, n_ref = refs[: len(kept)], refs[len(kept) : -2], refs[-2], refs[-1]
        side = (mine_ref[0] >> bit) & 1

        def put_total(out_ref, t, index):
            source = index
            if now is not None:
                source = insert_bit(index, now[0], (mine_ref[0] >> now[1]) & 1)
            for low, high, ((k, at), (r, start)) in spans:
                wide = high - low
                total = k_refs[k][source, :, at : at + wide].astype(F32)
                total += r_refs[r][index, :, start : start + wide].astype(F32)
                out_ref[t, :, low:high] = total.astype(BF)

        def move(t, carry):
            put_total(s_ref, t, insert_bit(t, position, 1 - side))
            put_total(n_ref, t, insert_bit(t, position, side))
            return carry

        lax.fori_loop(0, blocks // 2, move, 0)

    sources = [p[0] for p in kept + got]
    out = jax.ShapeDtypeStruct((blocks // 2, rows, columns), BF)
    return pl.pallas_call(
        body,
        out_shape=(out, out),
        in_specs=[SCALAR] + [WHOLE] * len(sources),
        out_specs=[WHOLE] * 2,
        cost_estimate=CHEAP,
        compiler_params=grant(*sources, out, out),
        name="fold",
    )(mine, *sources)


class Gather:
    def __init__(self, block, order, count):
        self.held, self.order, self.count, self.at = block, order, count, 0
        self.got = None

    def all(self, *after):
        if self.got is None:
            return tie(self.held, *after)
        return tie(jnp.concatenate([self.held, self.got], axis=0), *after)

    def step(self, *after):
        self.held = self.all(*after)
        self.got = swap(self.held, self.order[self.at], self.count)
        self.at += 1
        return self.got


class Scatter:
    def __init__(self, mine, kept, got, left, now, order, count):
        self.mine, self.kept, self.got, self.left = mine, kept, got, list(left)
        self.now, self.order, self.count, self.at, self.sent = now, order, count, 0, None

    def part(self, low, high, order):
        return Scatter(
            self.mine, cut(self.kept, low, high), cut(self.got, low, high), self.left, self.now, order, self.count
        )

    def beside(self, other, order):
        return Scatter(
            self.mine, self.kept + other.kept, self.got + other.got, self.left, None, order, self.count
        )

    def ready(self, *after):
        bit = self.order[self.at]
        position = self.left.index(bit)
        if self.got is None:
            kept = [(tie(a, *after), at, width) for a, at, width in self.kept[:1]] + self.kept[1:]
            self.kept = kept
            self.sent = pick(self.mine, kept, position, bit)
            self.now = (position, bit)
        else:
            got = [(tie(a, *after), at, width) for a, at, width in self.got[:1]] + self.got[1:]
            self.sent, rest = fold(self.mine, self.kept, got, self.now, position, bit)
            self.kept, self.now = pieces_of([rest]), None
        return self.sent

    def step(self, *after):
        self.ready(*after)
        bit = self.order[self.at]
        self.got = pieces_of([swap(self.sent, bit, self.count)])
        self.left.remove(bit)
        self.at += 1
        return self.got

    def total(self):
        return self.kept[0][0][0].astype(F32) + self.got[0][0][0].astype(F32)


def halves_of(shard, block):
    pieces = shard.shape[1] // (2 * block)

    def body(w_ref, even_ref, odd_ref):
        values = w_ref[...].astype(F32)
        for out, start in ((even_ref, 0), (odd_ref, block)):
            parts = [values[:, i * 2 * block + start : i * 2 * block + start + block] for i in range(pieces)]
            out[...] = jnp.concatenate(parts, axis=1).astype(out.dtype)

    out = jax.ShapeDtypeStruct((shard.shape[0], shard.shape[1] // 2), shard.dtype)
    return pl.pallas_call(
        body, out_shape=(out, out), cost_estimate=CHEAP, compiler_params=grant(shard, out, out), name="halves"
    )(shard)


def join_halves(even, odd, block):
    pieces = even.shape[1] // block

    def body(even_ref, odd_ref, o_ref):
        a, b = even_ref[...].astype(F32), odd_ref[...].astype(F32)
        parts = []
        for i in range(pieces):
            parts += [a[:, i * block : (i + 1) * block], b[:, i * block : (i + 1) * block]]
        o_ref[...] = jnp.concatenate(parts, axis=1)

    out = jax.ShapeDtypeStruct((even.shape[0], 2 * even.shape[1]), F32)
    return pl.pallas_call(
        body, out_shape=out, cost_estimate=CHEAP, compiler_params=grant(even, odd, out, out), name="join"
    )(even, odd)


def attend(qk, v, segment_row, segment_column, slopes, batches, slot):
    pairs = HEADS // 2
    width = 2 * HEAD_DIM

    def body(slope_ref, qk_ref, v_ref, row_ref, column_ref, o_ref, p_ref):
        pair = pl.program_id(1)
        at = pl.multiple_of(pair * width, width)
        query = qk_ref[:, pl.ds(at, width)]
        keyed = qk_ref[:, pl.ds(D + at, width)]
        value = v_ref[:, pl.ds(at, width)]
        lane = lax.broadcasted_iota(I32, (slot, width), 1)
        gap = jnp.abs(
            lax.broadcasted_iota(I32, (slot, slot), 0) - lax.broadcasted_iota(I32, (slot, slot), 1)
        ).astype(F32)
        same = column_ref[0] == row_ref[0]
        mixed = []
        for which in range(2):
            own = (lane >= HEAD_DIM) if which else (lane < HEAD_DIM)
            only = jnp.where(own, query, jnp.zeros_like(query))
            scores = lax.dot_general(only, keyed, (((1,), (1,)), ((), ())), preferred_element_type=F32)
            scores = jnp.where(same, scores * 0.125 - slope_ref[2 * pair + which] * gap, NEGATIVE)
            raised = jnp.exp(scores - jnp.max(scores, axis=1, keepdims=True))
            probs = (raised / jnp.sum(raised, axis=1, keepdims=True)).astype(BF)
            p_ref[0, 0, which] = probs
            mixed.append(jnp.dot(probs, value, preferred_element_type=F32))
        o_ref[:, pl.ds(at, width)] = jnp.where(lane < HEAD_DIM, mixed[0], mixed[1]).astype(BF)

    rows = batches * slot
    merged = jax.ShapeDtypeStruct((rows, D), BF)
    probs = jax.ShapeDtypeStruct((batches, pairs, 2, slot, slot), BF)
    return pl.pallas_call(
        body,
        out_shape=(merged, probs),
        grid=(batches, pairs),
        in_specs=[
            pl.BlockSpec(memory_space=pltpu.SMEM),
            pl.BlockSpec((slot, 2 * D), lambda b, h: (b, 0)),
            pl.BlockSpec((slot, D), lambda b, h: (b, 0)),
            pl.BlockSpec((1, 1, slot), lambda b, h: (b, 0, 0)),
            pl.BlockSpec((1, slot, 1), lambda b, h: (b, 0, 0)),
        ],
        out_specs=[
            pl.BlockSpec((slot, D), lambda b, h: (b, 0)),
            pl.BlockSpec((1, 1, 2, slot, slot), lambda b, h: (b, h, 0, 0, 0)),
        ],
        cost_estimate=CHEAP,
        compiler_params=pltpu.CompilerParams(vmem_limit_bytes=24 * 1024 * 1024),
        name="attend",
    )(slopes, qk, v, segment_row, segment_column)


def attend_back(qk, v, probs, do, batches, slot):
    pairs = HEADS // 2
    width = 2 * HEAD_DIM
    first = (((0,), (0,)), ((), ()))
    second = (((1,), (1,)), ((), ()))

    def body(qk_ref, v_ref, p_ref, do_ref, dqk_ref, dv_ref):
        at = pl.multiple_of(pl.program_id(1) * width, width)
        query = qk_ref[:, pl.ds(at, width)]
        keyed = qk_ref[:, pl.ds(D + at, width)]
        value = v_ref[:, pl.ds(at, width)]
        upstream = do_ref[:, pl.ds(at, width)]
        lane = lax.broadcasted_iota(I32, (slot, width), 1)
        dq, dk, dv = [], [], []
        for which in range(2):
            own = (lane >= HEAD_DIM) if which else (lane < HEAD_DIM)
            low = p_ref[0, 0, which]
            high = low.astype(F32)
            only = jnp.where(own, upstream, jnp.zeros_like(upstream))
            dp = lax.dot_general(only, value, second, preferred_element_type=F32)
            delta = jnp.sum(high * dp, axis=1, keepdims=True)
            ds = (high * (dp - delta)).astype(BF)
            dq.append(jnp.dot(ds, keyed, preferred_element_type=F32))
            dk.append(lax.dot_general(ds, query, first, preferred_element_type=F32))
            dv.append(lax.dot_general(low, upstream, first, preferred_element_type=F32))
        early = lane < HEAD_DIM
        dqk_ref[:, pl.ds(at, width)] = (jnp.where(early, dq[0], dq[1]) * 0.125).astype(BF)
        dqk_ref[:, pl.ds(D + at, width)] = (jnp.where(early, dk[0], dk[1]) * 0.125).astype(BF)
        dv_ref[:, pl.ds(at, width)] = jnp.where(early, dv[0], dv[1]).astype(BF)

    rows = batches * slot
    return pl.pallas_call(
        body,
        out_shape=(jax.ShapeDtypeStruct((rows, 2 * D), BF), jax.ShapeDtypeStruct((rows, D), BF)),
        grid=(batches, pairs),
        in_specs=[
            pl.BlockSpec((slot, 2 * D), lambda b, h: (b, 0)),
            pl.BlockSpec((slot, D), lambda b, h: (b, 0)),
            pl.BlockSpec((1, 1, 2, slot, slot), lambda b, h: (b, h, 0, 0, 0)),
            pl.BlockSpec((slot, D), lambda b, h: (b, 0)),
        ],
        out_specs=[
            pl.BlockSpec((slot, 2 * D), lambda b, h: (b, 0)),
            pl.BlockSpec((slot, D), lambda b, h: (b, 0)),
        ],
        cost_estimate=CHEAP,
        compiler_params=pltpu.CompilerParams(vmem_limit_bytes=24 * 1024 * 1024),
        name="attend_back",
    )(qk, v, probs, do)


TILE = 256
ROWS = (((0,), (0,)), ((), ()))
BACK = (((1,), (1,)), ((), ()))


def in_vmem(body, outs, *arrays, name):
    total = sum(a.size * a.dtype.itemsize for a in arrays + tuple(outs))
    return pl.pallas_call(
        body,
        out_shape=tuple(outs),
        in_specs=[WHOLE] * len(arrays),
        out_specs=tuple([WHOLE] * len(outs)),
        cost_estimate=CHEAP,
        compiler_params=pltpu.CompilerParams(vmem_limit_bytes=min(total + (16 << 20), 62 << 20)),
        name=name,
    )(*arrays)


def product(left, right, dims):
    return lax.dot_general(left, right, dims, preferred_element_type=F32)


def tiles(count, step):
    def run(i, carry):
        step(pl.multiple_of(i * TILE, TILE))
        return carry

    lax.fori_loop(0, count // TILE, run, 0)


def receive(arrived, sizes, count, batches, slot, held):
    per = slot // count
    spans = -(-sum(sizes) // held)

    def body(in_ref, x_ref, put_ref, *refs):
        outs, side_ref = refs[:-1], refs[-1]
        for b in range(batches):
            slots = in_ref[b, :, D:].astype(F32)[:, 127:128]
            put = (slots == lax.broadcasted_iota(I32, (slot, slot), 1).astype(F32)).astype(F32).astype(BF)
            put_ref[b] = put
            x_ref[b * slot : (b + 1) * slot, :] = product(put, in_ref[b, :, :D], ROWS).astype(BF)
        side_ref[...] = in_ref[0, :, D:].astype(F32)
        flat = jnp.concatenate(
            [side_ref[pl.ds(r, count, stride=per), :][:, :held] for r in range(spans)], axis=1
        )
        at = 0
        for out, size in zip(outs, sizes):
            for j in range(count):
                out[:, j * size : (j + 1) * size] = flat[j : j + 1, at : at + size]
            at += size

    outs = [
        jax.ShapeDtypeStruct((batches * slot, D), BF),
        jax.ShapeDtypeStruct((batches, slot, slot), BF),
    ] + [jax.ShapeDtypeStruct((1, count * size), F32) for size in sizes]
    return pl.pallas_call(
        body,
        out_shape=tuple(outs),
        in_specs=[WHOLE],
        out_specs=tuple([WHOLE] * len(outs)),
        scratch_shapes=[pltpu.VMEM((slot, 128), F32)],
        cost_estimate=CHEAP,
        compiler_params=pltpu.CompilerParams(vmem_limit_bytes=20 << 20),
        name="receive",
    )(arrived)


def project(x, weights, bias):
    def body(x_ref, w_ref, b_ref, qk_ref, v_ref):
        def step(at):
            here = pl.ds(at, TILE)
            tile = x_ref[here, :]
            q = jnp.dot(tile, w_ref[:, :D], preferred_element_type=F32) + b_ref[:, :D]
            qk_ref[here, :D] = q.astype(BF)
            qk_ref[here, D:] = jnp.dot(tile, w_ref[:, D : 2 * D], preferred_element_type=F32).astype(BF)
            v = jnp.dot(tile, w_ref[:, 2 * D : 3 * D], preferred_element_type=F32) + b_ref[:, D:]
            v_ref[here, :] = v.astype(BF)

        tiles(x.shape[0], step)

    outs = [jax.ShapeDtypeStruct((x.shape[0], 2 * D), BF), jax.ShapeDtypeStruct((x.shape[0], D), BF)]
    return in_vmem(body, outs, x, weights, bias, name="project")


def first_norm(x, merged, weights, bias, gain, shift):
    def body(x_ref, m_ref, w_ref, b_ref, g_ref, s_ref, r_ref, h_ref):
        def step(at):
            here = pl.ds(at, TILE)
            total = x_ref[here, :].astype(F32) + b_ref[...]
            total += jnp.dot(m_ref[here, :], w_ref[:, 3 * D :], preferred_element_type=F32)
            r_ref[here, :] = total
            h_ref[here, :] = (norm_stats(total)[0] * g_ref[...] + s_ref[...]).astype(BF)

        tiles(x.shape[0], step)

    outs = [jax.ShapeDtypeStruct(x.shape, F32), jax.ShapeDtypeStruct(x.shape, BF)]
    return in_vmem(body, outs, x, merged, weights, bias, gain, shift, name="first_norm")


def near(width):
    return pl.BlockSpec((TILE, width), lambda i: (jnp.minimum(i, 1), 0))


def far(width):
    return pl.BlockSpec((TILE, width), lambda i: (jnp.maximum(i - 2, 0), 0))


def tile_of(width):
    return pl.BlockSpec((TILE, width), lambda i: (i, 0))


def fixed(*shape):
    return pl.BlockSpec(shape, lambda i: (0, 0))


TILED_GRANT = pltpu.CompilerParams(vmem_limit_bytes=32 << 20)


def units(mine, h, h_other, w_gate, w_lin, even, odd, core):
    rows, hidden = h.shape[0], w_gate.shape[1]
    assert rows == 2 * TILE

    def body(mine_ref, h_ref, o_ref, g_ref, l_ref, e_ref, d_ref, a_ref, slope_ref, act_ref):
        first = ((mine_ref[0] >> core) & 1) == 0
        tile = jnp.where(pl.program_id(0) < 2, h_ref[...], o_ref[...])
        for lo in range(0, hidden, TILE):
            wide = slice(lo, lo + TILE)
            late = slice(hidden + lo, hidden + lo + TILE)
            gate = jnp.dot(tile, g_ref[:, wide], preferred_element_type=F32)
            gate += jnp.where(first, e_ref[:, wide], d_ref[:, wide])
            lin = jnp.dot(tile, l_ref[:, wide], preferred_element_type=F32)
            lin += jnp.where(first, e_ref[:, late], d_ref[:, late])
            cdf = 0.5 * (1.0 + lax.erf(gate * (0.5**0.5)))
            act = gate * cdf
            slope = cdf + gate * jnp.exp(-0.5 * gate * gate) * (1.0 / (2.0 * jnp.pi) ** 0.5)
            a_ref[:, wide] = (act * lin).astype(BF)
            slope_ref[:, wide] = (slope * lin).astype(BF)
            act_ref[:, wide] = act.astype(BF)

    out = jax.ShapeDtypeStruct((2 * rows, hidden), BF)
    return pl.pallas_call(
        body,
        out_shape=(out, out, out),
        grid=(4,),
        in_specs=[SCALAR, near(D), far(D)] + [fixed(D, hidden)] * 2 + [fixed(1, 2 * hidden)] * 2,
        out_specs=(tile_of(hidden),) * 3,
        cost_estimate=CHEAP,
        compiler_params=TILED_GRANT,
        name="units",
    )(mine, h, h_other, w_gate, w_lin, even, odd)


def down_weight_grad(a, df, df_other):
    rows = df.shape[0]

    def body(a_ref, d_ref, o_ref, g_ref):
        def step(at):
            g = product(a_ref[:rows, pl.ds(at, TILE)], d_ref[...], ROWS)
            g += product(a_ref[rows:, pl.ds(at, TILE)], o_ref[...], ROWS)
            g_ref[pl.ds(at, TILE), :] = g.astype(BF)

        tiles(a.shape[1], step)

    out = jax.ShapeDtypeStruct((a.shape[1], df.shape[1]), BF)
    return in_vmem(body, [out], a, df, df_other, name="down_grad")[0]


def units_back(df, df_other, w_dn, slope, act):
    rows, hidden = df.shape[0], w_dn.shape[0]

    def body(d_ref, o_ref, w_ref, s_ref, a_ref, du1_ref, du2_ref, sum_ref):
        i = pl.program_id(0)
        tile = jnp.where(i < 2, d_ref[...], o_ref[...])
        da = product(tile, w_ref[...], BACK).astype(BF).astype(F32)
        du1 = (da * s_ref[...].astype(F32)).astype(BF)
        du2 = (da * a_ref[...].astype(F32)).astype(BF)
        du1_ref[...] = du1
        du2_ref[...] = du2

        @pl.when(i == 0)
        def _():
            sum_ref[...] = jnp.zeros_like(sum_ref)

        sum_ref[0:1, :] += jnp.sum(du1.astype(F32), axis=0, keepdims=True)
        sum_ref[1:2, :] += jnp.sum(du2.astype(F32), axis=0, keepdims=True)

    du = jax.ShapeDtypeStruct((2 * rows, hidden), BF)
    sums = jax.ShapeDtypeStruct((2, hidden), F32)
    return pl.pallas_call(
        body,
        out_shape=(du, du, sums),
        grid=(4,),
        in_specs=[near(D), far(D), fixed(hidden, D), tile_of(hidden), tile_of(hidden)],
        out_specs=(tile_of(hidden), tile_of(hidden), fixed(2, hidden)),
        cost_estimate=CHEAP,
        compiler_params=TILED_GRANT,
        name="units_back",
    )(df, df_other, w_dn, slope, act)


def up_weight_grad(h, h_other, du):
    rows = h.shape[0]

    def body(h_ref, o_ref, d_ref, g_ref):
        def step(at):
            g = product(h_ref[:, pl.ds(at, TILE)], d_ref[:rows, :], ROWS)
            g += product(o_ref[:, pl.ds(at, TILE)], d_ref[rows:, :], ROWS)
            g_ref[pl.ds(at, TILE), :] = g.astype(BF)

        tiles(h.shape[1], step)

    out = jax.ShapeDtypeStruct((h.shape[1], du.shape[1]), BF)
    return in_vmem(body, [out], h, h_other, du, name="up_grad")[0]


def hidden_back(du1, du2, w_gate, w_lin):
    rows, hidden = du1.shape[0] // 2, du1.shape[1]

    def body(d1_ref, d2_ref, g_ref, l_ref, own_ref, other_ref):
        dh = product(d1_ref[...], g_ref[...], BACK) + product(d2_ref[...], l_ref[...], BACK)

        @pl.when(pl.program_id(0) < 2)
        def _():
            own_ref[...] = dh

        @pl.when(pl.program_id(0) >= 2)
        def _():
            other_ref[...] = dh.astype(BF)

    own = jax.ShapeDtypeStruct((rows, D), F32)
    other = jax.ShapeDtypeStruct((rows, D), BF)
    return pl.pallas_call(
        body,
        out_shape=(own, other),
        grid=(4,),
        in_specs=[tile_of(hidden)] * 2 + [fixed(D, hidden)] * 2,
        out_specs=(near(D), far(D)),
        cost_estimate=CHEAP,
        compiler_params=TILED_GRANT,
        name="hidden_back",
    )(du1, du2, w_gate, w_lin)


def down_product(a, w_dn):
    rows = a.shape[0] // 2

    def body(a_ref, w_ref, own_ref, other_ref):
        for base, out in ((0, own_ref), (rows, other_ref)):

            def step(at, base=base, out=out):
                out[pl.ds(at, TILE), :] = jnp.dot(
                    a_ref[pl.ds(base + at, TILE), :], w_ref[...], preferred_element_type=F32
                ).astype(out.dtype)

            tiles(rows, step)

    own = jax.ShapeDtypeStruct((rows, D), F32)
    other = jax.ShapeDtypeStruct((rows, D), BF)
    return in_vmem(body, [own, other], a, w_dn, name="down_product")


def second_norm(h, down, down_other, e, down_b, gain, shift):
    rows = h.shape[0]

    def body(h_ref, d_ref, o_ref, e_ref, b_ref, g_ref, s_ref, res_ref, dr_ref, df_ref, sum_ref):
        sum_ref[...] = jnp.zeros_like(sum_ref)
        bias, gains, shifts = b_ref[...], g_ref[...], s_ref[...]

        def step(at):
            here = pl.ds(at, TILE)
            total = h_ref[here, :].astype(F32) + d_ref[here, :] + o_ref[here, :].astype(F32) + bias
            normed, inverse = norm_stats(total)
            res_ref[here, :] = (normed * gains + shifts).astype(BF)
            up = e_ref[here, :]
            dr = norm_back(normed, inverse, gains, up)
            low = dr.astype(BF)
            dr_ref[here, :] = dr
            df_ref[here, :] = low
            sum_ref[0:1, :] += jnp.sum(up * normed, axis=0, keepdims=True)
            sum_ref[1:2, :] += jnp.sum(up, axis=0, keepdims=True)
            sum_ref[2:3, :] += jnp.sum(low.astype(F32), axis=0, keepdims=True)

        tiles(rows, step)

    low, wide = jax.ShapeDtypeStruct((rows, D), BF), jax.ShapeDtypeStruct((rows, D), F32)
    outs = [low, wide, low, jax.ShapeDtypeStruct((3, D), F32)]
    return in_vmem(body, outs, h, down, down_other, e, down_b, gain, shift, name="second_norm")


def first_norm_back(dh_own, dh_other, dr2, r1, gain, w_vo):
    rows = r1.shape[0]

    def body(d_ref, o_ref, r_ref, n_ref, g_ref, w_ref, dr_ref, dbr_ref, do_ref, sum_ref):
        sum_ref[...] = jnp.zeros_like(sum_ref)

        def step(at):
            here = pl.ds(at, TILE)
            dh = d_ref[here, :] + o_ref[here, :].astype(F32) + r_ref[here, :]
            normed, inverse = norm_stats(n_ref[here, :])
            dr = norm_back(normed, inverse, g_ref[...], dh)
            low = dr.astype(BF)
            dr_ref[here, :] = dr
            dbr_ref[here, :] = low
            do_ref[here, :] = product(low, w_ref[:, 3 * D :], BACK).astype(BF)
            sum_ref[0:1, :] += jnp.sum(dh * normed, axis=0, keepdims=True)
            sum_ref[1:2, :] += jnp.sum(dh, axis=0, keepdims=True)
            sum_ref[2:3, :] += jnp.sum(low.astype(F32), axis=0, keepdims=True)

        tiles(rows, step)

    low, wide = jax.ShapeDtypeStruct((rows, D), BF), jax.ShapeDtypeStruct((rows, D), F32)
    outs = [wide, low, low, jax.ShapeDtypeStruct((3, D), F32)]
    return in_vmem(body, outs, dh_own, dh_other, dr2, r1, gain, w_vo, name="first_norm_back")


def attention_weight_grads(x, dqk, dv, merged, dbr):
    def body(x_ref, qk_ref, v_ref, m_ref, d_ref, gqk_ref, gv_ref, go_ref, sum_ref):
        def step(at):
            here = pl.ds(at, TILE)
            gqk_ref[here, :] = product(x_ref[:, here], qk_ref[...], ROWS).astype(BF)
            gv_ref[here, :] = product(x_ref[:, here], v_ref[...], ROWS).astype(BF)
            go_ref[here, :] = product(m_ref[:, here], d_ref[...], ROWS).astype(BF)

        tiles(D, step)
        sum_ref[0:1, :] = jnp.sum(qk_ref[:, :D].astype(F32), axis=0, keepdims=True)
        sum_ref[1:2, :] = jnp.sum(v_ref[...].astype(F32), axis=0, keepdims=True)

    outs = [jax.ShapeDtypeStruct((D, n * D), BF) for n in (2, 1, 1)] + [jax.ShapeDtypeStruct((2, D), F32)]
    return in_vmem(body, outs, x, dqk, dv, merged, dbr, name="attention_grads")


def input_back(dr1, dqk, dv, weights):
    def body(r_ref, qk_ref, v_ref, w_ref, out_ref):
        def step(at):
            here = pl.ds(at, TILE)
            dx = r_ref[here, :] + product(qk_ref[here, :], w_ref[:, : 2 * D], BACK)
            out_ref[here, :] = (dx + product(v_ref[here, :], w_ref[:, 2 * D : 3 * D], BACK)).astype(BF)

        tiles(dr1.shape[0], step)

    return in_vmem(body, [jax.ShapeDtypeStruct(dr1.shape, BF)], dr1, dqk, dv, weights, name="input_back")[0]


def owner_sums(mine, qv, first, second, half, sizes, count, block, core):
    total = sum(sizes)
    lanes = total + -total % 128

    def body(mine_ref, q_ref, f_ref, s_ref, u_ref, o_ref):
        mine_side = (mine_ref[0] >> core) & 1
        pieces = []
        for g in range(2):
            for i in range(u_ref.shape[1] // block):
                part = u_ref[g : g + 1, i * block : (i + 1) * block]
                for side in range(2):
                    pieces.append(jnp.where(mine_side == side, part, 0.0))
        up = jnp.concatenate(pieces, axis=1)
        rows = [None] + [r[i : i + 1, :] for r, i in ((f_ref, 2), (f_ref, 0), (f_ref, 1))]
        rows += [up] + [r[i : i + 1, :] for r, i in ((s_ref, 2), (s_ref, 0), (s_ref, 1))]
        o_ref[...] = jnp.zeros_like(o_ref)
        for j in range(count):
            at = 0
            for k, size in enumerate(sizes):
                if k == 0:
                    row, lo = divmod(j * size, D)
                    piece = q_ref[row : row + 1, lo : lo + size]
                else:
                    piece = rows[k][:, j * size : (j + 1) * size]
                o_ref[j, :, at : at + size] = piece
                at += size

    out = jax.ShapeDtypeStruct((count, 1, lanes), F32)
    return pl.pallas_call(
        body,
        out_shape=out,
        in_specs=[SCALAR] + [WHOLE] * 4,
        out_specs=WHOLE,
        cost_estimate=CHEAP,
        compiler_params=pltpu.CompilerParams(vmem_limit_bytes=8 << 20),
        name="owner_sums",
    )(mine, qv, first, second, half)


def norm_stats(values):
    centre = jnp.mean(values, axis=-1, keepdims=True)
    centred = values - centre
    spread_of = jnp.mean(centred * centred, axis=-1, keepdims=True)
    inverse = lax.rsqrt(spread_of + EPS)
    return centred * inverse, inverse


def norm_back(normed, inverse, gain, upstream):
    scaled = upstream * gain
    first = jnp.mean(scaled, axis=-1, keepdims=True)
    second = jnp.mean(scaled * normed, axis=-1, keepdims=True)
    return (scaled - first - normed * second) * inverse


def dot(left, right):
    return jnp.dot(left, right, preferred_element_type=F32)


def dot_rows(left, right):
    return lax.dot_general(left, right, (((0,), (0,)), ((), ())), preferred_element_type=F32)


def dot_back(left, right):
    return lax.dot_general(left, right, (((1,), (1,)), ((), ())), preferred_element_type=F32)


def build(mesh):
    count = mesh.devices.size
    roles = bit_roles(mesh)
    every = list(range(len(roles)))

    def of(role):
        return [b for b in reversed(every) if roles[b] == role]

    core = roles.index("c")
    chips = [b for b in every if b != core]
    deep = of("z")
    one = deep + of("x") + of("y")
    two = deep + of("y") + of("x")
    flat_one, flat_two = of("x") + of("y"), of("y") + of("x")

    def chip_position(bit):
        return bit if bit < core else bit - 1

    def on_device(
        tokens,
        cotangent,
        target,
        lengths,
        w_qkv,
        qv_bias,
        w_out,
        out_bias,
        gain_one,
        shift_one,
        w_up,
        up_bias,
        w_down,
        down_bias,
        gain_two,
        shift_two,
    ):
        me = lax.axis_index(AXES).astype(I32)
        my_core = (me >> core) & 1
        mine = me.reshape(1)
        low = me & ((1 << core) - 1)
        my_chip = (((me >> (core + 1)) << core) | low).reshape(1)
        batches, slot, width = tokens.shape
        rows = batches * slot
        per = slot // count
        place = jnp.arange(slot, dtype=I32)
        unit_block = (FF // count) << core
        hidden = FF // 2

        even, odd = halves_of(w_up, unit_block)
        up_send = jnp.where(my_core == 0, odd, even)
        up_hold = jnp.where(my_core == 0, even, odd)
        chain_attn = Gather(jnp.concatenate([w_qkv, w_out], axis=1)[None], deep, count)
        up_got = swap(up_send, core, count)
        chain_up = Gather(jnp.stack([up_hold, up_got]), deep, count)
        down_order = flat_two + deep
        chain_down = Gather(w_down[None], down_order, count)

        smalls = [qv_bias, out_bias, gain_one, shift_one, up_bias, down_bias, gain_two, shift_two]
        sizes = [v.shape[0] for v in smalls]
        packed = jnp.concatenate(smalls)
        total = packed.shape[0]

        rank = jnp.sum((target[:, None, :] < target[:, :, None]).astype(I32), axis=2)
        chosen = (rank[:, None, :] == place[None, :, None]).astype(BF)
        slots = (target % slot).astype(BF)
        out_rows = jnp.einsum("bri,bid->brd", chosen, tokens, preferred_element_type=F32).astype(BF)
        out_up = jnp.einsum("bri,bid->brd", chosen, cotangent, preferred_element_type=F32).astype(BF)
        out_slots = jnp.einsum("bri,bi->br", chosen, slots, preferred_element_type=F32).astype(BF)

        def by_device(v):
            return v.reshape((batches, count, per) + v.shape[2:]).swapaxes(0, 1).reshape(
                (count, batches * per) + v.shape[2:]
            )

        extra_rows = batches * per
        held = 64
        spans = -(-total // held)
        side = jnp.pad(packed, (0, spans * held - total)).reshape(spans, held)
        side = jnp.pad(side, ((0, extra_rows - spans), (0, 127 - held)))
        payload = jnp.concatenate(
            [
                by_device(out_rows),
                jnp.broadcast_to(side[None], (count, extra_rows, 127)),
                by_device(out_slots)[..., None],
            ],
            axis=2,
        )
        first = lax.all_to_all(payload, AXES, split_axis=0, concat_axis=0, tiled=True)
        flat, zs = len(flat_one), len(deep)
        for _ in range(zs):
            chain_attn.step()
        for _ in range(flat):
            chain_down.step()
        attn = chain_attn.all()
        chain_qk = Gather(attn[:, :, : 2 * D], flat_one + [core], count)
        chain_vo = Gather(attn[:, :, 2 * D :], flat_two + [core], count)
        for k in range(flat):
            chain_qk.step()
            chain_vo.step()
            if k == 0:
                chain_up.step(chain_attn.got)
                for _ in range(zs - 1):
                    chain_up.step()

        def by_batch(v):
            return v.reshape((count, batches, per) + v.shape[2:]).swapaxes(0, 1).reshape(
                (batches, slot) + v.shape[2:]
            )

        x, put, *vectors = receive(by_batch(first), sizes, count, batches, slot, held)
        qv_b, out_b, gain1, shift1, up_b, down_b, gain2, shift2 = vectors

        after_chips = (chain_qk.got, chain_vo.got)
        chain_qk.step(x)
        chain_vo.step(x)
        ups = chain_up.all()
        chain_gate = Gather(ups[:, :, :hidden], flat_one, count)
        chain_lin = Gather(ups[:, :, hidden:], flat_two, count)
        for _ in range(flat - 1):
            chain_gate.step(*after_chips)
            chain_lin.step(*after_chips)
            after_chips = ()
        for _ in range(zs - 1):
            chain_down.step(chain_up.got)
        bounds = jnp.cumsum(lengths[:, 0], axis=-1)
        segment = jnp.sum((bounds[:, :, None] <= place).astype(I32), axis=1)
        slopes = jnp.exp2(-8.0 * (jnp.arange(HEADS, dtype=F32) + 1.0) / HEADS)

        weights = settle(
            mine,
            (chain_qk.held, chain_qk.got, one + [core]),
            (chain_vo.held, chain_vo.got, two + [core]),
        ).reshape(D, 4 * D)
        qk, v = project(x, weights, qv_b)
        qk = tie(qk, chain_gate.got, chain_lin.got)
        chain_gate.step()
        chain_lin.step()
        merged, probs = attend(qk, v, segment[:, None, :], segment[:, :, None], slopes, batches, slot)
        chain_down.got = tie(chain_down.got, merged)
        chain_down.step()
        r1, h = first_norm(x, merged, weights, out_b, gain1, shift1)

        h_other = swap(h, core, count)
        second = lax.all_to_all(tie(by_device(out_up), h), AXES, split_axis=0, concat_axis=0, tiled=True)
        w_gate = settle(mine, (chain_gate.held, chain_gate.got, [core] + one)).reshape(D, hidden)
        w_lin = settle(mine, (chain_lin.held, chain_lin.got, [core] + two)).reshape(D, hidden)
        even_b, odd_b = halves_of(up_b, unit_block)
        a, slope_low, act_low = units(mine, h, h_other, w_gate, w_lin, even_b, odd_b, core)
        down_got = tie(chain_down.got, a)
        w_dn = settle(
            my_chip, (chain_down.held, down_got, [chip_position(b) for b in down_order])
        ).reshape(hidden, D)
        down, down_send = down_product(a, w_dn)
        down_other = swap(down_send, core, count)
        e = jnp.einsum("bkp,bkd->bpd", put, by_batch(second), preferred_element_type=F32).reshape(rows, D)
        result, dr2, df, sums2 = second_norm(h, down, down_other, e, down_b, gain2, shift2)

        def back(rows_here, *after):
            sent = jnp.einsum(
                "bkp,bpd->bkd", put, rows_here.reshape(batches, slot, D), preferred_element_type=F32
            ).astype(BF)
            return lax.all_to_all(tie(by_device(sent), *after), AXES, split_axis=0, concat_axis=0, tiled=True)

        def given(got):
            return jnp.einsum("bri,brd->bid", chosen, by_batch(got), preferred_element_type=F32).astype(BF)

        df_other = swap(df, core, count)
        g_down = down_weight_grad(a, df, df_other).reshape(count // 2, FF // count, D)
        scatter_down = Scatter(mine, pieces_of([g_down]), None, chips, None, deep[::-1][:1] + flat_two[::-1] + deep[::-1][1:], count)
        scatter_down.step()
        du1, du2, g_half_b = units_back(tie(df, scatter_down.sent), df_other, w_dn, slope_low, act_low)
        blocks = (count, D // count, -1)
        g_gate = up_weight_grad(h, h_other, du1).reshape(blocks)
        scatter_gate = Scatter(mine, pieces_of([g_gate]), None, every, None, flat_one[::-1], count)
        scatter_gate.step()
        du2 = tie(du2, scatter_gate.sent)
        g_lin = up_weight_grad(h, h_other, du2).reshape(blocks)
        scatter_lin = Scatter(mine, pieces_of([g_lin]), None, every, None, flat_two[::-1], count)
        scatter_lin.step()
        du1 = tie(du1, scatter_lin.sent)
        dh_own, dh_send = hidden_back(du1, du2, w_gate, w_lin)
        scatter_down.step(dh_own)
        dh_other = swap(tie(dh_send, scatter_down.sent), core, count)
        scatter_gate.step(scatter_down.sent)
        scatter_lin.step(scatter_gate.sent)
        dr1, dbr, do, sums1 = first_norm_back(
            tie(dh_own, scatter_lin.sent), dh_other, dr2, r1, gain1, weights
        )
        back_out = back(result, do)
        dqk, dv = attend_back(qk, v, probs, do, batches, slot)
        g_qk, g_v, g_out, qv_sums = attention_weight_grads(x, dqk, dv, merged, dbr)
        g_qk, g_v, g_out = g_qk.reshape(blocks), g_v.reshape(blocks), g_out.reshape(blocks)

        scatter_up = scatter_gate.beside(scatter_lin, deep[::-1] + [core])
        scatter_up.step(g_out)
        scatter_attn = Scatter(mine, pieces_of([g_qk, g_v, g_out]), None, every, None, [core], count)
        scatter_attn.step(scatter_up.sent, back_out)
        dx = input_back(tie(dr1, scatter_attn.sent), dqk, dv, weights)
        last = dx

        def go(chain):
            nonlocal last
            chain.step(last)
            last = chain.sent

        scatter_qk = scatter_attn.part(0, 2 * D, flat_one[::-1])
        scatter_vo = scatter_attn.part(2 * D, 4 * D, flat_two[::-1])
        back_dx = back(dx)
        for _ in range(flat):
            go(scatter_qk)
            go(scatter_vo)
            if scatter_down.at < len(one):
                go(scatter_down)
        small_send = owner_sums(
            tie(mine, last), qv_sums, sums1, sums2, g_half_b, sizes, count, unit_block, core
        )
        small_got = lax.all_to_all(small_send, AXES, split_axis=0, concat_axis=0, tiled=True)
        small_sum = jnp.sum(small_got, axis=(0, 1))

        while scatter_up.at < len(deep):
            go(scatter_up)
        scatter_attn = scatter_qk.beside(scatter_vo, deep[::-1])
        scatter_attn.step(last, back_dx)
        last = scatter_attn.sent
        while scatter_down.at < len(one):
            go(scatter_down)
        up_last = scatter_up.ready(last)[0]
        up_kept = scatter_up.kept[0][0][0]
        up_came = swap(up_last, core, count)
        last = up_last
        while scatter_attn.at < len(deep):
            scatter_attn.step(last)
            last = scatter_attn.sent
        out_tokens = given(back_out)
        grad_tokens = given(back_dx)
        s_up = join_halves(
            jnp.where(my_core == 0, up_kept, up_came), jnp.where(my_core == 0, up_came, up_kept), unit_block
        )
        s_attn = scatter_attn.total()
        outs, at = [], 0
        for size in sizes:
            outs.append(small_sum[at : at + size])
            at += size
        return (
            out_tokens,
            grad_tokens,
            s_attn[:, : 3 * D],
            outs[0],
            s_attn[:, 3 * D : 4 * D],
            outs[1],
            outs[2],
            outs[3],
            s_up,
            outs[4],
            scatter_down.total(),
            outs[5],
            outs[6],
            outs[7],
        )

    return on_device


def solution(mesh):
    rows = P(None, AXES, None)
    matrix, vector = P(AXES, None), P(AXES)
    return jax.shard_map(
        build(mesh),
        mesh=mesh,
        in_specs=(rows, rows, P(None, AXES), rows)
        + (matrix, vector, matrix, vector, vector, vector, matrix, vector, matrix, vector, vector, vector),
        out_specs=(rows, rows)
        + (matrix, vector, matrix, vector, vector, vector, matrix, vector, matrix, vector, vector, vector),
        check_vma=False,
    )
```

```python
import jax
import jax.numpy as jnp
from jax import lax
from jax.experimental import pallas as pl
from jax.experimental.pallas import tpu as pltpu
from jax.sharding import PartitionSpec as P

D = 768
HEADS = 12
HEAD_DIM = 64
FF = 3072

EPS = 1e-05
NEGATIVE = -1e30
AXES = ("dp", "fsdp")
BF = jnp.bfloat16
F32 = jnp.float32
I32 = jnp.int32


def bit_roles(mesh):
    devices = mesh.devices.reshape(-1)
    count = devices.size.bit_length() - 1
    roles = []
    for bit in range(count):
        here, there = devices[0], devices[1 << bit]
        a, b = getattr(here, "coords", None), getattr(there, "coords", None)
        if a is None or b is None:
            roles.append("cyxzzzzzzz"[bit])
        elif tuple(a) == tuple(b):
            roles.append("c")
        else:
            roles.append("xyz"[[i for i in range(3) if a[i] != b[i]][0]])
    return roles


def swap(value, bit, count):
    return lax.ppermute(value, AXES, [(i, i ^ (1 << bit)) for i in range(count)])


def tie(value, *others):
    if not others:
        return value
    return lax.optimization_barrier((value,) + tuple(others))[0]


CHEAP = pl.CostEstimate(flops=1000, bytes_accessed=1000, transcendentals=0)


SCALAR = pl.BlockSpec(memory_space=pltpu.SMEM)
WHOLE = pl.BlockSpec(memory_space=pltpu.VMEM)


def grant(*arrays):
    total = sum(a.size * a.dtype.itemsize for a in arrays)
    return pltpu.CompilerParams(vmem_limit_bytes=min(2 * total + (4 << 20), 60 << 20))


def spread(t, positions):
    out = 0
    for k, position in enumerate(positions):
        out = out | (((t >> k) & 1) << position)
    return out


def settle(mine, *parts):
    half, rows, _ = parts[0][0].shape
    spans, columns = [], 0
    for first, _, _ in parts:
        spans.append(slice(columns, columns + first.shape[2]))
        columns += first.shape[2]

    def body(mine_ref, *refs):
        me, o_ref = mine_ref[0], refs[-1]

        def move(t, carry):
            for k, (here, (_, _, order)) in enumerate(zip(spans, parts)):
                o_ref[me ^ spread(t, order), :, here] = refs[2 * k][t]
                o_ref[me ^ spread(t + half, order), :, here] = refs[2 * k + 1][t]
            return carry

        lax.fori_loop(0, half, move, 0)

    arrays = [a for part in parts for a in part[:2]]
    out = jax.ShapeDtypeStruct((2 * half, rows, columns), BF)
    return pl.pallas_call(
        body,
        out_shape=out,
        in_specs=[SCALAR] + [WHOLE] * len(arrays),
        out_specs=WHOLE,
        cost_estimate=CHEAP,
        compiler_params=grant(*arrays, out),
        name="settle",
    )(mine, *arrays)


def insert_bit(index, position, value):
    low = index & ((1 << position) - 1)
    return ((index >> position) << (position + 1)) | (value << position) | low


def pieces_of(arrays):
    return [(a, 0, a.shape[2]) for a in arrays]


def cut(pieces, low, high):
    out, at = [], 0
    for array, start, width in pieces:
        lo, hi = max(low, at), min(high, at + width)
        if lo < hi:
            out.append((array, start + lo - at, hi - lo))
        at += width
    return out


def segments(*lists):
    edges = {0}
    for pieces in lists:
        at = 0
        for _, _, width in pieces:
            at += width
            edges.add(at)
    edges = sorted(edges)
    out = []
    for low, high in zip(edges, edges[1:]):
        found = []
        for pieces in lists:
            at = 0
            for k, (_, start, width) in enumerate(pieces):
                if at <= low < at + width:
                    found.append((k, start + low - at))
                at += width
        out.append((low, high, found))
    return out


def pick(mine, pieces, position, bit):
    blocks, rows, _ = pieces[0][0].shape
    spans = segments(pieces)
    columns = spans[-1][1]

    def body(mine_ref, *refs):
        o_ref = refs[-1]
        other = 1 - ((mine_ref[0] >> bit) & 1)

        def move(t, carry):
            index = insert_bit(t, position, other)
            for low, high, ((k, at),) in spans:
                o_ref[t, :, low:high] = refs[k][index, :, at : at + high - low]
            return carry

        lax.fori_loop(0, blocks // 2, move, 0)

    sources = [p[0] for p in pieces]
    out = jax.ShapeDtypeStruct((blocks // 2, rows, columns), BF)
    return pl.pallas_call(
        body,
        out_shape=out,
        in_specs=[SCALAR] + [WHOLE] * len(sources),
        out_specs=WHOLE,
        cost_estimate=CHEAP,
        compiler_params=grant(*sources, out),
        name="pick",
    )(mine, *sources)


def fold(mine, kept, got, now, position, bit):
    blocks, rows, _ = got[0][0].shape
    spans = segments(kept, got)
    columns = spans[-1][1]

    def body(mine_ref, *refs):
        k_refs, r_refs, s_ref, n_ref = refs[: len(kept)], refs[len(kept) : -2], refs[-2], refs[-1]
        side = (mine_ref[0] >> bit) & 1

        def put_total(out_ref, t, index):
            source = index
            if now is not None:
                source = insert_bit(index, now[0], (mine_ref[0] >> now[1]) & 1)
            for low, high, ((k, at), (r, start)) in spans:
                wide = high - low
                total = k_refs[k][source, :, at : at + wide].astype(F32)
                total += r_refs[r][index, :, start : start + wide].astype(F32)
                out_ref[t, :, low:high] = total.astype(BF)

        def move(t, carry):
            put_total(s_ref, t, insert_bit(t, position, 1 - side))
            put_total(n_ref, t, insert_bit(t, position, side))
            return carry

        lax.fori_loop(0, blocks // 2, move, 0)

    sources = [p[0] for p in kept + got]
    out = jax.ShapeDtypeStruct((blocks // 2, rows, columns), BF)
    return pl.pallas_call(
        body,
        out_shape=(out, out),
        in_specs=[SCALAR] + [WHOLE] * len(sources),
        out_specs=[WHOLE] * 2,
        cost_estimate=CHEAP,
        compiler_params=grant(*sources, out, out),
        name="fold",
    )(mine, *sources)


class Gather:
    def __init__(self, block, order, count):
        self.held, self.order, self.count, self.at = block, order, count, 0
        self.got = None

    def all(self, *after):
        if self.got is None:
            return tie(self.held, *after)
        return tie(jnp.concatenate([self.held, self.got], axis=0), *after)

    def step(self, *after):
        self.held = self.all(*after)
        self.got = swap(self.held, self.order[self.at], self.count)
        self.at += 1
        return self.got


class Scatter:
    def __init__(self, mine, kept, got, left, now, order, count):
        self.mine, self.kept, self.got, self.left = mine, kept, got, list(left)
        self.now, self.order, self.count, self.at, self.sent = now, order, count, 0, None

    def part(self, low, high, order):
        return Scatter(
            self.mine, cut(self.kept, low, high), cut(self.got, low, high), self.left, self.now, order, self.count
        )

    def beside(self, other, order):
        return Scatter(
            self.mine, self.kept + other.kept, self.got + other.got, self.left, None, order, self.count
        )

    def ready(self, *after):
        bit = self.order[self.at]
        position = self.left.index(bit)
        if self.got is None:
            kept = [(tie(a, *after), at, width) for a, at, width in self.kept[:1]] + self.kept[1:]
            self.kept = kept
            self.sent = pick(self.mine, kept, position, bit)
            self.now = (position, bit)
        else:
            got = [(tie(a, *after), at, width) for a, at, width in self.got[:1]] + self.got[1:]
            self.sent, rest = fold(self.mine, self.kept, got, self.now, position, bit)
            self.kept, self.now = pieces_of([rest]), None
        return self.sent

    def step(self, *after):
        self.ready(*after)
        bit = self.order[self.at]
        self.got = pieces_of([swap(self.sent, bit, self.count)])
        self.left.remove(bit)
        self.at += 1
        return self.got

    def total(self):
        return self.kept[0][0][0].astype(F32) + self.got[0][0][0].astype(F32)


def halves_of(shard, block):
    pieces = shard.shape[1] // (2 * block)

    def body(w_ref, even_ref, odd_ref):
        values = w_ref[...].astype(F32)
        for out, start in ((even_ref, 0), (odd_ref, block)):
            parts = [values[:, i * 2 * block + start : i * 2 * block + start + block] for i in range(pieces)]
            out[...] = jnp.concatenate(parts, axis=1).astype(out.dtype)

    out = jax.ShapeDtypeStruct((shard.shape[0], shard.shape[1] // 2), shard.dtype)
    return pl.pallas_call(
        body, out_shape=(out, out), cost_estimate=CHEAP, compiler_params=grant(shard, out, out), name="halves"
    )(shard)


def join_halves(even, odd, block):
    pieces = even.shape[1] // block

    def body(even_ref, odd_ref, o_ref):
        a, b = even_ref[...].astype(F32), odd_ref[...].astype(F32)
        parts = []
        for i in range(pieces):
            parts += [a[:, i * block : (i + 1) * block], b[:, i * block : (i + 1) * block]]
        o_ref[...] = jnp.concatenate(parts, axis=1)

    out = jax.ShapeDtypeStruct((even.shape[0], 2 * even.shape[1]), F32)
    return pl.pallas_call(
        body, out_shape=out, cost_estimate=CHEAP, compiler_params=grant(even, odd, out, out), name="join"
    )(even, odd)


def attend(qk, v, segment_row, segment_column, slopes, batches, slot):
    pairs = HEADS // 2
    width = 2 * HEAD_DIM

    def body(slope_ref, qk_ref, v_ref, row_ref, column_ref, o_ref, p_ref):
        pair = pl.program_id(1)
        at = pl.multiple_of(pair * width, width)
        query = qk_ref[:, pl.ds(at, width)]
        keyed = qk_ref[:, pl.ds(D + at, width)]
        value = v_ref[:, pl.ds(at, width)]
        lane = lax.broadcasted_iota(I32, (slot, width), 1)
        gap = jnp.abs(
            lax.broadcasted_iota(I32, (slot, slot), 0) - lax.broadcasted_iota(I32, (slot, slot), 1)
        ).astype(F32)
        same = column_ref[0] == row_ref[0]
        mixed = []
        for which in range(2):
            own = (lane >= HEAD_DIM) if which else (lane < HEAD_DIM)
            only = jnp.where(own, query, jnp.zeros_like(query))
            scores = lax.dot_general(only, keyed, (((1,), (1,)), ((), ())), preferred_element_type=F32)
            scores = jnp.where(same, scores * 0.125 - slope_ref[2 * pair + which] * gap, NEGATIVE)
            raised = jnp.exp(scores - jnp.max(scores, axis=1, keepdims=True))
            probs = (raised / jnp.sum(raised, axis=1, keepdims=True)).astype(BF)
            p_ref[0, 0, which] = probs
            mixed.append(jnp.dot(probs, value, preferred_element_type=F32))
        o_ref[:, pl.ds(at, width)] = jnp.where(lane < HEAD_DIM, mixed[0], mixed[1]).astype(BF)

    rows = batches * slot
    merged = jax.ShapeDtypeStruct((rows, D), BF)
    probs = jax.ShapeDtypeStruct((batches, pairs, 2, slot, slot), BF)
    return pl.pallas_call(
        body,
        out_shape=(merged, probs),
        grid=(batches, pairs),
        in_specs=[
            pl.BlockSpec(memory_space=pltpu.SMEM),
            pl.BlockSpec((slot, 2 * D), lambda b, h: (b, 0)),
            pl.BlockSpec((slot, D), lambda b, h: (b, 0)),
            pl.BlockSpec((1, 1, slot), lambda b, h: (b, 0, 0)),
            pl.BlockSpec((1, slot, 1), lambda b, h: (b, 0, 0)),
        ],
        out_specs=[
            pl.BlockSpec((slot, D), lambda b, h: (b, 0)),
            pl.BlockSpec((1, 1, 2, slot, slot), lambda b, h: (b, h, 0, 0, 0)),
        ],
        cost_estimate=CHEAP,
        compiler_params=pltpu.CompilerParams(vmem_limit_bytes=24 * 1024 * 1024),
        name="attend",
    )(slopes, qk, v, segment_row, segment_column)


def attend_back(qk, v, probs, do, batches, slot):
    pairs = HEADS // 2
    width = 2 * HEAD_DIM
    first = (((0,), (0,)), ((), ()))
    second = (((1,), (1,)), ((), ()))

    def body(qk_ref, v_ref, p_ref, do_ref, dqk_ref, dv_ref):
        at = pl.multiple_of(pl.program_id(1) * width, width)
        query = qk_ref[:, pl.ds(at, width)]
        keyed = qk_ref[:, pl.ds(D + at, width)]
        value = v_ref[:, pl.ds(at, width)]
        upstream = do_ref[:, pl.ds(at, width)]
        lane = lax.broadcasted_iota(I32, (slot, width), 1)
        dq, dk, dv = [], [], []
        for which in range(2):
            own = (lane >= HEAD_DIM) if which else (lane < HEAD_DIM)
            low = p_ref[0, 0, which]
            high = low.astype(F32)
            only = jnp.where(own, upstream, jnp.zeros_like(upstream))
            dp = lax.dot_general(only, value, second, preferred_element_type=F32)
            delta = jnp.sum(high * dp, axis=1, keepdims=True)
            ds = (high * (dp - delta)).astype(BF)
            dq.append(jnp.dot(ds, keyed, preferred_element_type=F32))
            dk.append(lax.dot_general(ds, query, first, preferred_element_type=F32))
            dv.append(lax.dot_general(low, upstream, first, preferred_element_type=F32))
        early = lane < HEAD_DIM
        dqk_ref[:, pl.ds(at, width)] = (jnp.where(early, dq[0], dq[1]) * 0.125).astype(BF)
        dqk_ref[:, pl.ds(D + at, width)] = (jnp.where(early, dk[0], dk[1]) * 0.125).astype(BF)
        dv_ref[:, pl.ds(at, width)] = jnp.where(early, dv[0], dv[1]).astype(BF)

    rows = batches * slot
    return pl.pallas_call(
        body,
        out_shape=(jax.ShapeDtypeStruct((rows, 2 * D), BF), jax.ShapeDtypeStruct((rows, D), BF)),
        grid=(batches, pairs),
        in_specs=[
            pl.BlockSpec((slot, 2 * D), lambda b, h: (b, 0)),
            pl.BlockSpec((slot, D), lambda b, h: (b, 0)),
            pl.BlockSpec((1, 1, 2, slot, slot), lambda b, h: (b, h, 0, 0, 0)),
            pl.BlockSpec((slot, D), lambda b, h: (b, 0)),
        ],
        out_specs=[
            pl.BlockSpec((slot, 2 * D), lambda b, h: (b, 0)),
            pl.BlockSpec((slot, D), lambda b, h: (b, 0)),
        ],
        cost_estimate=CHEAP,
        compiler_params=pltpu.CompilerParams(vmem_limit_bytes=24 * 1024 * 1024),
        name="attend_back",
    )(qk, v, probs, do)


TILE = 256
ROWS = (((0,), (0,)), ((), ()))
BACK = (((1,), (1,)), ((), ()))


def in_vmem(body, outs, *arrays, name):
    total = sum(a.size * a.dtype.itemsize for a in arrays + tuple(outs))
    return pl.pallas_call(
        body,
        out_shape=tuple(outs),
        in_specs=[WHOLE] * len(arrays),
        out_specs=tuple([WHOLE] * len(outs)),
        cost_estimate=CHEAP,
        compiler_params=pltpu.CompilerParams(vmem_limit_bytes=min(total + (16 << 20), 62 << 20)),
        name=name,
    )(*arrays)


def product(left, right, dims):
    return lax.dot_general(left, right, dims, preferred_element_type=F32)


def tiles(count, step):
    def run(i, carry):
        step(pl.multiple_of(i * TILE, TILE))
        return carry

    lax.fori_loop(0, count // TILE, run, 0)


def receive(arrived, sizes, count, batches, slot, held):
    per = slot // count
    spans = -(-sum(sizes) // held)

    def body(in_ref, x_ref, put_ref, *refs):
        outs, side_ref = refs[:-1], refs[-1]
        for b in range(batches):
            slots = in_ref[b, :, D:].astype(F32)[:, 127:128]
            put = (slots == lax.broadcasted_iota(I32, (slot, slot), 1).astype(F32)).astype(F32).astype(BF)
            put_ref[b] = put
            x_ref[b * slot : (b + 1) * slot, :] = product(put, in_ref[b, :, :D], ROWS).astype(BF)
        side_ref[...] = in_ref[0, :, D:].astype(F32)
        flat = jnp.concatenate(
            [side_ref[pl.ds(r, count, stride=per), :][:, :held] for r in range(spans)], axis=1
        )
        at = 0
        for out, size in zip(outs, sizes):
            for j in range(count):
                out[:, j * size : (j + 1) * size] = flat[j : j + 1, at : at + size]
            at += size

    outs = [
        jax.ShapeDtypeStruct((batches * slot, D), BF),
        jax.ShapeDtypeStruct((batches, slot, slot), BF),
    ] + [jax.ShapeDtypeStruct((1, count * size), F32) for size in sizes]
    return pl.pallas_call(
        body,
        out_shape=tuple(outs),
        in_specs=[WHOLE],
        out_specs=tuple([WHOLE] * len(outs)),
        scratch_shapes=[pltpu.VMEM((slot, 128), F32)],
        cost_estimate=CHEAP,
        compiler_params=pltpu.CompilerParams(vmem_limit_bytes=20 << 20),
        name="receive",
    )(arrived)


def project(x, weights, bias):
    def body(x_ref, w_ref, b_ref, qk_ref, v_ref):
        def step(at):
            here = pl.ds(at, TILE)
            tile = x_ref[here, :]
            q = jnp.dot(tile, w_ref[:, :D], preferred_element_type=F32) + b_ref[:, :D]
            qk_ref[here, :D] = q.astype(BF)
            qk_ref[here, D:] = jnp.dot(tile, w_ref[:, D : 2 * D], preferred_element_type=F32).astype(BF)
            v = jnp.dot(tile, w_ref[:, 2 * D : 3 * D], preferred_element_type=F32) + b_ref[:, D:]
            v_ref[here, :] = v.astype(BF)

        tiles(x.shape[0], step)

    outs = [jax.ShapeDtypeStruct((x.shape[0], 2 * D), BF), jax.ShapeDtypeStruct((x.shape[0], D), BF)]
    return in_vmem(body, outs, x, weights, bias, name="project")


def first_norm(x, merged, weights, bias, gain, shift):
    def body(x_ref, m_ref, w_ref, b_ref, g_ref, s_ref, r_ref, h_ref):
        def step(at):
            here = pl.ds(at, TILE)
            total = x_ref[here, :].astype(F32) + b_ref[...]
            total += jnp.dot(m_ref[here, :], w_ref[:, 3 * D :], preferred_element_type=F32)
            r_ref[here, :] = total
            h_ref[here, :] = (norm_stats(total)[0] * g_ref[...] + s_ref[...]).astype(BF)

        tiles(x.shape[0], step)

    outs = [jax.ShapeDtypeStruct(x.shape, F32), jax.ShapeDtypeStruct(x.shape, BF)]
    return in_vmem(body, outs, x, merged, weights, bias, gain, shift, name="first_norm")


def near(width):
    return pl.BlockSpec((TILE, width), lambda i: (jnp.minimum(i, 1), 0))


def far(width):
    return pl.BlockSpec((TILE, width), lambda i: (jnp.maximum(i - 2, 0), 0))


def tile_of(width):
    return pl.BlockSpec((TILE, width), lambda i: (i, 0))


def fixed(*shape):
    return pl.BlockSpec(shape, lambda i: (0, 0))


TILED_GRANT = pltpu.CompilerParams(vmem_limit_bytes=32 << 20)


def units(mine, h, h_other, w_gate, w_lin, even, odd, core):
    rows, hidden = h.shape[0], w_gate.shape[1]
    assert rows == 2 * TILE

    def body(mine_ref, h_ref, o_ref, g_ref, l_ref, e_ref, d_ref, a_ref, slope_ref, act_ref):
        first = ((mine_ref[0] >> core) & 1) == 0
        tile = jnp.where(pl.program_id(0) < 2, h_ref[...], o_ref[...])
        for lo in range(0, hidden, TILE):
            wide = slice(lo, lo + TILE)
            late = slice(hidden + lo, hidden + lo + TILE)
            gate = jnp.dot(tile, g_ref[:, wide], preferred_element_type=F32)
            gate += jnp.where(first, e_ref[:, wide], d_ref[:, wide])
            lin = jnp.dot(tile, l_ref[:, wide], preferred_element_type=F32)
            lin += jnp.where(first, e_ref[:, late], d_ref[:, late])
            cdf = 0.5 * (1.0 + lax.erf(gate * (0.5**0.5)))
            act = gate * cdf
            slope = cdf + gate * jnp.exp(-0.5 * gate * gate) * (1.0 / (2.0 * jnp.pi) ** 0.5)
            a_ref[:, wide] = (act * lin).astype(BF)
            slope_ref[:, wide] = (slope * lin).astype(BF)
            act_ref[:, wide] = act.astype(BF)

    out = jax.ShapeDtypeStruct((2 * rows, hidden), BF)
    return pl.pallas_call(
        body,
        out_shape=(out, out, out),
        grid=(4,),
        in_specs=[SCALAR, near(D), far(D)] + [fixed(D, hidden)] * 2 + [fixed(1, 2 * hidden)] * 2,
        out_specs=(tile_of(hidden),) * 3,
        cost_estimate=CHEAP,
        compiler_params=TILED_GRANT,
        name="units",
    )(mine, h, h_other, w_gate, w_lin, even, odd)


def down_weight_grad(a, df, df_other):
    rows = df.shape[0]

    def body(a_ref, d_ref, o_ref, g_ref):
        def step(at):
            g = product(a_ref[:rows, pl.ds(at, TILE)], d_ref[...], ROWS)
            g += product(a_ref[rows:, pl.ds(at, TILE)], o_ref[...], ROWS)
            g_ref[pl.ds(at, TILE), :] = g.astype(BF)

        tiles(a.shape[1], step)

    out = jax.ShapeDtypeStruct((a.shape[1], df.shape[1]), BF)
    return in_vmem(body, [out], a, df, df_other, name="down_grad")[0]


def units_back(df, df_other, w_dn, slope, act):
    rows, hidden = df.shape[0], w_dn.shape[0]

    def body(d_ref, o_ref, w_ref, s_ref, a_ref, du1_ref, du2_ref, sum_ref):
        i = pl.program_id(0)
        tile = jnp.where(i < 2, d_ref[...], o_ref[...])
        da = product(tile, w_ref[...], BACK).astype(BF).astype(F32)
        du1 = (da * s_ref[...].astype(F32)).astype(BF)
        du2 = (da * a_ref[...].astype(F32)).astype(BF)
        du1_ref[...] = du1
        du2_ref[...] = du2

        @pl.when(i == 0)
        def _():
            sum_ref[...] = jnp.zeros_like(sum_ref)

        sum_ref[0:1, :] += jnp.sum(du1.astype(F32), axis=0, keepdims=True)
        sum_ref[1:2, :] += jnp.sum(du2.astype(F32), axis=0, keepdims=True)

    du = jax.ShapeDtypeStruct((2 * rows, hidden), BF)
    sums = jax.ShapeDtypeStruct((2, hidden), F32)
    return pl.pallas_call(
        body,
        out_shape=(du, du, sums),
        grid=(4,),
        in_specs=[near(D), far(D), fixed(hidden, D), tile_of(hidden), tile_of(hidden)],
        out_specs=(tile_of(hidden), tile_of(hidden), fixed(2, hidden)),
        cost_estimate=CHEAP,
        compiler_params=TILED_GRANT,
        name="units_back",
    )(df, df_other, w_dn, slope, act)


def up_weight_grad(h, h_other, du):
    rows = h.shape[0]

    def body(h_ref, o_ref, d_ref, g_ref):
        def step(at):
            g = product(h_ref[:, pl.ds(at, TILE)], d_ref[:rows, :], ROWS)
            g += product(o_ref[:, pl.ds(at, TILE)], d_ref[rows:, :], ROWS)
            g_ref[pl.ds(at, TILE), :] = g.astype(BF)

        tiles(h.shape[1], step)

    out = jax.ShapeDtypeStruct((h.shape[1], du.shape[1]), BF)
    return in_vmem(body, [out], h, h_other, du, name="up_grad")[0]


def hidden_back(du1, du2, w_gate, w_lin):
    rows, hidden = du1.shape[0] // 2, du1.shape[1]

    def body(d1_ref, d2_ref, g_ref, l_ref, own_ref, other_ref):
        dh = product(d1_ref[...], g_ref[...], BACK) + product(d2_ref[...], l_ref[...], BACK)

        @pl.when(pl.program_id(0) < 2)
        def _():
            own_ref[...] = dh

        @pl.when(pl.program_id(0) >= 2)
        def _():
            other_ref[...] = dh.astype(BF)

    own = jax.ShapeDtypeStruct((rows, D), F32)
    other = jax.ShapeDtypeStruct((rows, D), BF)
    return pl.pallas_call(
        body,
        out_shape=(own, other),
        grid=(4,),
        in_specs=[tile_of(hidden)] * 2 + [fixed(D, hidden)] * 2,
        out_specs=(near(D), far(D)),
        cost_estimate=CHEAP,
        compiler_params=TILED_GRANT,
        name="hidden_back",
    )(du1, du2, w_gate, w_lin)


def down_product(a, w_dn):
    rows = a.shape[0] // 2

    def body(a_ref, w_ref, own_ref, other_ref):
        for base, out in ((0, own_ref), (rows, other_ref)):

            def step(at, base=base, out=out):
                out[pl.ds(at, TILE), :] = jnp.dot(
                    a_ref[pl.ds(base + at, TILE), :], w_ref[...], preferred_element_type=F32
                ).astype(out.dtype)

            tiles(rows, step)

    own = jax.ShapeDtypeStruct((rows, D), F32)
    other = jax.ShapeDtypeStruct((rows, D), BF)
    return in_vmem(body, [own, other], a, w_dn, name="down_product")


def second_norm(h, down, down_other, e, down_b, gain, shift):
    rows = h.shape[0]

    def body(h_ref, d_ref, o_ref, e_ref, b_ref, g_ref, s_ref, res_ref, dr_ref, df_ref, sum_ref):
        sum_ref[...] = jnp.zeros_like(sum_ref)
        bias, gains, shifts = b_ref[...], g_ref[...], s_ref[...]

        def step(at):
            here = pl.ds(at, TILE)
            total = h_ref[here, :].astype(F32) + d_ref[here, :] + o_ref[here, :].astype(F32) + bias
            normed, inverse = norm_stats(total)
            res_ref[here, :] = (normed * gains + shifts).astype(BF)
            up = e_ref[here, :]
            dr = norm_back(normed, inverse, gains, up)
            low = dr.astype(BF)
            dr_ref[here, :] = dr
            df_ref[here, :] = low
            sum_ref[0:1, :] += jnp.sum(up * normed, axis=0, keepdims=True)
            sum_ref[1:2, :] += jnp.sum(up, axis=0, keepdims=True)
            sum_ref[2:3, :] += jnp.sum(low.astype(F32), axis=0, keepdims=True)

        tiles(rows, step)

    low, wide = jax.ShapeDtypeStruct((rows, D), BF), jax.ShapeDtypeStruct((rows, D), F32)
    outs = [low, wide, low, jax.ShapeDtypeStruct((3, D), F32)]
    return in_vmem(body, outs, h, down, down_other, e, down_b, gain, shift, name="second_norm")


def first_norm_back(dh_own, dh_other, dr2, r1, gain, w_vo):
    rows = r1.shape[0]

    def body(d_ref, o_ref, r_ref, n_ref, g_ref, w_ref, dr_ref, dbr_ref, do_ref, sum_ref):
        sum_ref[...] = jnp.zeros_like(sum_ref)

        def step(at):
            here = pl.ds(at, TILE)
            dh = d_ref[here, :] + o_ref[here, :].astype(F32) + r_ref[here, :]
            normed, inverse = norm_stats(n_ref[here, :])
            dr = norm_back(normed, inverse, g_ref[...], dh)
            low = dr.astype(BF)
            dr_ref[here, :] = dr
            dbr_ref[here, :] = low
            do_ref[here, :] = product(low, w_ref[:, 3 * D :], BACK).astype(BF)
            sum_ref[0:1, :] += jnp.sum(dh * normed, axis=0, keepdims=True)
            sum_ref[1:2, :] += jnp.sum(dh, axis=0, keepdims=True)
            sum_ref[2:3, :] += jnp.sum(low.astype(F32), axis=0, keepdims=True)

        tiles(rows, step)

    low, wide = jax.ShapeDtypeStruct((rows, D), BF), jax.ShapeDtypeStruct((rows, D), F32)
    outs = [wide, low, low, jax.ShapeDtypeStruct((3, D), F32)]
    return in_vmem(body, outs, dh_own, dh_other, dr2, r1, gain, w_vo, name="first_norm_back")


def attention_weight_grads(x, dqk, dv, merged, dbr):
    def body(x_ref, qk_ref, v_ref, m_ref, d_ref, gqk_ref, gv_ref, go_ref, sum_ref):
        def step(at):
            here = pl.ds(at, TILE)
            gqk_ref[here, :] = product(x_ref[:, here], qk_ref[...], ROWS).astype(BF)
            gv_ref[here, :] = product(x_ref[:, here], v_ref[...], ROWS).astype(BF)
            go_ref[here, :] = product(m_ref[:, here], d_ref[...], ROWS).astype(BF)

        tiles(D, step)
        sum_ref[0:1, :] = jnp.sum(qk_ref[:, :D].astype(F32), axis=0, keepdims=True)
        sum_ref[1:2, :] = jnp.sum(v_ref[...].astype(F32), axis=0, keepdims=True)

    outs = [jax.ShapeDtypeStruct((D, n * D), BF) for n in (2, 1, 1)] + [jax.ShapeDtypeStruct((2, D), F32)]
    return in_vmem(body, outs, x, dqk, dv, merged, dbr, name="attention_grads")


def input_back(dr1, dqk, dv, weights):
    def body(r_ref, qk_ref, v_ref, w_ref, out_ref):
        def step(at):
            here = pl.ds(at, TILE)
            dx = r_ref[here, :] + product(qk_ref[here, :], w_ref[:, : 2 * D], BACK)
            out_ref[here, :] = (dx + product(v_ref[here, :], w_ref[:, 2 * D : 3 * D], BACK)).astype(BF)

        tiles(dr1.shape[0], step)

    return in_vmem(body, [jax.ShapeDtypeStruct(dr1.shape, BF)], dr1, dqk, dv, weights, name="input_back")[0]


def owner_sums(mine, qv, first, second, half, sizes, count, block, core):
    total = sum(sizes)
    lanes = total + -total % 128

    def body(mine_ref, q_ref, f_ref, s_ref, u_ref, o_ref):
        mine_side = (mine_ref[0] >> core) & 1
        pieces = []
        for g in range(2):
            for i in range(u_ref.shape[1] // block):
                part = u_ref[g : g + 1, i * block : (i + 1) * block]
                for side in range(2):
                    pieces.append(jnp.where(mine_side == side, part, 0.0))
        up = jnp.concatenate(pieces, axis=1)
        rows = [None] + [r[i : i + 1, :] for r, i in ((f_ref, 2), (f_ref, 0), (f_ref, 1))]
        rows += [up] + [r[i : i + 1, :] for r, i in ((s_ref, 2), (s_ref, 0), (s_ref, 1))]
        o_ref[...] = jnp.zeros_like(o_ref)
        for j in range(count):
            at = 0
            for k, size in enumerate(sizes):
                if k == 0:
                    row, lo = divmod(j * size, D)
                    piece = q_ref[row : row + 1, lo : lo + size]
                else:
                    piece = rows[k][:, j * size : (j + 1) * size]
                o_ref[j, :, at : at + size] = piece
                at += size

    out = jax.ShapeDtypeStruct((count, 1, lanes), F32)
    return pl.pallas_call(
        body,
        out_shape=out,
        in_specs=[SCALAR] + [WHOLE] * 4,
        out_specs=WHOLE,
        cost_estimate=CHEAP,
        compiler_params=pltpu.CompilerParams(vmem_limit_bytes=8 << 20),
        name="owner_sums",
    )(mine, qv, first, second, half)


def norm_stats(values):
    centre = jnp.mean(values, axis=-1, keepdims=True)
    centred = values - centre
    spread_of = jnp.mean(centred * centred, axis=-1, keepdims=True)
    inverse = lax.rsqrt(spread_of + EPS)
    return centred * inverse, inverse


def norm_back(normed, inverse, gain, upstream):
    scaled = upstream * gain
    first = jnp.mean(scaled, axis=-1, keepdims=True)
    second = jnp.mean(scaled * normed, axis=-1, keepdims=True)
    return (scaled - first - normed * second) * inverse


def dot(left, right):
    return jnp.dot(left, right, preferred_element_type=F32)


def dot_rows(left, right):
    return lax.dot_general(left, right, (((0,), (0,)), ((), ())), preferred_element_type=F32)


def dot_back(left, right):
    return lax.dot_general(left, right, (((1,), (1,)), ((), ())), preferred_element_type=F32)


def build(mesh):
    count = mesh.devices.size
    roles = bit_roles(mesh)
    every = list(range(len(roles)))

    def of(role):
        return [b for b in reversed(every) if roles[b] == role]

    core = roles.index("c")
    chips = [b for b in every if b != core]
    deep = of("z")
    one = deep + of("x") + of("y")
    two = deep + of("y") + of("x")
    flat_one, flat_two = of("x") + of("y"), of("y") + of("x")

    def chip_position(bit):
        return bit if bit < core else bit - 1

    def on_device(
        tokens,
        cotangent,
        target,
        lengths,
        w_qkv,
        qv_bias,
        w_out,
        out_bias,
        gain_one,
        shift_one,
        w_up,
        up_bias,
        w_down,
        down_bias,
        gain_two,
        shift_two,
    ):
        me = lax.axis_index(AXES).astype(I32)
        my_core = (me >> core) & 1
        mine = me.reshape(1)
        low = me & ((1 << core) - 1)
        my_chip = (((me >> (core + 1)) << core) | low).reshape(1)
        batches, slot, width = tokens.shape
        rows = batches * slot
        per = slot // count
        place = jnp.arange(slot, dtype=I32)
        unit_block = (FF // count) << core
        hidden = FF // 2

        even, odd = halves_of(w_up, unit_block)
        up_send = jnp.where(my_core == 0, odd, even)
        up_hold = jnp.where(my_core == 0, even, odd)
        chain_attn = Gather(jnp.concatenate([w_qkv, w_out], axis=1)[None], deep, count)
        up_got = swap(up_send, core, count)
        chain_up = Gather(jnp.stack([up_hold, up_got]), deep, count)
        down_order = flat_two + deep
        chain_down = Gather(w_down[None], down_order, count)

        smalls = [qv_bias, out_bias, gain_one, shift_one, up_bias, down_bias, gain_two, shift_two]
        sizes = [v.shape[0] for v in smalls]
        packed = jnp.concatenate(smalls)
        total = packed.shape[0]

        rank = jnp.sum((target[:, None, :] < target[:, :, None]).astype(I32), axis=2)
        chosen = (rank[:, None, :] == place[None, :, None]).astype(BF)
        slots = (target % slot).astype(BF)
        out_rows = jnp.einsum("bri,bid->brd", chosen, tokens, preferred_element_type=F32).astype(BF)
        out_up = jnp.einsum("bri,bid->brd", chosen, cotangent, preferred_element_type=F32).astype(BF)
        out_slots = jnp.einsum("bri,bi->br", chosen, slots, preferred_element_type=F32).astype(BF)

        def by_device(v):
            return v.reshape((batches, count, per) + v.shape[2:]).swapaxes(0, 1).reshape(
                (count, batches * per) + v.shape[2:]
            )

        extra_rows = batches * per
        held = 64
        spans = -(-total // held)
        side = jnp.pad(packed, (0, spans * held - total)).reshape(spans, held)
        side = jnp.pad(side, ((0, extra_rows - spans), (0, 127 - held)))
        payload = jnp.concatenate(
            [
                by_device(out_rows),
                jnp.broadcast_to(side[None], (count, extra_rows, 127)),
                by_device(out_slots)[..., None],
            ],
            axis=2,
        )
        first = lax.all_to_all(payload, AXES, split_axis=0, concat_axis=0, tiled=True)
        flat, zs = len(flat_one), len(deep)
        for _ in range(zs):
            chain_attn.step()
        for _ in range(flat):
            chain_down.step()
        attn = chain_attn.all()
        chain_qk = Gather(attn[:, :, : 2 * D], flat_one + [core], count)
        chain_vo = Gather(attn[:, :, 2 * D :], flat_two + [core], count)
        for k in range(flat):
            chain_qk.step()
            chain_vo.step()
            if k == 0:
                chain_up.step(chain_attn.got)
                for _ in range(zs - 1):
                    chain_up.step()

        def by_batch(v):
            return v.reshape((count, batches, per) + v.shape[2:]).swapaxes(0, 1).reshape(
                (batches, slot) + v.shape[2:]
            )

        x, put, *vectors = receive(by_batch(first), sizes, count, batches, slot, held)
        qv_b, out_b, gain1, shift1, up_b, down_b, gain2, shift2 = vectors

        after_chips = (chain_qk.got, chain_vo.got)
        chain_qk.step(x)
        chain_vo.step(x)
        ups = chain_up.all()
        chain_gate = Gather(ups[:, :, :hidden], flat_one, count)
        chain_lin = Gather(ups[:, :, hidden:], flat_two, count)
        for _ in range(flat - 1):
            chain_gate.step(*after_chips)
            chain_lin.step(*after_chips)
            after_chips = ()
        for _ in range(zs - 1):
            chain_down.step(chain_up.got)
        bounds = jnp.cumsum(lengths[:, 0], axis=-1)
        segment = jnp.sum((bounds[:, :, None] <= place).astype(I32), axis=1)
        slopes = jnp.exp2(-8.0 * (jnp.arange(HEADS, dtype=F32) + 1.0) / HEADS)

        weights = settle(
            mine,
            (chain_qk.held, chain_qk.got, one + [core]),
            (chain_vo.held, chain_vo.got, two + [core]),
        ).reshape(D, 4 * D)
        qk, v = project(x, weights, qv_b)
        qk = tie(qk, chain_gate.got, chain_lin.got)
        chain_gate.step()
        chain_lin.step()
        merged, probs = attend(qk, v, segment[:, None, :], segment[:, :, None], slopes, batches, slot)
        chain_down.got = tie(chain_down.got, merged)
        chain_down.step()
        r1, h = first_norm(x, merged, weights, out_b, gain1, shift1)

        h_other = swap(h, core, count)
        second = lax.all_to_all(tie(by_device(out_up), h), AXES, split_axis=0, concat_axis=0, tiled=True)
        w_gate = settle(mine, (chain_gate.held, chain_gate.got, [core] + one)).reshape(D, hidden)
        w_lin = settle(mine, (chain_lin.held, chain_lin.got, [core] + two)).reshape(D, hidden)
        even_b, odd_b = halves_of(up_b, unit_block)
        a, slope_low, act_low = units(mine, h, h_other, w_gate, w_lin, even_b, odd_b, core)
        down_got = tie(chain_down.got, a)
        w_dn = settle(
            my_chip, (chain_down.held, down_got, [chip_position(b) for b in down_order])
        ).reshape(hidden, D)
        down, down_send = down_product(a, w_dn)
        down_other = swap(down_send, core, count)
        e = jnp.einsum("bkp,bkd->bpd", put, by_batch(second), preferred_element_type=F32).reshape(rows, D)
        result, dr2, df, sums2 = second_norm(h, down, down_other, e, down_b, gain2, shift2)

        def back(rows_here, *after):
            sent = jnp.einsum(
                "bkp,bpd->bkd", put, rows_here.reshape(batches, slot, D), preferred_element_type=F32
            ).astype(BF)
            return lax.all_to_all(tie(by_device(sent), *after), AXES, split_axis=0, concat_axis=0, tiled=True)

        def given(got):
            return jnp.einsum("bri,brd->bid", chosen, by_batch(got), preferred_element_type=F32).astype(BF)

        df_other = swap(df, core, count)
        g_down = down_weight_grad(a, df, df_other).reshape(count // 2, FF // count, D)
        scatter_down = Scatter(mine, pieces_of([g_down]), None, chips, None, deep[::-1][:1] + flat_two[::-1] + deep[::-1][1:], count)
        scatter_down.step()
        du1, du2, g_half_b = units_back(tie(df, scatter_down.sent), df_other, w_dn, slope_low, act_low)
        blocks = (count, D // count, -1)
        g_gate = up_weight_grad(h, h_other, du1).reshape(blocks)
        scatter_gate = Scatter(mine, pieces_of([g_gate]), None, every, None, flat_one[::-1], count)
        scatter_gate.step()
        du2 = tie(du2, scatter_gate.sent)
        g_lin = up_weight_grad(h, h_other, du2).reshape(blocks)
        scatter_lin = Scatter(mine, pieces_of([g_lin]), None, every, None, flat_two[::-1], count)
        scatter_lin.step()
        du1 = tie(du1, scatter_lin.sent)
        dh_own, dh_send = hidden_back(du1, du2, w_gate, w_lin)
        scatter_down.step(dh_own)
        dh_other = swap(tie(dh_send, scatter_down.sent), core, count)
        scatter_gate.step(scatter_down.sent)
        scatter_lin.step(scatter_gate.sent)
        dr1, dbr, do, sums1 = first_norm_back(
            tie(dh_own, scatter_lin.sent), dh_other, dr2, r1, gain1, weights
        )
        back_out = back(result, do)
        dqk, dv = attend_back(qk, v, probs, do, batches, slot)
        g_qk, g_v, g_out, qv_sums = attention_weight_grads(x, dqk, dv, merged, dbr)
        g_qk, g_v, g_out = g_qk.reshape(blocks), g_v.reshape(blocks), g_out.reshape(blocks)

        scatter_up = scatter_gate.beside(scatter_lin, deep[::-1] + [core])
        scatter_up.step(g_out)
        scatter_attn = Scatter(mine, pieces_of([g_qk, g_v, g_out]), None, every, None, [core], count)
        scatter_attn.step(scatter_up.sent, back_out)
        dx = input_back(tie(dr1, scatter_attn.sent), dqk, dv, weights)
        last = dx

        def go(chain):
            nonlocal last
            chain.step(last)
            last = chain.sent

        scatter_qk = scatter_attn.part(0, 2 * D, flat_one[::-1])
        scatter_vo = scatter_attn.part(2 * D, 4 * D, flat_two[::-1])
        back_dx = back(dx)
        small_after = None
        for _ in range(flat):
            go(scatter_qk)
            go(scatter_vo)
            if small_after is None:
                small_after = last
        small_send = owner_sums(
            tie(mine, small_after), qv_sums, sums1, sums2, g_half_b, sizes, count, unit_block, core
        )
        small_got = lax.all_to_all(small_send, AXES, split_axis=0, concat_axis=0, tiled=True)
        small_sum = jnp.sum(small_got, axis=(0, 1))

        while scatter_up.at < len(deep):
            go(scatter_up)
        scatter_attn = scatter_qk.beside(scatter_vo, deep[::-1])
        scatter_attn.step(last, back_dx, small_got)
        last = scatter_attn.sent
        while scatter_down.at < len(one) - 1:
            go(scatter_down)
        up_last = scatter_up.ready(last)[0]
        up_kept = scatter_up.kept[0][0][0]
        up_came = swap(up_last, core, count)
        last = up_last
        while scatter_down.at < len(one):
            go(scatter_down)
        while scatter_attn.at < len(deep):
            scatter_attn.step(last)
            last = scatter_attn.sent
        out_tokens = given(back_out)
        grad_tokens = given(back_dx)
        s_up = join_halves(
            jnp.where(my_core == 0, up_kept, up_came), jnp.where(my_core == 0, up_came, up_kept), unit_block
        )
        s_attn = scatter_attn.total()
        outs, at = [], 0
        for size in sizes:
            outs.append(small_sum[at : at + size])
            at += size
        return (
            out_tokens,
            grad_tokens,
            s_attn[:, : 3 * D],
            outs[0],
            s_attn[:, 3 * D : 4 * D],
            outs[1],
            outs[2],
            outs[3],
            s_up,
            outs[4],
            scatter_down.total(),
            outs[5],
            outs[6],
            outs[7],
        )

    return on_device


def solution(mesh):
    rows = P(None, AXES, None)
    matrix, vector = P(AXES, None), P(AXES)
    return jax.shard_map(
        build(mesh),
        mesh=mesh,
        in_specs=(rows, rows, P(None, AXES), rows)
        + (matrix, vector, matrix, vector, vector, vector, matrix, vector, matrix, vector, vector, vector),
        out_specs=(rows, rows)
        + (matrix, vector, matrix, vector, vector, vector, matrix, vector, matrix, vector, vector, vector),
        check_vma=False,
    )
```

```python
import jax
import jax.numpy as jnp
from jax import lax
from jax.experimental import pallas as pl
from jax.experimental.pallas import tpu as pltpu
from jax.sharding import PartitionSpec as P

D = 768
HEADS = 12
HEAD_DIM = 64
FF = 3072

EPS = 1e-05
NEGATIVE = -1e30
AXES = ("dp", "fsdp")
BF = jnp.bfloat16
F32 = jnp.float32
I32 = jnp.int32


def bit_roles(mesh):
    devices = mesh.devices.reshape(-1)
    count = devices.size.bit_length() - 1
    roles = []
    for bit in range(count):
        here, there = devices[0], devices[1 << bit]
        a, b = getattr(here, "coords", None), getattr(there, "coords", None)
        if a is None or b is None:
            roles.append("cyxzzzzzzz"[bit])
        elif tuple(a) == tuple(b):
            roles.append("c")
        else:
            roles.append("xyz"[[i for i in range(3) if a[i] != b[i]][0]])
    return roles


def swap(value, bit, count):
    return lax.ppermute(value, AXES, [(i, i ^ (1 << bit)) for i in range(count)])


def tie(value, *others):
    if not others:
        return value
    return lax.optimization_barrier((value,) + tuple(others))[0]


CHEAP = pl.CostEstimate(flops=1000, bytes_accessed=1000, transcendentals=0)


SCALAR = pl.BlockSpec(memory_space=pltpu.SMEM)
WHOLE = pl.BlockSpec(memory_space=pltpu.VMEM)


def grant(*arrays):
    total = sum(a.size * a.dtype.itemsize for a in arrays)
    return pltpu.CompilerParams(vmem_limit_bytes=min(2 * total + (4 << 20), 60 << 20))


def spread(t, positions):
    out = 0
    for k, position in enumerate(positions):
        out = out | (((t >> k) & 1) << position)
    return out


def settle(mine, *parts):
    half, rows, _ = parts[0][0].shape
    spans, columns = [], 0
    for first, _, _ in parts:
        spans.append(slice(columns, columns + first.shape[2]))
        columns += first.shape[2]

    def body(mine_ref, *refs):
        me, o_ref = mine_ref[0], refs[-1]

        def move(t, carry):
            for k, (here, (_, _, order)) in enumerate(zip(spans, parts)):
                o_ref[me ^ spread(t, order), :, here] = refs[2 * k][t]
                o_ref[me ^ spread(t + half, order), :, here] = refs[2 * k + 1][t]
            return carry

        lax.fori_loop(0, half, move, 0)

    arrays = [a for part in parts for a in part[:2]]
    out = jax.ShapeDtypeStruct((2 * half, rows, columns), BF)
    return pl.pallas_call(
        body,
        out_shape=out,
        in_specs=[SCALAR] + [WHOLE] * len(arrays),
        out_specs=WHOLE,
        cost_estimate=CHEAP,
        compiler_params=grant(*arrays, out),
        name="settle",
    )(mine, *arrays)


def insert_bit(index, position, value):
    low = index & ((1 << position) - 1)
    return ((index >> position) << (position + 1)) | (value << position) | low


def pieces_of(arrays):
    return [(a, 0, a.shape[2]) for a in arrays]


def cut(pieces, low, high):
    out, at = [], 0
    for array, start, width in pieces:
        lo, hi = max(low, at), min(high, at + width)
        if lo < hi:
            out.append((array, start + lo - at, hi - lo))
        at += width
    return out


def segments(*lists):
    edges = {0}
    for pieces in lists:
        at = 0
        for _, _, width in pieces:
            at += width
            edges.add(at)
    edges = sorted(edges)
    out = []
    for low, high in zip(edges, edges[1:]):
        found = []
        for pieces in lists:
            at = 0
            for k, (_, start, width) in enumerate(pieces):
                if at <= low < at + width:
                    found.append((k, start + low - at))
                at += width
        out.append((low, high, found))
    return out


def pick(mine, pieces, position, bit):
    blocks, rows, _ = pieces[0][0].shape
    spans = segments(pieces)
    columns = spans[-1][1]

    def body(mine_ref, *refs):
        o_ref = refs[-1]
        other = 1 - ((mine_ref[0] >> bit) & 1)

        def move(t, carry):
            index = insert_bit(t, position, other)
            for low, high, ((k, at),) in spans:
                o_ref[t, :, low:high] = refs[k][index, :, at : at + high - low]
            return carry

        lax.fori_loop(0, blocks // 2, move, 0)

    sources = [p[0] for p in pieces]
    out = jax.ShapeDtypeStruct((blocks // 2, rows, columns), BF)
    return pl.pallas_call(
        body,
        out_shape=out,
        in_specs=[SCALAR] + [WHOLE] * len(sources),
        out_specs=WHOLE,
        cost_estimate=CHEAP,
        compiler_params=grant(*sources, out),
        name="pick",
    )(mine, *sources)


def fold(mine, kept, got, now, position, bit):
    blocks, rows, _ = got[0][0].shape
    spans = segments(kept, got)
    columns = spans[-1][1]

    def body(mine_ref, *refs):
        k_refs, r_refs, s_ref, n_ref = refs[: len(kept)], refs[len(kept) : -2], refs[-2], refs[-1]
        side = (mine_ref[0] >> bit) & 1

        def put_total(out_ref, t, index):
            source = index
            if now is not None:
                source = insert_bit(index, now[0], (mine_ref[0] >> now[1]) & 1)
            for low, high, ((k, at), (r, start)) in spans:
                wide = high - low
                total = k_refs[k][source, :, at : at + wide].astype(F32)
                total += r_refs[r][index, :, start : start + wide].astype(F32)
                out_ref[t, :, low:high] = total.astype(BF)

        def move(t, carry):
            put_total(s_ref, t, insert_bit(t, position, 1 - side))
            put_total(n_ref, t, insert_bit(t, position, side))
            return carry

        lax.fori_loop(0, blocks // 2, move, 0)

    sources = [p[0] for p in kept + got]
    out = jax.ShapeDtypeStruct((blocks // 2, rows, columns), BF)
    return pl.pallas_call(
        body,
        out_shape=(out, out),
        in_specs=[SCALAR] + [WHOLE] * len(sources),
        out_specs=[WHOLE] * 2,
        cost_estimate=CHEAP,
        compiler_params=grant(*sources, out, out),
        name="fold",
    )(mine, *sources)


class Gather:
    def __init__(self, block, order, count):
        self.held, self.order, self.count, self.at = block, order, count, 0
        self.got = None

    def all(self, *after):
        if self.got is None:
            return tie(self.held, *after)
        return tie(jnp.concatenate([self.held, self.got], axis=0), *after)

    def step(self, *after):
        self.held = self.all(*after)
        self.got = swap(self.held, self.order[self.at], self.count)
        self.at += 1
        return self.got


class Scatter:
    def __init__(self, mine, kept, got, left, now, order, count):
        self.mine, self.kept, self.got, self.left = mine, kept, got, list(left)
        self.now, self.order, self.count, self.at, self.sent = now, order, count, 0, None

    def part(self, low, high, order):
        return Scatter(
            self.mine, cut(self.kept, low, high), cut(self.got, low, high), self.left, self.now, order, self.count
        )

    def beside(self, other, order):
        return Scatter(
            self.mine, self.kept + other.kept, self.got + other.got, self.left, None, order, self.count
        )

    def ready(self, *after):
        bit = self.order[self.at]
        position = self.left.index(bit)
        if self.got is None:
            kept = [(tie(a, *after), at, width) for a, at, width in self.kept[:1]] + self.kept[1:]
            self.kept = kept
            self.sent = pick(self.mine, kept, position, bit)
            self.now = (position, bit)
        else:
            got = [(tie(a, *after), at, width) for a, at, width in self.got[:1]] + self.got[1:]
            self.sent, rest = fold(self.mine, self.kept, got, self.now, position, bit)
            self.kept, self.now = pieces_of([rest]), None
        return self.sent

    def step(self, *after):
        self.ready(*after)
        bit = self.order[self.at]
        self.got = pieces_of([swap(self.sent, bit, self.count)])
        self.left.remove(bit)
        self.at += 1
        return self.got

    def total(self):
        return self.kept[0][0][0].astype(F32) + self.got[0][0][0].astype(F32)


def halves_of(shard, block):
    pieces = shard.shape[1] // (2 * block)

    def body(w_ref, even_ref, odd_ref):
        values = w_ref[...].astype(F32)
        for out, start in ((even_ref, 0), (odd_ref, block)):
            parts = [values[:, i * 2 * block + start : i * 2 * block + start + block] for i in range(pieces)]
            out[...] = jnp.concatenate(parts, axis=1).astype(out.dtype)

    out = jax.ShapeDtypeStruct((shard.shape[0], shard.shape[1] // 2), shard.dtype)
    return pl.pallas_call(
        body, out_shape=(out, out), cost_estimate=CHEAP, compiler_params=grant(shard, out, out), name="halves"
    )(shard)


def join_halves(even, odd, block):
    pieces = even.shape[1] // block

    def body(even_ref, odd_ref, o_ref):
        a, b = even_ref[...].astype(F32), odd_ref[...].astype(F32)
        parts = []
        for i in range(pieces):
            parts += [a[:, i * block : (i + 1) * block], b[:, i * block : (i + 1) * block]]
        o_ref[...] = jnp.concatenate(parts, axis=1)

    out = jax.ShapeDtypeStruct((even.shape[0], 2 * even.shape[1]), F32)
    return pl.pallas_call(
        body, out_shape=out, cost_estimate=CHEAP, compiler_params=grant(even, odd, out, out), name="join"
    )(even, odd)


def attend(qk, v, segment_row, segment_column, slopes, batches, slot):
    pairs = HEADS // 2
    width = 2 * HEAD_DIM

    def body(slope_ref, qk_ref, v_ref, row_ref, column_ref, o_ref, p_ref):
        pair = pl.program_id(1)
        at = pl.multiple_of(pair * width, width)
        query = qk_ref[:, pl.ds(at, width)]
        keyed = qk_ref[:, pl.ds(D + at, width)]
        value = v_ref[:, pl.ds(at, width)]
        lane = lax.broadcasted_iota(I32, (slot, width), 1)
        gap = jnp.abs(
            lax.broadcasted_iota(I32, (slot, slot), 0) - lax.broadcasted_iota(I32, (slot, slot), 1)
        ).astype(F32)
        same = column_ref[0] == row_ref[0]
        mixed = []
        for which in range(2):
            own = (lane >= HEAD_DIM) if which else (lane < HEAD_DIM)
            only = jnp.where(own, query, jnp.zeros_like(query))
            scores = lax.dot_general(only, keyed, (((1,), (1,)), ((), ())), preferred_element_type=F32)
            scores = jnp.where(same, scores * 0.125 - slope_ref[2 * pair + which] * gap, NEGATIVE)
            raised = jnp.exp(scores - jnp.max(scores, axis=1, keepdims=True))
            probs = (raised / jnp.sum(raised, axis=1, keepdims=True)).astype(BF)
            p_ref[0, 0, which] = probs
            mixed.append(jnp.dot(probs, value, preferred_element_type=F32))
        o_ref[:, pl.ds(at, width)] = jnp.where(lane < HEAD_DIM, mixed[0], mixed[1]).astype(BF)

    rows = batches * slot
    merged = jax.ShapeDtypeStruct((rows, D), BF)
    probs = jax.ShapeDtypeStruct((batches, pairs, 2, slot, slot), BF)
    return pl.pallas_call(
        body,
        out_shape=(merged, probs),
        grid=(batches, pairs),
        in_specs=[
            pl.BlockSpec(memory_space=pltpu.SMEM),
            pl.BlockSpec((slot, 2 * D), lambda b, h: (b, 0)),
            pl.BlockSpec((slot, D), lambda b, h: (b, 0)),
            pl.BlockSpec((1, 1, slot), lambda b, h: (b, 0, 0)),
            pl.BlockSpec((1, slot, 1), lambda b, h: (b, 0, 0)),
        ],
        out_specs=[
            pl.BlockSpec((slot, D), lambda b, h: (b, 0)),
            pl.BlockSpec((1, 1, 2, slot, slot), lambda b, h: (b, h, 0, 0, 0)),
        ],
        cost_estimate=CHEAP,
        compiler_params=pltpu.CompilerParams(vmem_limit_bytes=24 * 1024 * 1024),
        name="attend",
    )(slopes, qk, v, segment_row, segment_column)


def attend_back(qk, v, probs, do, batches, slot):
    pairs = HEADS // 2
    width = 2 * HEAD_DIM
    first = (((0,), (0,)), ((), ()))
    second = (((1,), (1,)), ((), ()))

    def body(qk_ref, v_ref, p_ref, do_ref, dqk_ref, dv_ref):
        at = pl.multiple_of(pl.program_id(1) * width, width)
        query = qk_ref[:, pl.ds(at, width)]
        keyed = qk_ref[:, pl.ds(D + at, width)]
        value = v_ref[:, pl.ds(at, width)]
        upstream = do_ref[:, pl.ds(at, width)]
        lane = lax.broadcasted_iota(I32, (slot, width), 1)
        dq, dk, dv = [], [], []
        for which in range(2):
            own = (lane >= HEAD_DIM) if which else (lane < HEAD_DIM)
            low = p_ref[0, 0, which]
            high = low.astype(F32)
            only = jnp.where(own, upstream, jnp.zeros_like(upstream))
            dp = lax.dot_general(only, value, second, preferred_element_type=F32)
            delta = jnp.sum(high * dp, axis=1, keepdims=True)
            ds = (high * (dp - delta)).astype(BF)
            dq.append(jnp.dot(ds, keyed, preferred_element_type=F32))
            dk.append(lax.dot_general(ds, query, first, preferred_element_type=F32))
            dv.append(lax.dot_general(low, upstream, first, preferred_element_type=F32))
        early = lane < HEAD_DIM
        dqk_ref[:, pl.ds(at, width)] = (jnp.where(early, dq[0], dq[1]) * 0.125).astype(BF)
        dqk_ref[:, pl.ds(D + at, width)] = (jnp.where(early, dk[0], dk[1]) * 0.125).astype(BF)
        dv_ref[:, pl.ds(at, width)] = jnp.where(early, dv[0], dv[1]).astype(BF)

    rows = batches * slot
    return pl.pallas_call(
        body,
        out_shape=(jax.ShapeDtypeStruct((rows, 2 * D), BF), jax.ShapeDtypeStruct((rows, D), BF)),
        grid=(batches, pairs),
        in_specs=[
            pl.BlockSpec((slot, 2 * D), lambda b, h: (b, 0)),
            pl.BlockSpec((slot, D), lambda b, h: (b, 0)),
            pl.BlockSpec((1, 1, 2, slot, slot), lambda b, h: (b, h, 0, 0, 0)),
            pl.BlockSpec((slot, D), lambda b, h: (b, 0)),
        ],
        out_specs=[
            pl.BlockSpec((slot, 2 * D), lambda b, h: (b, 0)),
            pl.BlockSpec((slot, D), lambda b, h: (b, 0)),
        ],
        cost_estimate=CHEAP,
        compiler_params=pltpu.CompilerParams(vmem_limit_bytes=24 * 1024 * 1024),
        name="attend_back",
    )(qk, v, probs, do)


TILE = 256
ROWS = (((0,), (0,)), ((), ()))
BACK = (((1,), (1,)), ((), ()))


def in_vmem(body, outs, *arrays, name):
    total = sum(a.size * a.dtype.itemsize for a in arrays + tuple(outs))
    return pl.pallas_call(
        body,
        out_shape=tuple(outs),
        in_specs=[WHOLE] * len(arrays),
        out_specs=tuple([WHOLE] * len(outs)),
        cost_estimate=CHEAP,
        compiler_params=pltpu.CompilerParams(vmem_limit_bytes=min(total + (16 << 20), 62 << 20)),
        name=name,
    )(*arrays)


def product(left, right, dims):
    return lax.dot_general(left, right, dims, preferred_element_type=F32)


def tiles(count, step):
    def run(i, carry):
        step(pl.multiple_of(i * TILE, TILE))
        return carry

    lax.fori_loop(0, count // TILE, run, 0)


def receive(arrived, sizes, count, batches, slot, held):
    per = slot // count
    spans = -(-sum(sizes) // held)

    def body(in_ref, x_ref, put_ref, *refs):
        outs, side_ref = refs[:-1], refs[-1]
        for b in range(batches):
            slots = in_ref[b, :, D:].astype(F32)[:, 127:128]
            put = (slots == lax.broadcasted_iota(I32, (slot, slot), 1).astype(F32)).astype(F32).astype(BF)
            put_ref[b] = put
            x_ref[b * slot : (b + 1) * slot, :] = product(put, in_ref[b, :, :D], ROWS).astype(BF)
        side_ref[...] = in_ref[0, :, D:].astype(F32)
        flat = jnp.concatenate(
            [side_ref[pl.ds(r, count, stride=per), :][:, :held] for r in range(spans)], axis=1
        )
        at = 0
        for out, size in zip(outs, sizes):
            for j in range(count):
                out[:, j * size : (j + 1) * size] = flat[j : j + 1, at : at + size]
            at += size

    outs = [
        jax.ShapeDtypeStruct((batches * slot, D), BF),
        jax.ShapeDtypeStruct((batches, slot, slot), BF),
    ] + [jax.ShapeDtypeStruct((1, count * size), F32) for size in sizes]
    return pl.pallas_call(
        body,
        out_shape=tuple(outs),
        in_specs=[WHOLE],
        out_specs=tuple([WHOLE] * len(outs)),
        scratch_shapes=[pltpu.VMEM((slot, 128), F32)],
        cost_estimate=CHEAP,
        compiler_params=pltpu.CompilerParams(vmem_limit_bytes=20 << 20),
        name="receive",
    )(arrived)


def project(x, weights, bias):
    def body(x_ref, w_ref, b_ref, qk_ref, v_ref):
        def step(at):
            here = pl.ds(at, TILE)
            tile = x_ref[here, :]
            q = jnp.dot(tile, w_ref[:, :D], preferred_element_type=F32) + b_ref[:, :D]
            qk_ref[here, :D] = q.astype(BF)
            qk_ref[here, D:] = jnp.dot(tile, w_ref[:, D : 2 * D], preferred_element_type=F32).astype(BF)
            v = jnp.dot(tile, w_ref[:, 2 * D : 3 * D], preferred_element_type=F32) + b_ref[:, D:]
            v_ref[here, :] = v.astype(BF)

        tiles(x.shape[0], step)

    outs = [jax.ShapeDtypeStruct((x.shape[0], 2 * D), BF), jax.ShapeDtypeStruct((x.shape[0], D), BF)]
    return in_vmem(body, outs, x, weights, bias, name="project")


def first_norm(x, merged, weights, bias, gain, shift):
    def body(x_ref, m_ref, w_ref, b_ref, g_ref, s_ref, r_ref, h_ref):
        def step(at):
            here = pl.ds(at, TILE)
            total = x_ref[here, :].astype(F32) + b_ref[...]
            total += jnp.dot(m_ref[here, :], w_ref[:, 3 * D :], preferred_element_type=F32)
            r_ref[here, :] = total
            h_ref[here, :] = (norm_stats(total)[0] * g_ref[...] + s_ref[...]).astype(BF)

        tiles(x.shape[0], step)

    outs = [jax.ShapeDtypeStruct(x.shape, F32), jax.ShapeDtypeStruct(x.shape, BF)]
    return in_vmem(body, outs, x, merged, weights, bias, gain, shift, name="first_norm")


def near(width):
    return pl.BlockSpec((TILE, width), lambda i: (jnp.minimum(i, 1), 0))


def far(width):
    return pl.BlockSpec((TILE, width), lambda i: (jnp.maximum(i - 2, 0), 0))


def tile_of(width):
    return pl.BlockSpec((TILE, width), lambda i: (i, 0))


def fixed(*shape):
    return pl.BlockSpec(shape, lambda i: (0, 0))


TILED_GRANT = pltpu.CompilerParams(vmem_limit_bytes=32 << 20)


def units(mine, h, h_other, w_gate, w_lin, even, odd, core):
    rows, hidden = h.shape[0], w_gate.shape[1]
    assert rows == 2 * TILE

    def body(mine_ref, h_ref, o_ref, g_ref, l_ref, e_ref, d_ref, a_ref, slope_ref, act_ref):
        first = ((mine_ref[0] >> core) & 1) == 0
        tile = jnp.where(pl.program_id(0) < 2, h_ref[...], o_ref[...])
        for lo in range(0, hidden, TILE):
            wide = slice(lo, lo + TILE)
            late = slice(hidden + lo, hidden + lo + TILE)
            gate = jnp.dot(tile, g_ref[:, wide], preferred_element_type=F32)
            gate += jnp.where(first, e_ref[:, wide], d_ref[:, wide])
            lin = jnp.dot(tile, l_ref[:, wide], preferred_element_type=F32)
            lin += jnp.where(first, e_ref[:, late], d_ref[:, late])
            cdf = 0.5 * (1.0 + lax.erf(gate * (0.5**0.5)))
            act = gate * cdf
            slope = cdf + gate * jnp.exp(-0.5 * gate * gate) * (1.0 / (2.0 * jnp.pi) ** 0.5)
            a_ref[:, wide] = (act * lin).astype(BF)
            slope_ref[:, wide] = (slope * lin).astype(BF)
            act_ref[:, wide] = act.astype(BF)

    out = jax.ShapeDtypeStruct((2 * rows, hidden), BF)
    return pl.pallas_call(
        body,
        out_shape=(out, out, out),
        grid=(4,),
        in_specs=[SCALAR, near(D), far(D)] + [fixed(D, hidden)] * 2 + [fixed(1, 2 * hidden)] * 2,
        out_specs=(tile_of(hidden),) * 3,
        cost_estimate=CHEAP,
        compiler_params=TILED_GRANT,
        name="units",
    )(mine, h, h_other, w_gate, w_lin, even, odd)


def down_weight_grad(a, df, df_other):
    rows = df.shape[0]

    def body(a_ref, d_ref, o_ref, g_ref):
        def step(at):
            g = product(a_ref[:rows, pl.ds(at, TILE)], d_ref[...], ROWS)
            g += product(a_ref[rows:, pl.ds(at, TILE)], o_ref[...], ROWS)
            g_ref[pl.ds(at, TILE), :] = g.astype(BF)

        tiles(a.shape[1], step)

    out = jax.ShapeDtypeStruct((a.shape[1], df.shape[1]), BF)
    return in_vmem(body, [out], a, df, df_other, name="down_grad")[0]


def units_back(df, df_other, w_dn, slope, act):
    rows, hidden = df.shape[0], w_dn.shape[0]

    def body(d_ref, o_ref, w_ref, s_ref, a_ref, du1_ref, du2_ref, sum_ref):
        i = pl.program_id(0)
        tile = jnp.where(i < 2, d_ref[...], o_ref[...])
        da = product(tile, w_ref[...], BACK).astype(BF).astype(F32)
        du1 = (da * s_ref[...].astype(F32)).astype(BF)
        du2 = (da * a_ref[...].astype(F32)).astype(BF)
        du1_ref[...] = du1
        du2_ref[...] = du2

        @pl.when(i == 0)
        def _():
            sum_ref[...] = jnp.zeros_like(sum_ref)

        sum_ref[0:1, :] += jnp.sum(du1.astype(F32), axis=0, keepdims=True)
        sum_ref[1:2, :] += jnp.sum(du2.astype(F32), axis=0, keepdims=True)

    du = jax.ShapeDtypeStruct((2 * rows, hidden), BF)
    sums = jax.ShapeDtypeStruct((2, hidden), F32)
    return pl.pallas_call(
        body,
        out_shape=(du, du, sums),
        grid=(4,),
        in_specs=[near(D), far(D), fixed(hidden, D), tile_of(hidden), tile_of(hidden)],
        out_specs=(tile_of(hidden), tile_of(hidden), fixed(2, hidden)),
        cost_estimate=CHEAP,
        compiler_params=TILED_GRANT,
        name="units_back",
    )(df, df_other, w_dn, slope, act)


def up_weight_grad(h, h_other, du):
    rows = h.shape[0]

    def body(h_ref, o_ref, d_ref, g_ref):
        def step(at):
            g = product(h_ref[:, pl.ds(at, TILE)], d_ref[:rows, :], ROWS)
            g += product(o_ref[:, pl.ds(at, TILE)], d_ref[rows:, :], ROWS)
            g_ref[pl.ds(at, TILE), :] = g.astype(BF)

        tiles(h.shape[1], step)

    out = jax.ShapeDtypeStruct((h.shape[1], du.shape[1]), BF)
    return in_vmem(body, [out], h, h_other, du, name="up_grad")[0]


def hidden_back(du1, du2, w_gate, w_lin):
    rows, hidden = du1.shape[0] // 2, du1.shape[1]

    def body(d1_ref, d2_ref, g_ref, l_ref, own_ref, other_ref):
        dh = product(d1_ref[...], g_ref[...], BACK) + product(d2_ref[...], l_ref[...], BACK)

        @pl.when(pl.program_id(0) < 2)
        def _():
            own_ref[...] = dh

        @pl.when(pl.program_id(0) >= 2)
        def _():
            other_ref[...] = dh.astype(BF)

    own = jax.ShapeDtypeStruct((rows, D), F32)
    other = jax.ShapeDtypeStruct((rows, D), BF)
    return pl.pallas_call(
        body,
        out_shape=(own, other),
        grid=(4,),
        in_specs=[tile_of(hidden)] * 2 + [fixed(D, hidden)] * 2,
        out_specs=(near(D), far(D)),
        cost_estimate=CHEAP,
        compiler_params=TILED_GRANT,
        name="hidden_back",
    )(du1, du2, w_gate, w_lin)


def down_product(a, w_dn):
    rows = a.shape[0] // 2

    def body(a_ref, w_ref, own_ref, other_ref):
        for base, out in ((0, own_ref), (rows, other_ref)):

            def step(at, base=base, out=out):
                out[pl.ds(at, TILE), :] = jnp.dot(
                    a_ref[pl.ds(base + at, TILE), :], w_ref[...], preferred_element_type=F32
                ).astype(out.dtype)

            tiles(rows, step)

    own = jax.ShapeDtypeStruct((rows, D), F32)
    other = jax.ShapeDtypeStruct((rows, D), BF)
    return in_vmem(body, [own, other], a, w_dn, name="down_product")


def second_norm(h, down, down_other, e, down_b, gain, shift):
    rows = h.shape[0]

    def body(h_ref, d_ref, o_ref, e_ref, b_ref, g_ref, s_ref, res_ref, dr_ref, df_ref, sum_ref):
        sum_ref[...] = jnp.zeros_like(sum_ref)
        bias, gains, shifts = b_ref[...], g_ref[...], s_ref[...]

        def step(at):
            here = pl.ds(at, TILE)
            total = h_ref[here, :].astype(F32) + d_ref[here, :] + o_ref[here, :].astype(F32) + bias
            normed, inverse = norm_stats(total)
            res_ref[here, :] = (normed * gains + shifts).astype(BF)
            up = e_ref[here, :]
            dr = norm_back(normed, inverse, gains, up)
            low = dr.astype(BF)
            dr_ref[here, :] = dr
            df_ref[here, :] = low
            sum_ref[0:1, :] += jnp.sum(up * normed, axis=0, keepdims=True)
            sum_ref[1:2, :] += jnp.sum(up, axis=0, keepdims=True)
            sum_ref[2:3, :] += jnp.sum(low.astype(F32), axis=0, keepdims=True)

        tiles(rows, step)

    low, wide = jax.ShapeDtypeStruct((rows, D), BF), jax.ShapeDtypeStruct((rows, D), F32)
    outs = [low, wide, low, jax.ShapeDtypeStruct((3, D), F32)]
    return in_vmem(body, outs, h, down, down_other, e, down_b, gain, shift, name="second_norm")


def first_norm_back(dh_own, dh_other, dr2, r1, gain, w_vo):
    rows = r1.shape[0]

    def body(d_ref, o_ref, r_ref, n_ref, g_ref, w_ref, dr_ref, dbr_ref, do_ref, sum_ref):
        sum_ref[...] = jnp.zeros_like(sum_ref)

        def step(at):
            here = pl.ds(at, TILE)
            dh = d_ref[here, :] + o_ref[here, :].astype(F32) + r_ref[here, :]
            normed, inverse = norm_stats(n_ref[here, :])
            dr = norm_back(normed, inverse, g_ref[...], dh)
            low = dr.astype(BF)
            dr_ref[here, :] = dr
            dbr_ref[here, :] = low
            do_ref[here, :] = product(low, w_ref[:, 3 * D :], BACK).astype(BF)
            sum_ref[0:1, :] += jnp.sum(dh * normed, axis=0, keepdims=True)
            sum_ref[1:2, :] += jnp.sum(dh, axis=0, keepdims=True)
            sum_ref[2:3, :] += jnp.sum(low.astype(F32), axis=0, keepdims=True)

        tiles(rows, step)

    low, wide = jax.ShapeDtypeStruct((rows, D), BF), jax.ShapeDtypeStruct((rows, D), F32)
    outs = [wide, low, low, jax.ShapeDtypeStruct((3, D), F32)]
    return in_vmem(body, outs, dh_own, dh_other, dr2, r1, gain, w_vo, name="first_norm_back")


def attention_weight_grads(x, dqk, dv, merged, dbr):
    def body(x_ref, qk_ref, v_ref, m_ref, d_ref, gqk_ref, gv_ref, go_ref, sum_ref):
        def step(at):
            here = pl.ds(at, TILE)
            gqk_ref[here, :] = product(x_ref[:, here], qk_ref[...], ROWS).astype(BF)
            gv_ref[here, :] = product(x_ref[:, here], v_ref[...], ROWS).astype(BF)
            go_ref[here, :] = product(m_ref[:, here], d_ref[...], ROWS).astype(BF)

        tiles(D, step)
        sum_ref[0:1, :] = jnp.sum(qk_ref[:, :D].astype(F32), axis=0, keepdims=True)
        sum_ref[1:2, :] = jnp.sum(v_ref[...].astype(F32), axis=0, keepdims=True)

    outs = [jax.ShapeDtypeStruct((D, n * D), BF) for n in (2, 1, 1)] + [jax.ShapeDtypeStruct((2, D), F32)]
    return in_vmem(body, outs, x, dqk, dv, merged, dbr, name="attention_grads")


def input_back(dr1, dqk, dv, weights):
    def body(r_ref, qk_ref, v_ref, w_ref, out_ref):
        def step(at):
            here = pl.ds(at, TILE)
            dx = r_ref[here, :] + product(qk_ref[here, :], w_ref[:, : 2 * D], BACK)
            out_ref[here, :] = (dx + product(v_ref[here, :], w_ref[:, 2 * D : 3 * D], BACK)).astype(BF)

        tiles(dr1.shape[0], step)

    return in_vmem(body, [jax.ShapeDtypeStruct(dr1.shape, BF)], dr1, dqk, dv, weights, name="input_back")[0]


def owner_sums(mine, qv, first, second, half, sizes, count, block, core):
    rows_each = D // count
    assert sum(sizes) <= 128 * rows_each

    def body(mine_ref, q_ref, f_ref, s_ref, u_ref, o_ref, wide_ref):
        mine_side = (mine_ref[0] >> core) & 1
        pieces = []
        for g in range(2):
            for i in range(u_ref.shape[1] // block):
                part = u_ref[g : g + 1, i * block : (i + 1) * block]
                for side in range(2):
                    pieces.append(jnp.where(mine_side == side, part, 0.0))
        up = jnp.concatenate(pieces, axis=1)
        rows = [None] + [r[i : i + 1, :] for r, i in ((f_ref, 2), (f_ref, 0), (f_ref, 1))]
        rows += [up] + [r[i : i + 1, :] for r, i in ((s_ref, 2), (s_ref, 0), (s_ref, 1))]
        wide_ref[...] = jnp.zeros_like(wide_ref)
        for j in range(count):
            at = 0
            for k, size in enumerate(sizes):
                if k == 0:
                    row, lo = divmod(j * size, D)
                    piece = q_ref[row : row + 1, lo : lo + size]
                else:
                    piece = rows[k][:, j * size : (j + 1) * size]
                done = 0
                while done < size:
                    line, lane = divmod(at, 128)
                    take = min(size - done, 128 - lane)
                    wide_ref[j, line : line + 1, lane : lane + take] = piece[:, done : done + take]
                    done, at = done + take, at + take
        o_ref[...] = wide_ref[...].astype(BF)

    out = jax.ShapeDtypeStruct((count, rows_each, 128), BF)
    return pl.pallas_call(
        body,
        out_shape=out,
        in_specs=[SCALAR] + [WHOLE] * 4,
        out_specs=WHOLE,
        scratch_shapes=[pltpu.VMEM((count, rows_each, 128), F32)],
        cost_estimate=CHEAP,
        compiler_params=pltpu.CompilerParams(vmem_limit_bytes=8 << 20),
        name="owner_sums",
    )(mine, qv, first, second, half)


def norm_stats(values):
    centre = jnp.mean(values, axis=-1, keepdims=True)
    centred = values - centre
    spread_of = jnp.mean(centred * centred, axis=-1, keepdims=True)
    inverse = lax.rsqrt(spread_of + EPS)
    return centred * inverse, inverse


def norm_back(normed, inverse, gain, upstream):
    scaled = upstream * gain
    first = jnp.mean(scaled, axis=-1, keepdims=True)
    second = jnp.mean(scaled * normed, axis=-1, keepdims=True)
    return (scaled - first - normed * second) * inverse


def dot(left, right):
    return jnp.dot(left, right, preferred_element_type=F32)


def dot_rows(left, right):
    return lax.dot_general(left, right, (((0,), (0,)), ((), ())), preferred_element_type=F32)


def dot_back(left, right):
    return lax.dot_general(left, right, (((1,), (1,)), ((), ())), preferred_element_type=F32)


def build(mesh):
    count = mesh.devices.size
    roles = bit_roles(mesh)
    every = list(range(len(roles)))

    def of(role):
        return [b for b in reversed(every) if roles[b] == role]

    core = roles.index("c")
    chips = [b for b in every if b != core]
    deep = of("z")
    one = deep + of("x") + of("y")
    two = deep + of("y") + of("x")
    flat_one, flat_two = of("x") + of("y"), of("y") + of("x")

    def chip_position(bit):
        return bit if bit < core else bit - 1

    def on_device(
        tokens,
        cotangent,
        target,
        lengths,
        w_qkv,
        qv_bias,
        w_out,
        out_bias,
        gain_one,
        shift_one,
        w_up,
        up_bias,
        w_down,
        down_bias,
        gain_two,
        shift_two,
    ):
        me = lax.axis_index(AXES).astype(I32)
        my_core = (me >> core) & 1
        mine = me.reshape(1)
        low = me & ((1 << core) - 1)
        my_chip = (((me >> (core + 1)) << core) | low).reshape(1)
        batches, slot, width = tokens.shape
        rows = batches * slot
        per = slot // count
        place = jnp.arange(slot, dtype=I32)
        unit_block = (FF // count) << core
        hidden = FF // 2

        even, odd = halves_of(w_up, unit_block)
        up_send = jnp.where(my_core == 0, odd, even)
        up_hold = jnp.where(my_core == 0, even, odd)
        chain_attn = Gather(jnp.concatenate([w_qkv, w_out], axis=1)[None], deep, count)
        up_got = swap(up_send, core, count)
        chain_up = Gather(jnp.stack([up_hold, up_got]), deep, count)
        down_order = flat_two + deep
        chain_down = Gather(w_down[None], down_order, count)

        smalls = [qv_bias, out_bias, gain_one, shift_one, up_bias, down_bias, gain_two, shift_two]
        sizes = [v.shape[0] for v in smalls]
        packed = jnp.concatenate(smalls)
        total = packed.shape[0]

        rank = jnp.sum((target[:, None, :] < target[:, :, None]).astype(I32), axis=2)
        chosen = (rank[:, None, :] == place[None, :, None]).astype(BF)
        slots = (target % slot).astype(BF)
        out_rows = jnp.einsum("bri,bid->brd", chosen, tokens, preferred_element_type=F32).astype(BF)
        out_up = jnp.einsum("bri,bid->brd", chosen, cotangent, preferred_element_type=F32).astype(BF)
        out_slots = jnp.einsum("bri,bi->br", chosen, slots, preferred_element_type=F32).astype(BF)

        def by_device(v):
            return v.reshape((batches, count, per) + v.shape[2:]).swapaxes(0, 1).reshape(
                (count, batches * per) + v.shape[2:]
            )

        extra_rows = batches * per
        held = 64
        spans = -(-total // held)
        side = jnp.pad(packed, (0, spans * held - total)).reshape(spans, held)
        side = jnp.pad(side, ((0, extra_rows - spans), (0, 127 - held)))
        payload = jnp.concatenate(
            [
                by_device(out_rows),
                jnp.broadcast_to(side[None], (count, extra_rows, 127)),
                by_device(out_slots)[..., None],
            ],
            axis=2,
        )
        first = lax.all_to_all(payload, AXES, split_axis=0, concat_axis=0, tiled=True)
        flat, zs = len(flat_one), len(deep)
        for _ in range(zs):
            chain_attn.step()
        for _ in range(flat):
            chain_down.step()
        attn = chain_attn.all()
        chain_qk = Gather(attn[:, :, : 2 * D], flat_one + [core], count)
        chain_vo = Gather(attn[:, :, 2 * D :], flat_two + [core], count)
        for k in range(flat):
            chain_qk.step()
            chain_vo.step()
            if k == 0:
                chain_up.step(chain_attn.got)
                for _ in range(zs - 1):
                    chain_up.step()

        def by_batch(v):
            return v.reshape((count, batches, per) + v.shape[2:]).swapaxes(0, 1).reshape(
                (batches, slot) + v.shape[2:]
            )

        x, put, *vectors = receive(by_batch(first), sizes, count, batches, slot, held)
        qv_b, out_b, gain1, shift1, up_b, down_b, gain2, shift2 = vectors

        after_chips = (chain_qk.got, chain_vo.got)
        chain_qk.step(x)
        chain_vo.step(x)
        ups = chain_up.all()
        chain_gate = Gather(ups[:, :, :hidden], flat_one, count)
        chain_lin = Gather(ups[:, :, hidden:], flat_two, count)
        for _ in range(flat - 1):
            chain_gate.step(*after_chips)
            chain_lin.step(*after_chips)
            after_chips = ()
        for _ in range(zs - 1):
            chain_down.step(chain_up.got)
        bounds = jnp.cumsum(lengths[:, 0], axis=-1)
        segment = jnp.sum((bounds[:, :, None] <= place).astype(I32), axis=1)
        slopes = jnp.exp2(-8.0 * (jnp.arange(HEADS, dtype=F32) + 1.0) / HEADS)

        weights = settle(
            mine,
            (chain_qk.held, chain_qk.got, one + [core]),
            (chain_vo.held, chain_vo.got, two + [core]),
        ).reshape(D, 4 * D)
        qk, v = project(x, weights, qv_b)
        qk = tie(qk, chain_gate.got, chain_lin.got)
        chain_gate.step()
        chain_lin.step()
        merged, probs = attend(qk, v, segment[:, None, :], segment[:, :, None], slopes, batches, slot)
        chain_down.got = tie(chain_down.got, merged)
        chain_down.step()
        r1, h = first_norm(x, merged, weights, out_b, gain1, shift1)

        h_other = swap(h, core, count)
        second = lax.all_to_all(tie(by_device(out_up), h), AXES, split_axis=0, concat_axis=0, tiled=True)
        w_gate = settle(mine, (chain_gate.held, chain_gate.got, [core] + one)).reshape(D, hidden)
        w_lin = settle(mine, (chain_lin.held, chain_lin.got, [core] + two)).reshape(D, hidden)
        even_b, odd_b = halves_of(up_b, unit_block)
        a, slope_low, act_low = units(mine, h, h_other, w_gate, w_lin, even_b, odd_b, core)
        down_got = tie(chain_down.got, a)
        w_dn = settle(
            my_chip, (chain_down.held, down_got, [chip_position(b) for b in down_order])
        ).reshape(hidden, D)
        down, down_send = down_product(a, w_dn)
        down_other = swap(down_send, core, count)
        e = jnp.einsum("bkp,bkd->bpd", put, by_batch(second), preferred_element_type=F32).reshape(rows, D)
        result, dr2, df, sums2 = second_norm(h, down, down_other, e, down_b, gain2, shift2)

        def back(rows_here, *after):
            sent = jnp.einsum(
                "bkp,bpd->bkd", put, rows_here.reshape(batches, slot, D), preferred_element_type=F32
            ).astype(BF)
            return lax.all_to_all(tie(by_device(sent), *after), AXES, split_axis=0, concat_axis=0, tiled=True)

        def given(got):
            return jnp.einsum("bri,brd->bid", chosen, by_batch(got), preferred_element_type=F32).astype(BF)

        df_other = swap(df, core, count)
        g_down = down_weight_grad(a, df, df_other).reshape(count // 2, FF // count, D)
        scatter_down = Scatter(mine, pieces_of([g_down]), None, chips, None, deep[::-1][:1] + flat_two[::-1] + deep[::-1][1:], count)
        scatter_down.step()
        du1, du2, g_half_b = units_back(tie(df, scatter_down.sent), df_other, w_dn, slope_low, act_low)
        blocks = (count, D // count, -1)
        g_gate = up_weight_grad(h, h_other, du1).reshape(blocks)
        scatter_gate = Scatter(mine, pieces_of([g_gate]), None, every, None, flat_one[::-1], count)
        scatter_gate.step()
        du2 = tie(du2, scatter_gate.sent)
        g_lin = up_weight_grad(h, h_other, du2).reshape(blocks)
        scatter_lin = Scatter(mine, pieces_of([g_lin]), None, every, None, flat_two[::-1], count)
        scatter_lin.step()
        du1 = tie(du1, scatter_lin.sent)
        dh_own, dh_send = hidden_back(du1, du2, w_gate, w_lin)
        scatter_down.step(dh_own)
        dh_other = swap(tie(dh_send, scatter_down.sent), core, count)
        scatter_gate.step(scatter_down.sent)
        scatter_lin.step(scatter_gate.sent)
        dr1, dbr, do, sums1 = first_norm_back(
            tie(dh_own, scatter_lin.sent), dh_other, dr2, r1, gain1, weights
        )
        back_out = back(result, do)
        dqk, dv = attend_back(qk, v, probs, do, batches, slot)
        g_qk, g_v, g_out, qv_sums = attention_weight_grads(x, dqk, dv, merged, dbr)
        g_qk, g_v, g_out = g_qk.reshape(blocks), g_v.reshape(blocks), g_out.reshape(blocks)

        scatter_up = scatter_gate.beside(scatter_lin, deep[::-1] + [core])
        scatter_up.step(g_out)
        g_small = owner_sums(mine, qv_sums, sums1, sums2, g_half_b, sizes, count, unit_block, core)
        scatter_attn = Scatter(mine, pieces_of([g_qk, g_v, g_out, g_small]), None, every, None, [core], count)
        scatter_attn.step(scatter_up.sent, back_out)
        dx = input_back(tie(dr1, scatter_attn.sent), dqk, dv, weights)
        last = dx

        def go(chain):
            nonlocal last
            chain.step(last)
            last = chain.sent

        scatter_qk = scatter_attn.part(0, 2 * D, flat_one[::-1])
        scatter_vo = scatter_attn.part(2 * D, 4 * D + 128, flat_two[::-1])
        back_dx = back(dx)
        for _ in range(flat):
            go(scatter_qk)
            go(scatter_vo)
        while scatter_up.at < len(deep):
            go(scatter_up)
        scatter_attn = scatter_qk.beside(scatter_vo, deep[::-1])
        scatter_attn.step(last, back_dx)
        last = scatter_attn.sent
        while scatter_down.at < len(one) - 1:
            go(scatter_down)
        up_last = scatter_up.ready(last)[0]
        up_kept = scatter_up.kept[0][0][0]
        up_came = swap(up_last, core, count)
        last = up_last
        while scatter_down.at < len(one):
            go(scatter_down)
        while scatter_attn.at < len(deep):
            scatter_attn.step(last)
            last = scatter_attn.sent
        out_tokens = given(back_out)
        grad_tokens = given(back_dx)
        s_up = join_halves(
            jnp.where(my_core == 0, up_kept, up_came), jnp.where(my_core == 0, up_came, up_kept), unit_block
        )
        s_attn = scatter_attn.total()
        small_sum = s_attn[:, 4 * D :].reshape(-1)
        outs, at = [], 0
        for size in sizes:
            outs.append(small_sum[at : at + size])
            at += size
        return (
            out_tokens,
            grad_tokens,
            s_attn[:, : 3 * D],
            outs[0],
            s_attn[:, 3 * D : 4 * D],
            outs[1],
            outs[2],
            outs[3],
            s_up,
            outs[4],
            scatter_down.total(),
            outs[5],
            outs[6],
            outs[7],
        )

    return on_device


def solution(mesh):
    rows = P(None, AXES, None)
    matrix, vector = P(AXES, None), P(AXES)
    return jax.shard_map(
        build(mesh),
        mesh=mesh,
        in_specs=(rows, rows, P(None, AXES), rows)
        + (matrix, vector, matrix, vector, vector, vector, matrix, vector, matrix, vector, vector, vector),
        out_specs=(rows, rows)
        + (matrix, vector, matrix, vector, vector, vector, matrix, vector, matrix, vector, vector, vector),
        check_vma=False,
    )
```

```python
import jax
import jax.numpy as jnp
from jax import lax
from jax.experimental import pallas as pl
from jax.experimental.pallas import tpu as pltpu
from jax.sharding import PartitionSpec as P

D = 768
HEADS = 12
HEAD_DIM = 64
FF = 3072

EPS = 1e-05
NEGATIVE = -1e30
AXES = ("dp", "fsdp")
BF = jnp.bfloat16
F32 = jnp.float32
I32 = jnp.int32


def bit_roles(mesh):
    devices = mesh.devices.reshape(-1)
    count = devices.size.bit_length() - 1
    roles = []
    for bit in range(count):
        here, there = devices[0], devices[1 << bit]
        a, b = getattr(here, "coords", None), getattr(there, "coords", None)
        if a is None or b is None:
            roles.append("cyxzzzzzzz"[bit])
        elif tuple(a) == tuple(b):
            roles.append("c")
        else:
            roles.append("xyz"[[i for i in range(3) if a[i] != b[i]][0]])
    return roles


def swap(value, bit, count):
    return lax.ppermute(value, AXES, [(i, i ^ (1 << bit)) for i in range(count)])


def tie(value, *others):
    if not others:
        return value
    return lax.optimization_barrier((value,) + tuple(others))[0]


CHEAP = pl.CostEstimate(flops=1000, bytes_accessed=1000, transcendentals=0)


SCALAR = pl.BlockSpec(memory_space=pltpu.SMEM)
WHOLE = pl.BlockSpec(memory_space=pltpu.VMEM)


def grant(*arrays):
    total = sum(a.size * a.dtype.itemsize for a in arrays)
    return pltpu.CompilerParams(vmem_limit_bytes=min(2 * total + (4 << 20), 60 << 20))


def spread(t, positions):
    out = 0
    for k, position in enumerate(positions):
        out = out | (((t >> k) & 1) << position)
    return out


def settle(mine, *parts):
    half, rows, _ = parts[0][0].shape
    spans, columns = [], 0
    for first, _, _ in parts:
        spans.append(slice(columns, columns + first.shape[2]))
        columns += first.shape[2]

    def body(mine_ref, *refs):
        me, o_ref = mine_ref[0], refs[-1]

        def move(t, carry):
            for k, (here, (_, _, order)) in enumerate(zip(spans, parts)):
                o_ref[me ^ spread(t, order), :, here] = refs[2 * k][t]
                o_ref[me ^ spread(t + half, order), :, here] = refs[2 * k + 1][t]
            return carry

        lax.fori_loop(0, half, move, 0)

    arrays = [a for part in parts for a in part[:2]]
    out = jax.ShapeDtypeStruct((2 * half, rows, columns), BF)
    return pl.pallas_call(
        body,
        out_shape=out,
        in_specs=[SCALAR] + [WHOLE] * len(arrays),
        out_specs=WHOLE,
        cost_estimate=CHEAP,
        compiler_params=grant(*arrays, out),
        name="settle",
    )(mine, *arrays)


def insert_bit(index, position, value):
    low = index & ((1 << position) - 1)
    return ((index >> position) << (position + 1)) | (value << position) | low


def pieces_of(arrays):
    return [(a, 0, a.shape[2]) for a in arrays]


def cut(pieces, low, high):
    out, at = [], 0
    for array, start, width in pieces:
        lo, hi = max(low, at), min(high, at + width)
        if lo < hi:
            out.append((array, start + lo - at, hi - lo))
        at += width
    return out


def segments(*lists):
    edges = {0}
    for pieces in lists:
        at = 0
        for _, _, width in pieces:
            at += width
            edges.add(at)
    edges = sorted(edges)
    out = []
    for low, high in zip(edges, edges[1:]):
        found = []
        for pieces in lists:
            at = 0
            for k, (_, start, width) in enumerate(pieces):
                if at <= low < at + width:
                    found.append((k, start + low - at))
                at += width
        out.append((low, high, found))
    return out


def pick(mine, pieces, position, bit):
    blocks, rows, _ = pieces[0][0].shape
    spans = segments(pieces)
    columns = spans[-1][1]

    def body(mine_ref, *refs):
        o_ref = refs[-1]
        other = 1 - ((mine_ref[0] >> bit) & 1)

        def move(t, carry):
            index = insert_bit(t, position, other)
            for low, high, ((k, at),) in spans:
                o_ref[t, :, low:high] = refs[k][index, :, at : at + high - low]
            return carry

        lax.fori_loop(0, blocks // 2, move, 0)

    sources = [p[0] for p in pieces]
    out = jax.ShapeDtypeStruct((blocks // 2, rows, columns), BF)
    return pl.pallas_call(
        body,
        out_shape=out,
        in_specs=[SCALAR] + [WHOLE] * len(sources),
        out_specs=WHOLE,
        cost_estimate=CHEAP,
        compiler_params=grant(*sources, out),
        name="pick",
    )(mine, *sources)


def fold(mine, kept, got, now, position, bit):
    blocks, rows, _ = got[0][0].shape
    spans = segments(kept, got)
    columns = spans[-1][1]

    def body(mine_ref, *refs):
        k_refs, r_refs, s_ref, n_ref = refs[: len(kept)], refs[len(kept) : -2], refs[-2], refs[-1]
        side = (mine_ref[0] >> bit) & 1

        def put_total(out_ref, t, index):
            source = index
            if now is not None:
                source = insert_bit(index, now[0], (mine_ref[0] >> now[1]) & 1)
            for low, high, ((k, at), (r, start)) in spans:
                wide = high - low
                total = k_refs[k][source, :, at : at + wide].astype(F32)
                total += r_refs[r][index, :, start : start + wide].astype(F32)
                out_ref[t, :, low:high] = total.astype(BF)

        def move(t, carry):
            put_total(s_ref, t, insert_bit(t, position, 1 - side))
            put_total(n_ref, t, insert_bit(t, position, side))
            return carry

        lax.fori_loop(0, blocks // 2, move, 0)

    sources = [p[0] for p in kept + got]
    out = jax.ShapeDtypeStruct((blocks // 2, rows, columns), BF)
    return pl.pallas_call(
        body,
        out_shape=(out, out),
        in_specs=[SCALAR] + [WHOLE] * len(sources),
        out_specs=[WHOLE] * 2,
        cost_estimate=CHEAP,
        compiler_params=grant(*sources, out, out),
        name="fold",
    )(mine, *sources)


class Gather:
    def __init__(self, block, order, count):
        self.held, self.order, self.count, self.at = block, order, count, 0
        self.got = None

    def all(self, *after):
        if self.got is None:
            return tie(self.held, *after)
        return tie(jnp.concatenate([self.held, self.got], axis=0), *after)

    def step(self, *after):
        self.held = self.all(*after)
        self.got = swap(self.held, self.order[self.at], self.count)
        self.at += 1
        return self.got


class Scatter:
    def __init__(self, mine, kept, got, left, now, order, count):
        self.mine, self.kept, self.got, self.left = mine, kept, got, list(left)
        self.now, self.order, self.count, self.at, self.sent = now, order, count, 0, None

    def part(self, low, high, order):
        return Scatter(
            self.mine, cut(self.kept, low, high), cut(self.got, low, high), self.left, self.now, order, self.count
        )

    def beside(self, other, order):
        return Scatter(
            self.mine, self.kept + other.kept, self.got + other.got, self.left, None, order, self.count
        )

    def ready(self, *after):
        bit = self.order[self.at]
        position = self.left.index(bit)
        if self.got is None:
            kept = [(tie(a, *after), at, width) for a, at, width in self.kept[:1]] + self.kept[1:]
            self.kept = kept
            self.sent = pick(self.mine, kept, position, bit)
            self.now = (position, bit)
        else:
            got = [(tie(a, *after), at, width) for a, at, width in self.got[:1]] + self.got[1:]
            self.sent, rest = fold(self.mine, self.kept, got, self.now, position, bit)
            self.kept, self.now = pieces_of([rest]), None
        return self.sent

    def step(self, *after):
        self.ready(*after)
        bit = self.order[self.at]
        self.got = pieces_of([swap(self.sent, bit, self.count)])
        self.left.remove(bit)
        self.at += 1
        return self.got

    def total(self):
        return self.kept[0][0][0].astype(F32) + self.got[0][0][0].astype(F32)


def halves_of(shard, block):
    pieces = shard.shape[1] // (2 * block)

    def body(w_ref, even_ref, odd_ref):
        values = w_ref[...].astype(F32)
        for out, start in ((even_ref, 0), (odd_ref, block)):
            parts = [values[:, i * 2 * block + start : i * 2 * block + start + block] for i in range(pieces)]
            out[...] = jnp.concatenate(parts, axis=1).astype(out.dtype)

    out = jax.ShapeDtypeStruct((shard.shape[0], shard.shape[1] // 2), shard.dtype)
    return pl.pallas_call(
        body, out_shape=(out, out), cost_estimate=CHEAP, compiler_params=grant(shard, out, out), name="halves"
    )(shard)


def join_halves(even, odd, block):
    pieces = even.shape[1] // block

    def body(even_ref, odd_ref, o_ref):
        a, b = even_ref[...].astype(F32), odd_ref[...].astype(F32)
        parts = []
        for i in range(pieces):
            parts += [a[:, i * block : (i + 1) * block], b[:, i * block : (i + 1) * block]]
        o_ref[...] = jnp.concatenate(parts, axis=1)

    out = jax.ShapeDtypeStruct((even.shape[0], 2 * even.shape[1]), F32)
    return pl.pallas_call(
        body, out_shape=out, cost_estimate=CHEAP, compiler_params=grant(even, odd, out, out), name="join"
    )(even, odd)


def attend(qk, v, segment_row, segment_column, slopes, batches, slot):
    pairs = HEADS // 2
    width = 2 * HEAD_DIM

    def body(slope_ref, qk_ref, v_ref, row_ref, column_ref, o_ref, p_ref):
        pair = pl.program_id(1)
        at = pl.multiple_of(pair * width, width)
        query = qk_ref[:, pl.ds(at, width)]
        keyed = qk_ref[:, pl.ds(D + at, width)]
        value = v_ref[:, pl.ds(at, width)]
        lane = lax.broadcasted_iota(I32, (slot, width), 1)
        gap = jnp.abs(
            lax.broadcasted_iota(I32, (slot, slot), 0) - lax.broadcasted_iota(I32, (slot, slot), 1)
        ).astype(F32)
        same = column_ref[0] == row_ref[0]
        mixed = []
        for which in range(2):
            own = (lane >= HEAD_DIM) if which else (lane < HEAD_DIM)
            only = jnp.where(own, query, jnp.zeros_like(query))
            scores = lax.dot_general(only, keyed, (((1,), (1,)), ((), ())), preferred_element_type=F32)
            scores = jnp.where(same, scores * 0.125 - slope_ref[2 * pair + which] * gap, NEGATIVE)
            raised = jnp.exp(scores - jnp.max(scores, axis=1, keepdims=True))
            probs = (raised / jnp.sum(raised, axis=1, keepdims=True)).astype(BF)
            p_ref[0, 0, which] = probs
            mixed.append(jnp.dot(probs, value, preferred_element_type=F32))
        o_ref[:, pl.ds(at, width)] = jnp.where(lane < HEAD_DIM, mixed[0], mixed[1]).astype(BF)

    rows = batches * slot
    merged = jax.ShapeDtypeStruct((rows, D), BF)
    probs = jax.ShapeDtypeStruct((batches, pairs, 2, slot, slot), BF)
    return pl.pallas_call(
        body,
        out_shape=(merged, probs),
        grid=(batches, pairs),
        in_specs=[
            pl.BlockSpec(memory_space=pltpu.SMEM),
            pl.BlockSpec((slot, 2 * D), lambda b, h: (b, 0)),
            pl.BlockSpec((slot, D), lambda b, h: (b, 0)),
            pl.BlockSpec((1, 1, slot), lambda b, h: (b, 0, 0)),
            pl.BlockSpec((1, slot, 1), lambda b, h: (b, 0, 0)),
        ],
        out_specs=[
            pl.BlockSpec((slot, D), lambda b, h: (b, 0)),
            pl.BlockSpec((1, 1, 2, slot, slot), lambda b, h: (b, h, 0, 0, 0)),
        ],
        cost_estimate=CHEAP,
        compiler_params=pltpu.CompilerParams(vmem_limit_bytes=24 * 1024 * 1024),
        name="attend",
    )(slopes, qk, v, segment_row, segment_column)


def attend_back(qk, v, probs, do, batches, slot):
    pairs = HEADS // 2
    width = 2 * HEAD_DIM
    first = (((0,), (0,)), ((), ()))
    second = (((1,), (1,)), ((), ()))

    def body(qk_ref, v_ref, p_ref, do_ref, dqk_ref, dv_ref):
        at = pl.multiple_of(pl.program_id(1) * width, width)
        query = qk_ref[:, pl.ds(at, width)]
        keyed = qk_ref[:, pl.ds(D + at, width)]
        value = v_ref[:, pl.ds(at, width)]
        upstream = do_ref[:, pl.ds(at, width)]
        lane = lax.broadcasted_iota(I32, (slot, width), 1)
        dq, dk, dv = [], [], []
        for which in range(2):
            own = (lane >= HEAD_DIM) if which else (lane < HEAD_DIM)
            low = p_ref[0, 0, which]
            high = low.astype(F32)
            only = jnp.where(own, upstream, jnp.zeros_like(upstream))
            dp = lax.dot_general(only, value, second, preferred_element_type=F32)
            delta = jnp.sum(high * dp, axis=1, keepdims=True)
            ds = (high * (dp - delta)).astype(BF)
            dq.append(jnp.dot(ds, keyed, preferred_element_type=F32))
            dk.append(lax.dot_general(ds, query, first, preferred_element_type=F32))
            dv.append(lax.dot_general(low, upstream, first, preferred_element_type=F32))
        early = lane < HEAD_DIM
        dqk_ref[:, pl.ds(at, width)] = (jnp.where(early, dq[0], dq[1]) * 0.125).astype(BF)
        dqk_ref[:, pl.ds(D + at, width)] = (jnp.where(early, dk[0], dk[1]) * 0.125).astype(BF)
        dv_ref[:, pl.ds(at, width)] = jnp.where(early, dv[0], dv[1]).astype(BF)

    rows = batches * slot
    return pl.pallas_call(
        body,
        out_shape=(jax.ShapeDtypeStruct((rows, 2 * D), BF), jax.ShapeDtypeStruct((rows, D), BF)),
        grid=(batches, pairs),
        in_specs=[
            pl.BlockSpec((slot, 2 * D), lambda b, h: (b, 0)),
            pl.BlockSpec((slot, D), lambda b, h: (b, 0)),
            pl.BlockSpec((1, 1, 2, slot, slot), lambda b, h: (b, h, 0, 0, 0)),
            pl.BlockSpec((slot, D), lambda b, h: (b, 0)),
        ],
        out_specs=[
            pl.BlockSpec((slot, 2 * D), lambda b, h: (b, 0)),
            pl.BlockSpec((slot, D), lambda b, h: (b, 0)),
        ],
        cost_estimate=CHEAP,
        compiler_params=pltpu.CompilerParams(vmem_limit_bytes=24 * 1024 * 1024),
        name="attend_back",
    )(qk, v, probs, do)


TILE = 256
ROWS = (((0,), (0,)), ((), ()))
BACK = (((1,), (1,)), ((), ()))


def in_vmem(body, outs, *arrays, name):
    total = sum(a.size * a.dtype.itemsize for a in arrays + tuple(outs))
    return pl.pallas_call(
        body,
        out_shape=tuple(outs),
        in_specs=[WHOLE] * len(arrays),
        out_specs=tuple([WHOLE] * len(outs)),
        cost_estimate=CHEAP,
        compiler_params=pltpu.CompilerParams(vmem_limit_bytes=min(total + (16 << 20), 62 << 20)),
        name=name,
    )(*arrays)


def product(left, right, dims):
    return lax.dot_general(left, right, dims, preferred_element_type=F32)


def tiles(count, step):
    def run(i, carry):
        step(pl.multiple_of(i * TILE, TILE))
        return carry

    lax.fori_loop(0, count // TILE, run, 0)


def receive(arrived, sizes, count, batches, slot, held):
    per = slot // count
    spans = -(-sum(sizes) // held)

    def body(in_ref, x_ref, put_ref, *refs):
        outs, side_ref = refs[:-1], refs[-1]
        for b in range(batches):
            slots = in_ref[b, :, D:].astype(F32)[:, 127:128]
            put = (slots == lax.broadcasted_iota(I32, (slot, slot), 1).astype(F32)).astype(F32).astype(BF)
            put_ref[b] = put
            x_ref[b * slot : (b + 1) * slot, :] = product(put, in_ref[b, :, :D], ROWS).astype(BF)
        side_ref[...] = in_ref[0, :, D:].astype(F32)
        flat = jnp.concatenate(
            [side_ref[pl.ds(r, count, stride=per), :][:, :held] for r in range(spans)], axis=1
        )
        at = 0
        for out, size in zip(outs, sizes):
            for j in range(count):
                out[:, j * size : (j + 1) * size] = flat[j : j + 1, at : at + size]
            at += size

    outs = [
        jax.ShapeDtypeStruct((batches * slot, D), BF),
        jax.ShapeDtypeStruct((batches, slot, slot), BF),
    ] + [jax.ShapeDtypeStruct((1, count * size), F32) for size in sizes]
    return pl.pallas_call(
        body,
        out_shape=tuple(outs),
        in_specs=[WHOLE],
        out_specs=tuple([WHOLE] * len(outs)),
        scratch_shapes=[pltpu.VMEM((slot, 128), F32)],
        cost_estimate=CHEAP,
        compiler_params=pltpu.CompilerParams(vmem_limit_bytes=20 << 20),
        name="receive",
    )(arrived)


def project(x, weights, bias):
    def body(x_ref, w_ref, b_ref, qk_ref, v_ref):
        def step(at):
            here = pl.ds(at, TILE)
            tile = x_ref[here, :]
            q = jnp.dot(tile, w_ref[:, :D], preferred_element_type=F32) + b_ref[:, :D]
            qk_ref[here, :D] = q.astype(BF)
            qk_ref[here, D:] = jnp.dot(tile, w_ref[:, D : 2 * D], preferred_element_type=F32).astype(BF)
            v = jnp.dot(tile, w_ref[:, 2 * D : 3 * D], preferred_element_type=F32) + b_ref[:, D:]
            v_ref[here, :] = v.astype(BF)

        tiles(x.shape[0], step)

    outs = [jax.ShapeDtypeStruct((x.shape[0], 2 * D), BF), jax.ShapeDtypeStruct((x.shape[0], D), BF)]
    return in_vmem(body, outs, x, weights, bias, name="project")


def first_norm(x, merged, weights, bias, gain, shift):
    def body(x_ref, m_ref, w_ref, b_ref, g_ref, s_ref, r_ref, h_ref):
        def step(at):
            here = pl.ds(at, TILE)
            total = x_ref[here, :].astype(F32) + b_ref[...]
            total += jnp.dot(m_ref[here, :], w_ref[:, 3 * D :], preferred_element_type=F32)
            r_ref[here, :] = total
            h_ref[here, :] = (norm_stats(total)[0] * g_ref[...] + s_ref[...]).astype(BF)

        tiles(x.shape[0], step)

    outs = [jax.ShapeDtypeStruct(x.shape, F32), jax.ShapeDtypeStruct(x.shape, BF)]
    return in_vmem(body, outs, x, merged, weights, bias, gain, shift, name="first_norm")


def near(width):
    return pl.BlockSpec((TILE, width), lambda i: (jnp.minimum(i, 1), 0))


def far(width):
    return pl.BlockSpec((TILE, width), lambda i: (jnp.maximum(i - 2, 0), 0))


def tile_of(width):
    return pl.BlockSpec((TILE, width), lambda i: (i, 0))


def fixed(*shape):
    return pl.BlockSpec(shape, lambda i: (0, 0))


TILED_GRANT = pltpu.CompilerParams(vmem_limit_bytes=32 << 20)


def units(mine, h, h_other, w_gate, w_lin, even, odd, core):
    rows, hidden = h.shape[0], w_gate.shape[1]
    assert rows == 2 * TILE

    def body(mine_ref, h_ref, o_ref, g_ref, l_ref, e_ref, d_ref, a_ref, slope_ref, act_ref):
        first = ((mine_ref[0] >> core) & 1) == 0
        tile = jnp.where(pl.program_id(0) < 2, h_ref[...], o_ref[...])
        for lo in range(0, hidden, TILE):
            wide = slice(lo, lo + TILE)
            late = slice(hidden + lo, hidden + lo + TILE)
            gate = jnp.dot(tile, g_ref[:, wide], preferred_element_type=F32)
            gate += jnp.where(first, e_ref[:, wide], d_ref[:, wide])
            lin = jnp.dot(tile, l_ref[:, wide], preferred_element_type=F32)
            lin += jnp.where(first, e_ref[:, late], d_ref[:, late])
            cdf = 0.5 * (1.0 + lax.erf(gate * (0.5**0.5)))
            act = gate * cdf
            slope = cdf + gate * jnp.exp(-0.5 * gate * gate) * (1.0 / (2.0 * jnp.pi) ** 0.5)
            a_ref[:, wide] = (act * lin).astype(BF)
            slope_ref[:, wide] = (slope * lin).astype(BF)
            act_ref[:, wide] = act.astype(BF)

    out = jax.ShapeDtypeStruct((2 * rows, hidden), BF)
    return pl.pallas_call(
        body,
        out_shape=(out, out, out),
        grid=(4,),
        in_specs=[SCALAR, near(D), far(D)] + [fixed(D, hidden)] * 2 + [fixed(1, 2 * hidden)] * 2,
        out_specs=(tile_of(hidden),) * 3,
        cost_estimate=CHEAP,
        compiler_params=TILED_GRANT,
        name="units",
    )(mine, h, h_other, w_gate, w_lin, even, odd)


def down_weight_grad(a, df, df_other):
    rows = df.shape[0]

    def body(a_ref, d_ref, o_ref, g_ref):
        def step(at):
            g = product(a_ref[:rows, pl.ds(at, TILE)], d_ref[...], ROWS)
            g += product(a_ref[rows:, pl.ds(at, TILE)], o_ref[...], ROWS)
            g_ref[pl.ds(at, TILE), :] = g.astype(BF)

        tiles(a.shape[1], step)

    out = jax.ShapeDtypeStruct((a.shape[1], df.shape[1]), BF)
    return in_vmem(body, [out], a, df, df_other, name="down_grad")[0]


def units_back(df, df_other, w_dn, slope, act):
    rows, hidden = df.shape[0], w_dn.shape[0]

    def body(d_ref, o_ref, w_ref, s_ref, a_ref, du1_ref, du2_ref, sum_ref):
        i = pl.program_id(0)
        tile = jnp.where(i < 2, d_ref[...], o_ref[...])
        da = product(tile, w_ref[...], BACK).astype(BF).astype(F32)
        du1 = (da * s_ref[...].astype(F32)).astype(BF)
        du2 = (da * a_ref[...].astype(F32)).astype(BF)
        du1_ref[...] = du1
        du2_ref[...] = du2

        @pl.when(i == 0)
        def _():
            sum_ref[...] = jnp.zeros_like(sum_ref)

        sum_ref[0:1, :] += jnp.sum(du1.astype(F32), axis=0, keepdims=True)
        sum_ref[1:2, :] += jnp.sum(du2.astype(F32), axis=0, keepdims=True)

    du = jax.ShapeDtypeStruct((2 * rows, hidden), BF)
    sums = jax.ShapeDtypeStruct((2, hidden), F32)
    return pl.pallas_call(
        body,
        out_shape=(du, du, sums),
        grid=(4,),
        in_specs=[near(D), far(D), fixed(hidden, D), tile_of(hidden), tile_of(hidden)],
        out_specs=(tile_of(hidden), tile_of(hidden), fixed(2, hidden)),
        cost_estimate=CHEAP,
        compiler_params=TILED_GRANT,
        name="units_back",
    )(df, df_other, w_dn, slope, act)


def up_weight_grad(h, h_other, du):
    rows = h.shape[0]

    def body(h_ref, o_ref, d_ref, g_ref):
        def step(at):
            g = product(h_ref[:, pl.ds(at, TILE)], d_ref[:rows, :], ROWS)
            g += product(o_ref[:, pl.ds(at, TILE)], d_ref[rows:, :], ROWS)
            g_ref[pl.ds(at, TILE), :] = g.astype(BF)

        tiles(h.shape[1], step)

    out = jax.ShapeDtypeStruct((h.shape[1], du.shape[1]), BF)
    return in_vmem(body, [out], h, h_other, du, name="up_grad")[0]


def hidden_back(du1, du2, w_gate, w_lin):
    rows, hidden = du1.shape[0] // 2, du1.shape[1]

    def body(d1_ref, d2_ref, g_ref, l_ref, own_ref, other_ref):
        dh = product(d1_ref[...], g_ref[...], BACK) + product(d2_ref[...], l_ref[...], BACK)

        @pl.when(pl.program_id(0) < 2)
        def _():
            own_ref[...] = dh

        @pl.when(pl.program_id(0) >= 2)
        def _():
            other_ref[...] = dh.astype(BF)

    own = jax.ShapeDtypeStruct((rows, D), F32)
    other = jax.ShapeDtypeStruct((rows, D), BF)
    return pl.pallas_call(
        body,
        out_shape=(own, other),
        grid=(4,),
        in_specs=[tile_of(hidden)] * 2 + [fixed(D, hidden)] * 2,
        out_specs=(near(D), far(D)),
        cost_estimate=CHEAP,
        compiler_params=TILED_GRANT,
        name="hidden_back",
    )(du1, du2, w_gate, w_lin)


def down_product(a, w_dn):
    rows = a.shape[0] // 2

    def body(a_ref, w_ref, own_ref, other_ref):
        for base, out in ((0, own_ref), (rows, other_ref)):

            def step(at, base=base, out=out):
                out[pl.ds(at, TILE), :] = jnp.dot(
                    a_ref[pl.ds(base + at, TILE), :], w_ref[...], preferred_element_type=F32
                ).astype(out.dtype)

            tiles(rows, step)

    own = jax.ShapeDtypeStruct((rows, D), F32)
    other = jax.ShapeDtypeStruct((rows, D), BF)
    return in_vmem(body, [own, other], a, w_dn, name="down_product")


def second_norm(h, down, down_other, e, down_b, gain, shift):
    rows = h.shape[0]

    def body(h_ref, d_ref, o_ref, e_ref, b_ref, g_ref, s_ref, res_ref, dr_ref, df_ref, sum_ref):
        sum_ref[...] = jnp.zeros_like(sum_ref)
        bias, gains, shifts = b_ref[...], g_ref[...], s_ref[...]

        def step(at):
            here = pl.ds(at, TILE)
            total = h_ref[here, :].astype(F32) + d_ref[here, :] + o_ref[here, :].astype(F32) + bias
            normed, inverse = norm_stats(total)
            res_ref[here, :] = (normed * gains + shifts).astype(BF)
            up = e_ref[here, :]
            dr = norm_back(normed, inverse, gains, up)
            low = dr.astype(BF)
            dr_ref[here, :] = dr
            df_ref[here, :] = low
            sum_ref[0:1, :] += jnp.sum(up * normed, axis=0, keepdims=True)
            sum_ref[1:2, :] += jnp.sum(up, axis=0, keepdims=True)
            sum_ref[2:3, :] += jnp.sum(low.astype(F32), axis=0, keepdims=True)

        tiles(rows, step)

    low, wide = jax.ShapeDtypeStruct((rows, D), BF), jax.ShapeDtypeStruct((rows, D), F32)
    outs = [low, wide, low, jax.ShapeDtypeStruct((3, D), F32)]
    return in_vmem(body, outs, h, down, down_other, e, down_b, gain, shift, name="second_norm")


def first_norm_back(dh_own, dh_other, dr2, r1, gain, w_vo):
    rows = r1.shape[0]

    def body(d_ref, o_ref, r_ref, n_ref, g_ref, w_ref, dr_ref, dbr_ref, do_ref, sum_ref):
        sum_ref[...] = jnp.zeros_like(sum_ref)

        def step(at):
            here = pl.ds(at, TILE)
            dh = d_ref[here, :] + o_ref[here, :].astype(F32) + r_ref[here, :]
            normed, inverse = norm_stats(n_ref[here, :])
            dr = norm_back(normed, inverse, g_ref[...], dh)
            low = dr.astype(BF)
            dr_ref[here, :] = dr
            dbr_ref[here, :] = low
            do_ref[here, :] = product(low, w_ref[:, 3 * D :], BACK).astype(BF)
            sum_ref[0:1, :] += jnp.sum(dh * normed, axis=0, keepdims=True)
            sum_ref[1:2, :] += jnp.sum(dh, axis=0, keepdims=True)
            sum_ref[2:3, :] += jnp.sum(low.astype(F32), axis=0, keepdims=True)

        tiles(rows, step)

    low, wide = jax.ShapeDtypeStruct((rows, D), BF), jax.ShapeDtypeStruct((rows, D), F32)
    outs = [wide, low, low, jax.ShapeDtypeStruct((3, D), F32)]
    return in_vmem(body, outs, dh_own, dh_other, dr2, r1, gain, w_vo, name="first_norm_back")


def attention_weight_grads(x, dqk, dv, merged, dbr):
    def body(x_ref, qk_ref, v_ref, m_ref, d_ref, gqk_ref, gv_ref, go_ref, sum_ref):
        def step(at):
            here = pl.ds(at, TILE)
            gqk_ref[here, :] = product(x_ref[:, here], qk_ref[...], ROWS).astype(BF)
            gv_ref[here, :] = product(x_ref[:, here], v_ref[...], ROWS).astype(BF)
            go_ref[here, :] = product(m_ref[:, here], d_ref[...], ROWS).astype(BF)

        tiles(D, step)
        sum_ref[0:1, :] = jnp.sum(qk_ref[:, :D].astype(F32), axis=0, keepdims=True)
        sum_ref[1:2, :] = jnp.sum(v_ref[...].astype(F32), axis=0, keepdims=True)

    outs = [jax.ShapeDtypeStruct((D, n * D), BF) for n in (2, 1, 1)] + [jax.ShapeDtypeStruct((2, D), F32)]
    return in_vmem(body, outs, x, dqk, dv, merged, dbr, name="attention_grads")


def input_back(dr1, dqk, dv, weights):
    def body(r_ref, qk_ref, v_ref, w_ref, out_ref):
        def step(at):
            here = pl.ds(at, TILE)
            dx = r_ref[here, :] + product(qk_ref[here, :], w_ref[:, : 2 * D], BACK)
            out_ref[here, :] = (dx + product(v_ref[here, :], w_ref[:, 2 * D : 3 * D], BACK)).astype(BF)

        tiles(dr1.shape[0], step)

    return in_vmem(body, [jax.ShapeDtypeStruct(dr1.shape, BF)], dr1, dqk, dv, weights, name="input_back")[0]


def owner_sums(mine, qv, first, second, half, sizes, count, block, core):
    total = sum(sizes)
    lanes = total + -total % 128

    def body(mine_ref, q_ref, f_ref, s_ref, u_ref, o_ref):
        mine_side = (mine_ref[0] >> core) & 1
        pieces = []
        for g in range(2):
            for i in range(u_ref.shape[1] // block):
                part = u_ref[g : g + 1, i * block : (i + 1) * block]
                for side in range(2):
                    pieces.append(jnp.where(mine_side == side, part, 0.0))
        up = jnp.concatenate(pieces, axis=1)
        rows = [None] + [r[i : i + 1, :] for r, i in ((f_ref, 2), (f_ref, 0), (f_ref, 1))]
        rows += [up] + [r[i : i + 1, :] for r, i in ((s_ref, 2), (s_ref, 0), (s_ref, 1))]
        o_ref[...] = jnp.zeros_like(o_ref)
        for j in range(count):
            at = 0
            for k, size in enumerate(sizes):
                if k == 0:
                    row, lo = divmod(j * size, D)
                    piece = q_ref[row : row + 1, lo : lo + size]
                else:
                    piece = rows[k][:, j * size : (j + 1) * size]
                o_ref[j, :, at : at + size] = piece
                at += size

    out = jax.ShapeDtypeStruct((count, 1, lanes), F32)
    return pl.pallas_call(
        body,
        out_shape=out,
        in_specs=[SCALAR] + [WHOLE] * 4,
        out_specs=WHOLE,
        cost_estimate=CHEAP,
        compiler_params=pltpu.CompilerParams(vmem_limit_bytes=8 << 20),
        name="owner_sums",
    )(mine, qv, first, second, half)


def norm_stats(values):
    centre = jnp.mean(values, axis=-1, keepdims=True)
    centred = values - centre
    spread_of = jnp.mean(centred * centred, axis=-1, keepdims=True)
    inverse = lax.rsqrt(spread_of + EPS)
    return centred * inverse, inverse


def norm_back(normed, inverse, gain, upstream):
    scaled = upstream * gain
    first = jnp.mean(scaled, axis=-1, keepdims=True)
    second = jnp.mean(scaled * normed, axis=-1, keepdims=True)
    return (scaled - first - normed * second) * inverse


def dot(left, right):
    return jnp.dot(left, right, preferred_element_type=F32)


def dot_rows(left, right):
    return lax.dot_general(left, right, (((0,), (0,)), ((), ())), preferred_element_type=F32)


def dot_back(left, right):
    return lax.dot_general(left, right, (((1,), (1,)), ((), ())), preferred_element_type=F32)


def build(mesh):
    count = mesh.devices.size
    roles = bit_roles(mesh)
    every = list(range(len(roles)))

    def of(role):
        return [b for b in reversed(every) if roles[b] == role]

    core = roles.index("c")
    chips = [b for b in every if b != core]
    deep = of("z")
    one = deep + of("x") + of("y")
    two = deep + of("y") + of("x")
    flat_one, flat_two = of("x") + of("y"), of("y") + of("x")

    def chip_position(bit):
        return bit if bit < core else bit - 1

    def on_device(
        tokens,
        cotangent,
        target,
        lengths,
        w_qkv,
        qv_bias,
        w_out,
        out_bias,
        gain_one,
        shift_one,
        w_up,
        up_bias,
        w_down,
        down_bias,
        gain_two,
        shift_two,
    ):
        me = lax.axis_index(AXES).astype(I32)
        my_core = (me >> core) & 1
        mine = me.reshape(1)
        low = me & ((1 << core) - 1)
        my_chip = (((me >> (core + 1)) << core) | low).reshape(1)
        batches, slot, width = tokens.shape
        rows = batches * slot
        per = slot // count
        place = jnp.arange(slot, dtype=I32)
        unit_block = (FF // count) << core
        hidden = FF // 2

        even, odd = halves_of(w_up, unit_block)
        up_send = jnp.where(my_core == 0, odd, even)
        up_hold = jnp.where(my_core == 0, even, odd)
        chain_attn = Gather(jnp.concatenate([w_qkv, w_out], axis=1)[None], deep, count)
        up_got = swap(up_send, core, count)
        chain_up = Gather(jnp.stack([up_hold, up_got]), deep, count)
        down_order = flat_two + deep
        chain_down = Gather(w_down[None], down_order, count)

        smalls = [qv_bias, out_bias, gain_one, shift_one, up_bias, down_bias, gain_two, shift_two]
        sizes = [v.shape[0] for v in smalls]
        packed = jnp.concatenate(smalls)
        total = packed.shape[0]

        rank = jnp.sum((target[:, None, :] < target[:, :, None]).astype(I32), axis=2)
        chosen = (rank[:, None, :] == place[None, :, None]).astype(BF)
        slots = (target % slot).astype(BF)
        out_rows = jnp.einsum("bri,bid->brd", chosen, tokens, preferred_element_type=F32).astype(BF)
        out_up = jnp.einsum("bri,bid->brd", chosen, cotangent, preferred_element_type=F32).astype(BF)
        out_slots = jnp.einsum("bri,bi->br", chosen, slots, preferred_element_type=F32).astype(BF)

        def by_device(v):
            return v.reshape((batches, count, per) + v.shape[2:]).swapaxes(0, 1).reshape(
                (count, batches * per) + v.shape[2:]
            )

        extra_rows = batches * per
        held = 64
        spans = -(-total // held)
        side = jnp.pad(packed, (0, spans * held - total)).reshape(spans, held)
        side = jnp.pad(side, ((0, extra_rows - spans), (0, 127 - held)))
        payload = jnp.concatenate(
            [
                by_device(out_rows),
                jnp.broadcast_to(side[None], (count, extra_rows, 127)),
                by_device(out_slots)[..., None],
            ],
            axis=2,
        )
        first = lax.all_to_all(payload, AXES, split_axis=0, concat_axis=0, tiled=True)
        flat, zs = len(flat_one), len(deep)
        for _ in range(zs):
            chain_attn.step()
        for _ in range(flat):
            chain_down.step()
        attn = chain_attn.all()
        chain_qk = Gather(attn[:, :, : 2 * D], flat_one + [core], count)
        chain_vo = Gather(attn[:, :, 2 * D :], flat_two + [core], count)
        for k in range(flat):
            chain_qk.step()
            chain_vo.step()
            if k == 0:
                chain_up.step(chain_attn.got)
                for _ in range(zs - 1):
                    chain_up.step()

        def by_batch(v):
            return v.reshape((count, batches, per) + v.shape[2:]).swapaxes(0, 1).reshape(
                (batches, slot) + v.shape[2:]
            )

        x, put, *vectors = receive(by_batch(first), sizes, count, batches, slot, held)
        qv_b, out_b, gain1, shift1, up_b, down_b, gain2, shift2 = vectors

        after_chips = (chain_qk.got, chain_vo.got)
        chain_qk.step(x)
        chain_vo.step(x)
        ups = chain_up.all()
        chain_gate = Gather(ups[:, :, :hidden], flat_one, count)
        chain_lin = Gather(ups[:, :, hidden:], flat_two, count)
        for _ in range(flat - 1):
            chain_gate.step(*after_chips)
            chain_lin.step(*after_chips)
            after_chips = ()
        for _ in range(zs - 1):
            chain_down.step(chain_up.got)
        bounds = jnp.cumsum(lengths[:, 0], axis=-1)
        segment = jnp.sum((bounds[:, :, None] <= place).astype(I32), axis=1)
        slopes = jnp.exp2(-8.0 * (jnp.arange(HEADS, dtype=F32) + 1.0) / HEADS)

        weights = settle(
            mine,
            (chain_qk.held, chain_qk.got, one + [core]),
            (chain_vo.held, chain_vo.got, two + [core]),
        ).reshape(D, 4 * D)
        qk, v = project(x, weights, qv_b)
        qk = tie(qk, chain_gate.got, chain_lin.got)
        chain_gate.step()
        chain_lin.step()
        merged, probs = attend(qk, v, segment[:, None, :], segment[:, :, None], slopes, batches, slot)
        chain_down.got = tie(chain_down.got, merged)
        chain_down.step()
        r1, h = first_norm(x, merged, weights, out_b, gain1, shift1)

        h_other = swap(h, core, count)
        second = lax.all_to_all(tie(by_device(out_up), h), AXES, split_axis=0, concat_axis=0, tiled=True)
        w_gate = settle(mine, (chain_gate.held, chain_gate.got, [core] + one)).reshape(D, hidden)
        w_lin = settle(mine, (chain_lin.held, chain_lin.got, [core] + two)).reshape(D, hidden)
        even_b, odd_b = halves_of(up_b, unit_block)
        a, slope_low, act_low = units(mine, h, h_other, w_gate, w_lin, even_b, odd_b, core)
        down_got = tie(chain_down.got, a)
        w_dn = settle(
            my_chip, (chain_down.held, down_got, [chip_position(b) for b in down_order])
        ).reshape(hidden, D)
        down, down_send = down_product(a, w_dn)
        down_other = swap(down_send, core, count)
        e = jnp.einsum("bkp,bkd->bpd", put, by_batch(second), preferred_element_type=F32).reshape(rows, D)
        result, dr2, df, sums2 = second_norm(h, down, down_other, e, down_b, gain2, shift2)

        def back(rows_here, *after):
            sent = jnp.einsum(
                "bkp,bpd->bkd", put, rows_here.reshape(batches, slot, D), preferred_element_type=F32
            ).astype(BF)
            return lax.all_to_all(tie(by_device(sent), *after), AXES, split_axis=0, concat_axis=0, tiled=True)

        def given(got):
            return jnp.einsum("bri,brd->bid", chosen, by_batch(got), preferred_element_type=F32).astype(BF)

        df_other = swap(df, core, count)
        g_down = down_weight_grad(a, df, df_other).reshape(count // 2, FF // count, D)
        scatter_down = Scatter(mine, pieces_of([g_down]), None, chips, None, deep[::-1][:1] + flat_two[::-1] + deep[::-1][1:], count)
        scatter_down.step()
        du1, du2, g_half_b = units_back(tie(df, scatter_down.sent), df_other, w_dn, slope_low, act_low)
        blocks = (count, D // count, -1)
        g_gate = up_weight_grad(h, h_other, du1).reshape(blocks)
        scatter_gate = Scatter(mine, pieces_of([g_gate]), None, every, None, flat_one[::-1], count)
        scatter_gate.step()
        du2 = tie(du2, scatter_gate.sent)
        g_lin = up_weight_grad(h, h_other, du2).reshape(blocks)
        scatter_lin = Scatter(mine, pieces_of([g_lin]), None, every, None, flat_two[::-1], count)
        scatter_lin.step()
        du1 = tie(du1, scatter_lin.sent)
        dh_own, dh_send = hidden_back(du1, du2, w_gate, w_lin)
        scatter_down.step(dh_own)
        dh_other = swap(tie(dh_send, scatter_down.sent), core, count)
        scatter_gate.step(scatter_down.sent)
        scatter_lin.step(scatter_gate.sent)
        dr1, dbr, do, sums1 = first_norm_back(
            tie(dh_own, scatter_lin.sent), dh_other, dr2, r1, gain1, weights
        )
        back_out = back(result, do)
        dqk, dv = attend_back(qk, v, probs, do, batches, slot)
        g_qk, g_v, g_out, qv_sums = attention_weight_grads(x, dqk, dv, merged, dbr)
        g_qk, g_v, g_out = g_qk.reshape(blocks), g_v.reshape(blocks), g_out.reshape(blocks)

        scatter_up = scatter_gate.beside(scatter_lin, deep[::-1] + [core])
        scatter_up.step(g_out)
        scatter_attn = Scatter(mine, pieces_of([g_qk, g_v, g_out]), None, every, None, [core], count)
        scatter_attn.step(scatter_up.sent, back_out)
        dx = input_back(tie(dr1, scatter_attn.sent), dqk, dv, weights)
        last = dx

        def go(chain):
            nonlocal last
            chain.step(last)
            last = chain.sent

        scatter_qk = scatter_attn.part(0, 2 * D, flat_one[::-1])
        scatter_vo = scatter_attn.part(2 * D, 4 * D, flat_two[::-1])
        back_dx = back(dx)
        small_after = None
        for _ in range(flat):
            go(scatter_qk)
            go(scatter_vo)
            if small_after is None:
                small_after = last
        small_send = owner_sums(
            tie(mine, small_after), qv_sums, sums1, sums2, g_half_b, sizes, count, unit_block, core
        )
        small_got = lax.all_to_all(small_send, AXES, split_axis=0, concat_axis=0, tiled=True)
        small_sum = jnp.sum(small_got, axis=(0, 1))

        while scatter_up.at < len(deep):
            go(scatter_up)
        scatter_attn = scatter_qk.beside(scatter_vo, deep[::-1])
        scatter_attn.step(last, back_dx)
        last = scatter_attn.sent
        while scatter_down.at < len(one) - 1:
            go(scatter_down)
        up_last = scatter_up.ready(last)[0]
        up_kept = scatter_up.kept[0][0][0]
        up_came = swap(up_last, core, count)
        last = up_last
        while scatter_down.at < len(one):
            go(scatter_down)
        while scatter_attn.at < len(deep):
            scatter_attn.step(last, small_got)
            last = scatter_attn.sent
        out_tokens = given(back_out)
        grad_tokens = given(back_dx)
        s_up = join_halves(
            jnp.where(my_core == 0, up_kept, up_came), jnp.where(my_core == 0, up_came, up_kept), unit_block
        )
        s_attn = scatter_attn.total()
        outs, at = [], 0
        for size in sizes:
            outs.append(small_sum[at : at + size])
            at += size
        return (
            out_tokens,
            grad_tokens,
            s_attn[:, : 3 * D],
            outs[0],
            s_attn[:, 3 * D : 4 * D],
            outs[1],
            outs[2],
            outs[3],
            s_up,
            outs[4],
            scatter_down.total(),
            outs[5],
            outs[6],
            outs[7],
        )

    return on_device


def solution(mesh):
    rows = P(None, AXES, None)
    matrix, vector = P(AXES, None), P(AXES)
    return jax.shard_map(
        build(mesh),
        mesh=mesh,
        in_specs=(rows, rows, P(None, AXES), rows)
        + (matrix, vector, matrix, vector, vector, vector, matrix, vector, matrix, vector, vector, vector),
        out_specs=(rows, rows)
        + (matrix, vector, matrix, vector, vector, vector, matrix, vector, matrix, vector, vector, vector),
        check_vma=False,
    )
```
